32 devices in a mesh: dp: 8 (over y, x, core), tensor: 4 (over z).
Axes of the slice: x: 2, y: 2, z: 4, core: 2. Of those that a mesh axis runs over, the one named last changes fastest.
Arguments:
- tokens: bfloat16 [8192, 1024], P(('dp', 'tensor')), may hold values from -6 to 6
- time_embed: bfloat16 [8192, 256], P(('dp', 'tensor')), may hold values from -6 to 6
- segment_ids: int32 [8, 1024], P('dp'), may hold values from 0 to 3, as said below
- positions: int32 [8, 1024], P('dp'), may hold values from 0 to 2047, as said below
- first_gain: float32 [1024], replicated, may hold values from 0.1 to 1.9
- first_bias: float32 [1024], replicated, may hold values from -4 to 4
- second_gain: float32 [1024], replicated, may hold values from 0.1 to 1.9
- second_bias: float32 [1024], replicated, may hold values from -4 to 4
- time_weight: bfloat16 [256, 4, 1024], replicated, may hold values from -0.1875 to 0.1875
- time_bias: float32 [4, 1024], replicated, may hold values from -4 to 4
- qkv_weight: bfloat16 [1024, 3, 1024], P(None, None, 'tensor'), may hold values from -0.1875 to 0.1875
- out_weight: bfloat16 [1024, 1024], P('tensor'), may hold values from -0.75 to 0.75
- up_weight: bfloat16 [1024, 4096], P(None, 'tensor'), may hold values from -0.1875 to 0.1875
- down_weight: bfloat16 [4096, 1024], P('tensor'), may hold values from -0.09375 to 0.09375
- cotangent: bfloat16 [8192, 1024], P(('dp', 'tensor')), may hold values from -6 to 6
Outputs:
- result: bfloat16 [8192, 1024], P(('dp', 'tensor'))
- input_grad: float32 [8192, 1024], P(('dp', 'tensor'))
- first_gain_grad: float32 [1024], replicated
- first_bias_grad: float32 [1024], replicated
- second_gain_grad: float32 [1024], replicated
- second_bias_grad: float32 [1024], replicated
- time_weight_grad: float32 [256, 4, 1024], replicated
- time_bias_grad: float32 [4, 1024], replicated
- qkv_grad: float32 [1024, 3, 1024], P(None, None, 'tensor')
- out_weight_grad: float32 [1024, 1024], P('tensor')
- up_grad: float32 [1024, 4096], P(None, 'tensor')
- down_grad: float32 [4096, 1024], P('tensor')
The draws below stay inside these ranges and needn't reach their ends.
Inputs may be any that keep to these rules, and one draw needn't show every extreme that they name: `segment_ids`: in each row of 1024 positions the ids never fall; they are 0 at the first position and 3 at the last. Within a segment the positions rise by one from each place to the next; each row's first segment starts at 0 and its last segment ends at 2047.
All inputs are finite; a program needn't handle non-finite values.
Results may differ from the reference program's by a relative error of at most 0.014.
The reference program's roundings to bfloat16 on the way count: a program that leaves them out, or rounds other values in their place, can miss the bound.
Values may be sent and summed in bfloat16 or wider, within the bound.
No kernel may reach another device: no remote copies, remote signals or barrier semaphores. Data moves between devices by JAX's collectives and lax.ppermute only.
A program may use at most 128 MiB of HBM per device.

```python
import math
import jax
import jax.numpy as jnp
from jax import lax

D = 1024
HEADS = 16
HEAD = 64
FF = 4096
TE = 256
SEQ = 1024
ROWS = 8
TOKENS = 8192


def segment_layout(key):
    boundaries = jax.random.randint(jax.random.fold_in(key, 7), (ROWS, 3), 1, SEQ)
    offsets = jax.random.randint(jax.random.fold_in(key, 11), (ROWS, 4), 0, SEQ)
    last_start = jnp.max(boundaries, axis=1).astype(jnp.int32)
    offsets = offsets.at[:, 0].set(0)
    offsets = offsets.at[:, 3].set(SEQ + last_start)
    return (boundaries, offsets.astype(jnp.int32))


def draw_segment_ids(key, part):
    boundaries, offsets = segment_layout(key)
    places = jnp.arange(SEQ, dtype=jnp.int32)
    passed = (places[None, :, None] >= boundaries[:, None, :]).astype(jnp.int32)
    return jnp.sum(passed, axis=2).astype(jnp.int32)


def draw_positions(key, part):
    boundaries, offsets = segment_layout(key)
    places = jnp.arange(SEQ, dtype=jnp.int32)
    passed = places[None, :, None] >= boundaries[:, None, :]
    identity = jnp.sum(passed.astype(jnp.int32), axis=2).astype(jnp.int32)
    starts = jnp.max(jnp.where(passed, boundaries[:, None, :], 0), axis=2).astype(jnp.int32)
    shifted = jnp.take_along_axis(offsets, identity, axis=1).astype(jnp.int32)
    return (places[None, :] - starts + shifted).astype(jnp.int32)


def block_levels(key, extent, pieces, smallest, largest):
    level, own = 1.0, jax.random.fold_in(key, 6)
    for axis_at, blocks in pieces:
        heights = jnp.exp(jax.random.uniform(jax.random.fold_in(own, axis_at), (blocks,), jnp.float32, smallest / len(pieces), largest / len(pieces)))
        level = level * jnp.repeat(heights, extent[axis_at] // blocks).reshape([-1 if axis == axis_at else 1 for axis in range(len(extent))])
    return level


def centred(stream_key, shape, scale, most, shards=(), kind=jnp.bfloat16):
    drawn = jax.random.normal(stream_key, shape, jnp.float32) * scale
    if len(shards) > 0:
        drawn = block_levels(stream_key, shape, shards, -0.22, 0.18) * drawn
    return jnp.clip(drawn, min=-most, max=most).astype(kind)


def setup_inputs(seed: int = 0) -> dict:
    arg_keys = jax.random.split(jax.random.key(seed), 16)
    return {
        "tokens": centred(arg_keys[0], (TOKENS, D), 1.0, 6.0, ((0, 32),)),
        "time_embed": centred(arg_keys[1], (TOKENS, TE), 1.0, 6.0, ((0, 32),)),
        "segment_ids": draw_segment_ids(jax.random.fold_in(arg_keys[15], 71), 0),
        "positions": draw_positions(jax.random.fold_in(arg_keys[15], 71), 0),
        "first_gain": jnp.clip(1.0 + 0.18 * jax.random.normal(arg_keys[4], (D,), jnp.float32), 0.1, 1.9),
        "first_bias": centred(arg_keys[5], (D,), 0.3, 4.0, (), jnp.float32),
        "second_gain": jnp.clip(1.0 + 0.18 * jax.random.normal(arg_keys[6], (D,), jnp.float32), 0.1, 1.9),
        "second_bias": centred(arg_keys[7], (D,), 0.3, 4.0, (), jnp.float32),
        "time_weight": centred(arg_keys[8], (TE, 4, D), (4 * TE) ** -0.5, 0.1875),
        "time_bias": centred(arg_keys[9], (4, D), 0.3, 4.0, (), jnp.float32),
        "qkv_weight": centred(arg_keys[10], (D, 3, D), D ** -0.5, 0.1875, ((2, 4),)),
        "out_weight": centred(arg_keys[11], (D, D), (D // 16) ** -0.5, 0.75, ((0, 4),)),
        "up_weight": centred(arg_keys[12], (D, FF), D ** -0.5, 0.1875, ((1, 4),)),
        "down_weight": centred(arg_keys[13], (FF, D), FF ** -0.5, 0.09375, ((0, 4),)),
        "cotangent": centred(arg_keys[14], (TOKENS, D), 1.0, 6.0, ((0, 32),)),
    }


@jax.custom_vjp
def low(v):
    return lax.optimization_barrier(v.astype(jnp.bfloat16)).astype(jnp.float32)

@jax.custom_vjp
def low_back(v):
    return v

def low_keep(v):
    return (low(v), None)

def low_pass(kept, grad):
    return (grad,)

def back_keep(v):
    return (v, None)

def back_low(kept, grad):
    return (low(grad),)
low.defvjp(low_keep, low_pass)
low_back.defvjp(back_keep, back_low)

def matmul(left_side, right_side):
    return jnp.dot(left_side, right_side, precision=lax.Precision.HIGHEST)

def modulated_norm(values, norm_gain, norm_bias, mod_scale, mod_shift):
    centre = values - lax.optimization_barrier(jnp.mean(values, axis=-1, keepdims=True))
    spread = lax.optimization_barrier(jnp.mean(centre * centre, axis=-1, keepdims=True))
    normed = centre * lax.rsqrt(spread + 1e-05)
    return (normed * norm_gain + norm_bias) * (1.0 + mod_scale) + mod_shift

def rotary_tables(position_list):
    half_size = HEAD // 2
    frequency = jnp.exp(jnp.arange(half_size, dtype=jnp.float32) * (-math.log(10000.0) / half_size))
    angles = position_list.astype(jnp.float32)[:, None] * frequency[None, :]
    return (jnp.cos(angles)[:, None, :], jnp.sin(angles)[:, None, :])

def rotate(values, cosine_table, sine_table):
    first_half = values[..., :HEAD // 2]
    second_half = values[..., HEAD // 2:]
    return jnp.concatenate([first_half * cosine_table - second_half * sine_table, second_half * cosine_table + first_half * sine_table], axis=-1)

def attend_row(inputs):
    query_rows, key_rows, value_rows, segments = inputs
    score_scale = 1.0 / math.sqrt(HEAD)
    scores = jnp.einsum('qhd,khd->hqk', query_rows, key_rows, precision=lax.Precision.HIGHEST) * score_scale
    scores = low_back(scores)
    allowed = segments[:, None] == segments[None, :]
    scores = jnp.where(allowed[None], scores, -1e+30)
    row_peak = lax.optimization_barrier(jnp.max(scores, axis=-1, keepdims=True))
    raised = jnp.exp(scores - row_peak)
    attention = low(raised / lax.optimization_barrier(jnp.sum(raised, axis=-1, keepdims=True)))
    mixed_heads = jnp.einsum('hqk,khd->qhd', attention, value_rows, precision=lax.Precision.HIGHEST)
    return mixed_heads.reshape(SEQ, HEADS * HEAD)

def forward(tokens, first_gain, first_bias, second_gain, second_bias, time_weight, time_bias, qkv_weight, out_weight, up_weight, down_weight, time_embed, segment_ids, positions):
    row_total = tokens.shape[0]
    modulation = low_back(matmul(time_embed, time_weight.reshape(TE, 4 * D))).reshape(row_total, 4, D) + time_bias
    first_normed = low(modulated_norm(tokens, first_gain, first_bias, modulation[:, 0], modulation[:, 1]))
    projected = low_back(matmul(first_normed, qkv_weight.reshape(D, 3 * D))).reshape(row_total, 3, HEADS, HEAD)
    cosine_table, sine_table = rotary_tables(positions.reshape(-1))
    queries = low(rotate(projected[:, 0], cosine_table, sine_table))
    keys_all = low(rotate(projected[:, 1], cosine_table, sine_table))
    values_all = low(projected[:, 2])
    mixed_heads = lax.map(jax.checkpoint(attend_row), (queries.reshape(ROWS, SEQ, HEADS, HEAD), keys_all.reshape(ROWS, SEQ, HEADS, HEAD), values_all.reshape(ROWS, SEQ, HEADS, HEAD), segment_ids))
    mixed_heads = low_back(low(mixed_heads.reshape(row_total, D)))
    attended = low_back(matmul(mixed_heads, out_weight))
    residual = tokens + attended
    second_normed = low(modulated_norm(residual, second_gain, second_bias, modulation[:, 2], modulation[:, 3]))
    hidden = low_back(matmul(second_normed, up_weight))
    active = low(jax.nn.gelu(hidden, approximate=False))
    branch = low_back(matmul(active, down_weight))
    return residual + branch

def reference(tokens, time_embed, segment_ids, positions, first_gain, first_bias, second_gain, second_bias, time_weight, time_bias, qkv_weight, out_weight, up_weight, down_weight, cotangent):
    embed_float = time_embed.astype(jnp.float32)

    def closed(*parameters):
        return forward(*parameters, embed_float, segment_ids, positions)
    primals = (tokens.astype(jnp.float32), first_gain.astype(jnp.float32), first_bias.astype(jnp.float32), second_gain.astype(jnp.float32), second_bias.astype(jnp.float32), time_weight.astype(jnp.float32), time_bias.astype(jnp.float32), qkv_weight.astype(jnp.float32), out_weight.astype(jnp.float32), up_weight.astype(jnp.float32), down_weight.astype(jnp.float32))
    output_value, pullback = jax.vjp(closed, *primals)
    gradients = pullback(cotangent.astype(jnp.float32))
    return (output_value.astype(jnp.bfloat16), gradients[0], gradients[1], gradients[2], gradients[3], gradients[4], gradients[5], gradients[6], gradients[7], gradients[8], gradients[9], gradients[10])
```

```python
import math

import jax
import jax.numpy as jnp
from jax import lax
from jax.sharding import PartitionSpec as P

HEAD = 64


def modulated_norm(values, norm_gain, norm_bias, mod_scale, mod_shift):
    centre = values - jnp.mean(values, axis=-1, keepdims=True)
    spread = jnp.mean(centre * centre, axis=-1, keepdims=True)
    normed = centre * lax.rsqrt(spread + 1e-05)
    return (normed * norm_gain + norm_bias) * (1.0 + mod_scale) + mod_shift


def rotary_tables(position_list):
    half_size = HEAD // 2
    frequency = jnp.exp(jnp.arange(half_size, dtype=jnp.float32) * (-math.log(10000.0) / half_size))
    angles = position_list.astype(jnp.float32)[:, None] * frequency[None, :]
    return (jnp.cos(angles)[:, None, :], jnp.sin(angles)[:, None, :])


def rotate(values, cosine_table, sine_table):
    first_half = values[..., : HEAD // 2]
    second_half = values[..., HEAD // 2 :]
    return jnp.concatenate(
        [
            first_half * cosine_table - second_half * sine_table,
            second_half * cosine_table + first_half * sine_table,
        ],
        axis=-1,
    )


def unrotate(grads_in, cosine_table, sine_table):
    first_half = grads_in[..., : HEAD // 2]
    second_half = grads_in[..., HEAD // 2 :]
    return jnp.concatenate(
        [
            first_half * cosine_table + second_half * sine_table,
            second_half * cosine_table - first_half * sine_table,
        ],
        axis=-1,
    )


def gelu_exact(values):
    return jax.nn.gelu(values, approximate=False)


def masked_scores(query_block, key_rows, segment_block, segments, score_scale):
    scores = (
        jnp.einsum("qhd,khd->hqk", query_block, key_rows, preferred_element_type=jnp.float32)
        * score_scale
    )
    allowed = segment_block[:, None] == segments[None, :]
    return jnp.where(allowed[None], scores, -1e30)


def attend_row(inputs):
    query_rows, key_rows, value_rows, segments = inputs
    seq_len = query_rows.shape[0]
    block_len = min(512, seq_len)
    score_scale = 1.0 / math.sqrt(HEAD)
    outputs = []
    logsums = []
    for offset in range(0, seq_len, block_len):
        scores = masked_scores(
            query_rows[offset : offset + block_len],
            key_rows,
            segments[offset : offset + block_len],
            segments,
            score_scale,
        )
        row_peak = jnp.max(scores, axis=-1, keepdims=True)
        raised = jnp.exp(scores - row_peak)
        row_total = jnp.sum(raised, axis=-1, keepdims=True)
        attention = (raised / row_total).astype(jnp.bfloat16)
        mixed_block = jnp.einsum(
            "hqk,khd->qhd", attention, value_rows, preferred_element_type=jnp.float32
        )
        outputs.append(mixed_block.astype(jnp.bfloat16))
        logsums.append((row_peak + jnp.log(row_total))[..., 0])
    return (jnp.concatenate(outputs, axis=0), jnp.concatenate(logsums, axis=1))


def attend_back(inputs):
    query_rows, key_rows, value_rows, segments, logsum, mixed_grad = inputs
    seq_len = query_rows.shape[0]
    block_len = min(512, seq_len)
    score_scale = 1.0 / math.sqrt(HEAD)
    key_total = jnp.zeros(key_rows.shape, jnp.float32)
    value_total = jnp.zeros(value_rows.shape, jnp.float32)
    query_parts = []
    for offset in range(0, seq_len, block_len):
        query_block = query_rows[offset : offset + block_len]
        grad_block = mixed_grad[offset : offset + block_len]
        scores = masked_scores(
            query_block, key_rows, segments[offset : offset + block_len], segments, score_scale
        )
        probability = jnp.exp(scores - logsum[:, offset : offset + block_len, None])
        attention = probability.astype(jnp.bfloat16)
        value_total = value_total + jnp.einsum(
            "hqk,qhd->khd", attention, grad_block, preferred_element_type=jnp.float32
        )
        prob_grad = jnp.einsum(
            "qhd,khd->hqk", grad_block, value_rows, preferred_element_type=jnp.float32
        )
        row_dot = jnp.sum(probability * prob_grad, axis=-1, keepdims=True)
        score_grad = (probability * (prob_grad - row_dot)).astype(jnp.bfloat16)
        query_parts.append(
            jnp.einsum("hqk,khd->qhd", score_grad, key_rows, preferred_element_type=jnp.float32)
            * score_scale
        )
        key_total = (
            key_total
            + jnp.einsum(
                "hqk,qhd->khd", score_grad, query_block, preferred_element_type=jnp.float32
            )
            * score_scale
        )
    return (jnp.concatenate(query_parts, axis=0), key_total, value_total)


def local(
    tokens,
    time_embed,
    segment_ids,
    positions,
    first_gain,
    first_bias,
    second_gain,
    second_bias,
    time_weight,
    time_bias,
    qkv_weight,
    out_weight,
    up_weight,
    down_weight,
    cotangent,
):
    local_rows = tokens.shape[0]
    model_width = tokens.shape[1]
    embed_width = time_embed.shape[1]
    row_count, seq_len = segment_ids.shape
    group_rows = row_count * seq_len
    local_width = qkv_weight.shape[2]
    head_local = local_width // HEAD
    lead_pair = (((0,), (0,)), ((), ()))
    trail_pair = (((1,), (1,)), ((), ()))
    tokens_float = tokens.astype(jnp.float32)
    modulation = (
        jnp.dot(
            time_embed,
            time_weight.reshape(embed_width, 4 * model_width),
            preferred_element_type=jnp.float32,
        ).reshape(local_rows, 4, model_width)
        + time_bias
    )
    first_normed = modulated_norm(
        tokens_float, first_gain, first_bias, modulation[:, 0], modulation[:, 1]
    ).astype(jnp.bfloat16)
    first_all = lax.all_gather(first_normed, "tensor", axis=0, tiled=True)
    qkv_flat = qkv_weight.reshape(model_width, 3 * local_width)
    projected = jnp.dot(first_all, qkv_flat, preferred_element_type=jnp.float32)
    projected = projected.reshape(group_rows, 3, head_local, HEAD)
    cosine_table, sine_table = rotary_tables(positions.reshape(-1))
    row_shape = (row_count, seq_len, head_local, HEAD)
    queries = (
        rotate(projected[:, 0], cosine_table, sine_table).astype(jnp.bfloat16).reshape(row_shape)
    )
    keys_all = (
        rotate(projected[:, 1], cosine_table, sine_table).astype(jnp.bfloat16).reshape(row_shape)
    )
    values_all = projected[:, 2].astype(jnp.bfloat16).reshape(row_shape)
    mixed_heads, logsum = lax.map(attend_row, (queries, keys_all, values_all, segment_ids))
    mixed_flat = mixed_heads.reshape(group_rows, local_width)
    picked = lax.slice_in_dim(mixed_flat, 0, lax.axis_size("tensor") * local_rows, axis=0)
    attended = lax.psum_scatter(
        jnp.dot(picked, out_weight, preferred_element_type=jnp.float32).astype(jnp.bfloat16),
        "tensor",
        scatter_dimension=0,
        tiled=True,
    ).astype(jnp.float32)
    residual = tokens_float + attended
    second_normed = modulated_norm(
        residual, second_gain, second_bias, modulation[:, 2], modulation[:, 3]
    ).astype(jnp.bfloat16)
    second_all = lax.all_gather(second_normed, "tensor", axis=0, tiled=True)
    hidden = jnp.dot(second_all, up_weight, preferred_element_type=jnp.float32)
    active = gelu_exact(hidden).astype(jnp.bfloat16)
    picked = lax.slice_in_dim(active, 0, local_rows * lax.axis_size("tensor"), axis=0)
    branch = lax.psum_scatter(
        jnp.dot(picked, down_weight, preferred_element_type=jnp.float32).astype(jnp.bfloat16),
        "tensor",
        scatter_dimension=0,
        tiled=True,
    ).astype(jnp.float32)
    result = (residual + branch).astype(jnp.bfloat16)
    grad_float = cotangent.astype(jnp.float32)
    branch_all = lax.all_gather(cotangent, "tensor", axis=0, tiled=True)
    down_grad = lax.dot_general(active, branch_all, lead_pair, preferred_element_type=jnp.float32)
    active_grad = lax.dot_general(
        branch_all, down_weight, trail_pair, preferred_element_type=jnp.float32
    )
    gelu_value, gelu_pull = jax.vjp(gelu_exact, hidden)
    hidden_grad = gelu_pull(active_grad)[0].astype(jnp.bfloat16)
    up_grad = lax.dot_general(
        second_all, hidden_grad, lead_pair, preferred_element_type=jnp.float32
    )
    picked = lax.slice_in_dim(hidden_grad, 0, lax.axis_size("tensor") * local_rows, axis=0)
    second_grad = lax.psum_scatter(
        lax.dot_general(picked, up_weight, trail_pair, preferred_element_type=jnp.float32).astype(
            jnp.bfloat16
        ),
        "tensor",
        scatter_dimension=0,
        tiled=True,
    ).astype(jnp.float32)
    norm_value, second_pull = jax.vjp(
        modulated_norm, residual, second_gain, second_bias, modulation[:, 2], modulation[:, 3]
    )
    residual_back, second_gain_grad, second_bias_grad, scale_two_grad, shift_two_grad = second_pull(
        second_grad
    )
    residual_grad = grad_float + residual_back
    attended_all = lax.all_gather(residual_grad.astype(jnp.bfloat16), "tensor", axis=0, tiled=True)
    out_weight_grad = lax.dot_general(
        mixed_flat, attended_all, lead_pair, preferred_element_type=jnp.float32
    )
    mixed_grad = lax.dot_general(
        attended_all, out_weight, trail_pair, preferred_element_type=jnp.float32
    ).astype(jnp.bfloat16)
    query_grad, key_grad, value_grad = lax.map(
        attend_back,
        (queries, keys_all, values_all, segment_ids, logsum, mixed_grad.reshape(row_shape)),
    )
    flat_shape = (group_rows, head_local, HEAD)
    query_pre = unrotate(query_grad.reshape(flat_shape), cosine_table, sine_table)
    key_pre = unrotate(key_grad.reshape(flat_shape), cosine_table, sine_table)
    projected_grad = jnp.stack([query_pre, key_pre, value_grad.reshape(flat_shape)], axis=1)
    projected_grad = projected_grad.astype(jnp.bfloat16).reshape(group_rows, 3 * local_width)
    qkv_grad = lax.dot_general(
        first_all, projected_grad, lead_pair, preferred_element_type=jnp.float32
    )
    qkv_grad = qkv_grad.reshape(model_width, 3, local_width)
    picked = projected_grad
    first_grad = lax.psum_scatter(
        lax.dot_general(picked, qkv_flat, trail_pair, preferred_element_type=jnp.float32).astype(
            jnp.bfloat16
        ),
        "tensor",
        scatter_dimension=0,
        tiled=True,
    ).astype(jnp.float32)
    first_value, first_pull = jax.vjp(
        modulated_norm, tokens_float, first_gain, first_bias, modulation[:, 0], modulation[:, 1]
    )
    input_back, first_gain_grad, first_bias_grad, scale_one_grad, shift_one_grad = first_pull(
        first_grad
    )
    input_grad = residual_grad + input_back
    modulation_grad = jnp.stack(
        [scale_one_grad, shift_one_grad, scale_two_grad, shift_two_grad], axis=1
    )
    time_bias_grad = jnp.sum(modulation_grad, axis=0)
    time_weight_grad = lax.dot_general(
        time_embed,
        modulation_grad.astype(jnp.bfloat16).reshape(local_rows, 4 * model_width),
        lead_pair,
        preferred_element_type=jnp.float32,
    ).reshape(embed_width, 4, model_width)
    shared = lax.psum(
        (
            first_gain_grad,
            first_bias_grad,
            second_gain_grad,
            second_bias_grad,
            time_weight_grad.astype(jnp.bfloat16),
            time_bias_grad,
        ),
        ("dp", "tensor"),
    )
    halves = lax.psum(
        tuple(
            part.astype(jnp.bfloat16) for part in (qkv_grad, out_weight_grad, up_grad, down_grad)
        ),
        "dp",
    )
    qkv_summed, out_summed, up_summed, down_summed = (part.astype(jnp.float32) for part in halves)
    return (
        result,
        input_grad,
        shared[0],
        shared[1],
        shared[2],
        shared[3],
        shared[4].astype(jnp.float32),
        shared[5],
        qkv_summed,
        out_summed,
        up_summed,
        down_summed,
    )


def solution(mesh):
    return jax.shard_map(
        local,
        mesh=mesh,
        in_specs=(
            P(("dp", "tensor"), None),
            P(("dp", "tensor"), None),
            P("dp", None),
            P("dp", None),
            P(),
            P(),
            P(),
            P(),
            P(),
            P(),
            P(None, None, "tensor"),
            P("tensor", None),
            P(None, "tensor"),
            P("tensor", None),
            P(("dp", "tensor"), None),
        ),
        out_specs=(
            P(("dp", "tensor"), None),
            P(("dp", "tensor"), None),
            P(),
            P(),
            P(),
            P(),
            P(),
            P(),
            P(None, None, "tensor"),
            P("tensor", None),
            P(None, "tensor"),
            P("tensor", None),
        ),
        check_vma=False,
    )
```

```python
import math

import jax
import jax.numpy as jnp
from jax import lax
from jax.sharding import Mesh
from jax.sharding import PartitionSpec as P

HEAD = 64
F32 = jnp.float32
BF16 = jnp.bfloat16
LEAD = (((0,), (0,)), ((), ()))
TRAIL = (((1,), (1,)), ((), ()))


def product(left, right, dims=(((1,), (0,)), ((), ()))):
    return lax.dot_general(left, right, dims, preferred_element_type=F32)


def norm_parts(values):
    centre = values - jnp.mean(values, axis=-1, keepdims=True)
    spread = jnp.mean(centre * centre, axis=-1, keepdims=True)
    scale = lax.rsqrt(spread + 1e-05)
    return (centre * scale, scale)


def norm_input_back(grads, normed, scale, gain, mod_scale):
    inner = grads * (1.0 + mod_scale) * gain
    return scale * (
        inner
        - jnp.mean(inner, axis=-1, keepdims=True)
        - normed * jnp.mean(inner * normed, axis=-1, keepdims=True)
    )


def rotary_tables(position_list):
    half_size = HEAD // 2
    frequency = jnp.exp(jnp.arange(half_size, dtype=F32) * (-math.log(10000.0) / half_size))
    angles = position_list.astype(F32)[:, None] * frequency[None, :]
    return (jnp.cos(angles)[:, None, :], jnp.sin(angles)[:, None, :])


def rotate(values, cosine_table, sine_table):
    first_half = values[..., : HEAD // 2]
    second_half = values[..., HEAD // 2 :]
    return jnp.concatenate(
        [
            first_half * cosine_table - second_half * sine_table,
            second_half * cosine_table + first_half * sine_table,
        ],
        axis=-1,
    )


def unrotate(grads_in, cosine_table, sine_table):
    return rotate(grads_in, cosine_table, -sine_table)


def masked_scores(query_block, key_rows, segment_block, segments, score_scale):
    scores = (
        jnp.einsum("qhd,khd->hqk", query_block, key_rows, preferred_element_type=F32) * score_scale
    )
    allowed = segment_block[:, None] == segments[None, :]
    return jnp.where(allowed[None], scores, -1e30)


def attend_block(query_block, key_rows, value_rows, segment_block, segments):
    scores = masked_scores(query_block, key_rows, segment_block, segments, 1.0 / math.sqrt(HEAD))
    row_peak = jnp.max(scores, axis=-1, keepdims=True)
    raised = jnp.exp(scores - row_peak)
    row_total = jnp.sum(raised, axis=-1, keepdims=True)
    attention = (raised / row_total).astype(BF16)
    mixed = jnp.einsum("hqk,khd->qhd", attention, value_rows, preferred_element_type=F32)
    return (mixed.astype(BF16), row_peak + jnp.log(row_total))


def attend_back_block(query_block, key_rows, value_rows, segment_block, segments, logsum, grad_block):
    score_scale = 1.0 / math.sqrt(HEAD)
    scores = masked_scores(query_block, key_rows, segment_block, segments, score_scale)
    probability = jnp.exp(scores - logsum)
    attention = probability.astype(BF16)
    value_part = jnp.einsum("hqk,qhd->khd", attention, grad_block, preferred_element_type=F32)
    prob_grad = jnp.einsum("qhd,khd->hqk", grad_block, value_rows, preferred_element_type=F32)
    row_dot = jnp.sum(probability * prob_grad, axis=-1, keepdims=True)
    score_grad = (probability * (prob_grad - row_dot)).astype(BF16)
    query_part = (
        jnp.einsum("hqk,khd->qhd", score_grad, key_rows, preferred_element_type=F32) * score_scale
    )
    key_part = (
        jnp.einsum("hqk,qhd->khd", score_grad, query_block, preferred_element_type=F32)
        * score_scale
    )
    return (query_part, key_part, value_part)


def swap(values, axis_name, bit):
    size = lax.axis_size(axis_name)
    return lax.ppermute(values, axis_name, [(at, at ^ (1 << bit)) for at in range(size)])


def bit_of(axis_name, bit):
    return (lax.axis_index(axis_name) >> bit) & 1


def halve(values, axis_name, bit, dim):
    own = bit_of(axis_name, bit)
    kept = lax.dynamic_index_in_dim(values, own, dim, keepdims=False)
    sent = lax.dynamic_index_in_dim(values, 1 - own, dim, keepdims=False)
    got = swap(sent, axis_name, bit)
    return (kept.astype(F32) + got.astype(F32)).astype(BF16)


def double(values, axis_name, bit, dim):
    own = bit_of(axis_name, bit) == 0
    got = swap(values, axis_name, bit)
    return jnp.stack([jnp.where(own, values, got), jnp.where(own, got, values)], axis=dim)


def plane_scatter(values, order, dim):
    bits = len(order)
    shape = values.shape
    values = values.reshape(shape[:dim] + (2,) * bits + shape[dim + 1 :])
    left = list(range(bits - 1, -1, -1))
    for bit in order:
        values = halve(values, "plane", bit, dim + left.index(bit))
        left.remove(bit)
    return values


def plane_gather(values, order, dim):
    bits = len(order)
    left = []
    for bit in reversed(order):
        left = sorted(left + [bit], reverse=True)
        values = double(values, "plane", bit, dim + left.index(bit))
    shape = values.shape
    return values.reshape(shape[:dim] + (1 << bits,) + shape[dim + bits :])


def tensor_scatter(values):
    size = lax.axis_size("tensor")
    own = lax.axis_index("tensor")
    total = lax.dynamic_index_in_dim(values, own, 0, keepdims=False).astype(F32)
    for hop in range(1, size):
        sent = lax.dynamic_index_in_dim(values, (own + hop) % size, 0, keepdims=False)
        got = lax.ppermute(sent, "tensor", [(at, (at + hop) % size) for at in range(size)])
        total = total + got.astype(F32)
    return total.astype(BF16)


def ring_gather(shard):
    size = lax.axis_size("tensor")
    half = shard.shape[0] // 2
    right, left = [shard[:half]], [shard[half:]]
    for _ in range(size - 1):
        right.append(lax.ppermute(right[-1], "tensor", [(at, (at + 1) % size) for at in range(size)]))
        left.append(lax.ppermute(left[-1], "tensor", [(at, (at - 1) % size) for at in range(size)]))
    return [(right[(size - at) % size], left[at]) for at in range(size)]


def ring_scatter(chunks):
    size = len(chunks)
    half = chunks[0].shape[0] // 2
    right = chunks[size - 1][:half]
    left = chunks[1 % size][half:]
    for step in range(1, size):
        right = lax.ppermute(right, "tensor", [(at, (at + 1) % size) for at in range(size)])
        left = lax.ppermute(left, "tensor", [(at, (at - 1) % size) for at in range(size)])
        right = right.astype(F32) + chunks[size - 1 - step][:half].astype(F32)
        left = left.astype(F32) + chunks[(step + 1) % size][half:].astype(F32)
        if step < size - 1:
            right, left = right.astype(BF16), left.astype(BF16)
    return jnp.concatenate([right, left], axis=0)


def after(values, *others):
    return lax.optimization_barrier((values, others))[0]


def own_first(values, dim):
    size = lax.axis_size("tensor")
    stretch = values.shape[dim] // size
    doubled = jnp.concatenate([values, values], axis=dim)
    return lax.dynamic_slice_in_dim(
        doubled, lax.axis_index("tensor") * stretch, values.shape[dim], dim
    )


def tensor_sum(values):
    size = lax.axis_size("tensor")
    for bit in range(size.bit_length() - 1):
        values = (values.astype(F32) + swap(values, "tensor", bit).astype(F32)).astype(BF16)
    return values


def local(
    tokens,
    time_embed,
    segment_ids,
    positions,
    first_gain,
    first_bias,
    second_gain,
    second_bias,
    time_weight,
    time_bias,
    qkv_weight,
    out_weight,
    up_weight,
    down_weight,
    cotangent,
):
    local_rows, width = tokens.shape
    embed_width = time_embed.shape[1]
    group_rows = segment_ids.shape[1]
    local_width = qkv_weight.shape[2]
    head_local = local_width // HEAD
    hidden_local = up_weight.shape[1]
    half_hidden = hidden_local // 2
    planes = lax.axis_size("plane")
    groups = lax.axis_size("tensor")
    plane_at = lax.axis_index("plane")
    core_at = lax.axis_index("core")
    rising = list(range(planes.bit_length() - 1))
    falling = rising[::-1]

    up_rows = width // planes
    up_piece = lax.dynamic_slice(
        up_weight, (plane_at * up_rows, core_at * half_hidden), (up_rows, half_hidden)
    )
    down_rows = half_hidden // planes
    down_piece = lax.dynamic_slice(
        down_weight, (core_at * half_hidden + plane_at * down_rows, 0), (down_rows, width)
    )
    gathered = ring_gather(jnp.concatenate([tokens, time_embed], axis=1))
    gathered = jnp.concatenate([half for pair in gathered for half in pair], axis=0)
    tokens_all = gathered[:, :width]
    embed_all = gathered[:, width:]
    segments = own_first(segment_ids, 1)[0]
    places = own_first(positions, 1)[0]
    up_all = lax.all_gather(up_piece, ("tensor", "plane"), axis=0, tiled=True)
    up_all = up_all.reshape(groups, width, half_hidden)
    down_all = lax.all_gather(down_piece, ("tensor", "plane"), axis=0, tiled=True)
    down_all = down_all.reshape(groups, half_hidden, width)

    time_flat = time_weight.reshape(embed_width, 4 * width)
    bias_flat = time_bias.reshape(4 * width)

    tokens_float = tokens_all.astype(F32)
    normed_all, _ = norm_parts(tokens_float)
    mod_all = product(embed_all, time_flat[:, : 2 * width]) + bias_flat[: 2 * width]
    base_all = normed_all * first_gain + first_bias
    scale_all = 1.0 + mod_all[:, :width]
    first_all = (base_all * scale_all + mod_all[:, width:]).astype(BF16)

    qkv_flat = qkv_weight.reshape(width, 3 * local_width)
    projected = product(first_all, qkv_flat).reshape(group_rows, 3, head_local, HEAD)
    cosine_table, sine_table = rotary_tables(places)
    queries = rotate(projected[:, 0], cosine_table, sine_table).astype(BF16)
    keys_all = rotate(projected[:, 1], cosine_table, sine_table).astype(BF16)
    values_all = projected[:, 2].astype(BF16)
    spans = [slice(at * local_rows, (at + 1) * local_rows) for at in range(groups)]
    forward_blocks = [
        attend_block(queries[span], keys_all, values_all, segments[span], segments)
        for span in spans
    ]
    mixed_blocks = [pair[0].reshape(local_rows, local_width) for pair in forward_blocks]
    attended = ring_scatter([product(block, out_weight).astype(BF16) for block in mixed_blocks])
    own_tokens = tokens.astype(F32)
    residual = own_tokens + attended

    mod_own = product(time_embed, time_flat) + bias_flat
    second_base_normed, second_scale = norm_parts(residual)
    second_base = second_base_normed * second_gain + second_bias
    mod_two = mod_own[:, 2 * width : 3 * width]
    second_normed = (second_base * (1.0 + mod_two) + mod_own[:, 3 * width :]).astype(BF16)
    second_both = jnp.concatenate([second_normed, swap(second_normed, "core", 0)], axis=0)
    grad_both = jnp.concatenate([cotangent, swap(cotangent, "core", 0)], axis=0)

    branch_part = 0.0
    second_part = 0.0
    up_parts = []
    down_parts = []
    for at in range(groups):
        hidden = product(second_both, up_all[at])
        tail = 0.5 * (1.0 + lax.erf(hidden * math.sqrt(0.5)))
        slope = tail + hidden * jnp.exp(hidden * hidden * -0.5) * (1.0 / math.sqrt(2.0 * math.pi))
        active = (hidden * tail).astype(BF16)
        branch_part = branch_part + product(active, down_all[at])
        down_parts.append(product(active, grad_both, LEAD).astype(BF16))
        hidden_grad = (product(grad_both, down_all[at], TRAIL) * slope).astype(BF16)
        second_part = second_part + product(hidden_grad, up_all[at], TRAIL)
        up_parts.append(product(second_both, hidden_grad, LEAD).astype(BF16))
    second_grad = second_part[:local_rows] + swap(second_part[local_rows:], "core", 0)
    branch = branch_part[:local_rows] + swap(branch_part[local_rows:], "core", 0)
    result = (residual + branch).astype(BF16)

    residual_grad = cotangent.astype(F32) + norm_input_back(
        second_grad, second_base_normed, second_scale, second_gain, mod_two
    )
    second_weighted = second_grad * (1.0 + mod_two)
    scale_two_grad = second_grad * second_base

    down_stack = jnp.stack(down_parts).reshape(groups, planes, down_rows, width)
    up_stack = jnp.stack(up_parts).reshape(groups, planes, up_rows, half_hidden)
    down_sum = plane_scatter(down_stack, rising, 1)
    up_sum = plane_scatter(up_stack, falling, 1)

    attended_halves = ring_gather(residual_grad.astype(BF16))
    attended_blocks = [jnp.concatenate(pair, axis=0) for pair in attended_halves]
    attended_all = jnp.concatenate(attended_blocks, axis=0)
    out_weight_grad = product(jnp.concatenate(mixed_blocks, axis=0), attended_all, LEAD).astype(BF16)
    back_blocks = [
        attend_back_block(
            queries[span],
            keys_all,
            values_all,
            segments[span],
            segments,
            pair[1],
            product(block, out_weight, TRAIL).astype(BF16).reshape(local_rows, head_local, HEAD),
        )
        for span, pair, block in zip(spans, forward_blocks, attended_blocks)
    ]
    query_grad = jnp.concatenate([triple[0] for triple in back_blocks], axis=0)
    key_grad = sum(triple[1] for triple in back_blocks)
    value_grad = sum(triple[2] for triple in back_blocks)
    query_pre = unrotate(query_grad, cosine_table, sine_table)
    key_pre = unrotate(key_grad, cosine_table, sine_table)
    projected_grad = jnp.stack([query_pre, key_pre, value_grad], axis=1)
    projected_grad = projected_grad.astype(BF16).reshape(group_rows, 3 * local_width)
    projected_grad = after(projected_grad, down_sum, up_sum)
    first_part = product(projected_grad, qkv_flat, TRAIL)
    first_half = first_part.astype(BF16)
    first_grad = ring_scatter([first_half[span] for span in spans])
    qkv_grad = product(first_all, projected_grad, LEAD).astype(BF16)

    down_own = tensor_scatter(down_sum)
    up_own = tensor_scatter(up_sum)
    down_half = plane_gather(down_own, rising, 0).reshape(half_hidden, width)
    up_half = plane_gather(up_own, falling, 0).reshape(width, half_hidden)
    down_summed = double(down_half, "core", 0, 0).reshape(hidden_local, width).astype(F32)
    up_summed = double(up_half, "core", 0, 1).reshape(width, hidden_local).astype(F32)

    scale_one_part = first_part * base_all
    weighted = first_part * scale_all
    small = jnp.stack(
        [
            jnp.sum(weighted * normed_all, axis=0),
            jnp.sum(weighted, axis=0),
            jnp.sum(second_weighted * second_base_normed, axis=0),
            jnp.sum(second_weighted, axis=0),
            jnp.sum(scale_one_part, axis=0),
            jnp.sum(first_part, axis=0),
            jnp.sum(scale_two_grad, axis=0),
            jnp.sum(second_grad, axis=0),
        ]
    )
    time_parts = [
        product(embed_all, scale_one_part.astype(BF16), LEAD).astype(BF16),
        product(embed_all, first_half, LEAD).astype(BF16),
        product(time_embed, scale_two_grad.astype(BF16), LEAD).astype(BF16),
        product(time_embed, second_grad.astype(BF16), LEAD).astype(BF16),
    ]
    lanes = 8 * width // embed_width
    small_rows = jnp.pad(small.reshape(embed_width, lanes), ((0, 0), (0, -lanes % 128))).astype(BF16)
    blocks = width // embed_width
    qkv_blocks = [qkv_grad[at * embed_width : (at + 1) * embed_width] for at in range(blocks)]
    shared_pack = jnp.concatenate(time_parts + [small_rows], axis=1)
    share_width = shared_pack.shape[1]
    pack = jnp.concatenate([shared_pack, out_weight_grad] + qkv_blocks, axis=1)
    pack = halve(pack.reshape(2, embed_width // 2, -1), "core", 0, 0)
    pack = pack.reshape(planes, embed_width // (2 * planes), -1)
    pack = plane_scatter(pack, rising, 0)
    pack = jnp.concatenate([tensor_sum(pack[:, :share_width]), pack[:, share_width:]], axis=1)
    pack = plane_gather(pack, rising, 0).reshape(embed_width // 2, -1)
    pack = double(pack, "core", 0, 0).reshape(embed_width, -1)
    time_weight_grad = pack[:, : 4 * width].astype(F32).reshape(embed_width, 4, width)
    small = pack[:, 4 * width : 4 * width + lanes].astype(F32).reshape(8, width)
    at = share_width
    out_summed = pack[:, at : at + width].astype(F32)
    at += width
    qkv_summed = jnp.concatenate(
        [
            pack[:, at + 3 * local_width * block : at + 3 * local_width * (block + 1)]
            for block in range(blocks)
        ],
        axis=0,
    )
    qkv_summed = qkv_summed.astype(F32).reshape(width, 3, local_width)

    own_normed, own_scale = norm_parts(own_tokens)
    input_grad = residual_grad + norm_input_back(
        first_grad, own_normed, own_scale, first_gain, mod_own[:, :width]
    )
    return (
        result,
        input_grad,
        small[0],
        small[1],
        small[2],
        small[3],
        time_weight_grad,
        small[4:],
        qkv_summed,
        out_summed,
        up_summed,
        down_summed,
    )


def solution(mesh):
    whole, tensor = mesh.devices.shape
    finer = Mesh(mesh.devices.reshape(whole // 2, 2, tensor), ("plane", "core", "tensor"))
    rows = P(("plane", "core", "tensor"), None)
    group = P(("plane", "core"), None)
    return jax.shard_map(
        local,
        mesh=finer,
        in_specs=(
            rows,
            rows,
            group,
            group,
            P(),
            P(),
            P(),
            P(),
            P(),
            P(),
            P(None, None, "tensor"),
            P("tensor", None),
            P(None, "tensor"),
            P("tensor", None),
            rows,
        ),
        out_specs=(
            rows,
            rows,
            P(),
            P(),
            P(),
            P(),
            P(),
            P(),
            P(None, None, "tensor"),
            P("tensor", None),
            P(None, "tensor"),
            P("tensor", None),
        ),
        check_vma=False,
    )
```

```python
import functools
import math

import jax
import jax.numpy as jnp
from jax import lax
from jax.experimental import pallas as pl
from jax.experimental.pallas import tpu as pltpu
from jax.sharding import Mesh
from jax.sharding import PartitionSpec as P

HEAD = 64
F32 = jnp.float32
BF16 = jnp.bfloat16
LEAD = (((0,), (0,)), ((), ()))
TRAIL = (((1,), (1,)), ((), ()))


def product(left, right, dims=(((1,), (0,)), ((), ()))):
    return lax.dot_general(left, right, dims, preferred_element_type=F32)


def norm_parts(values):
    centre = values - jnp.mean(values, axis=-1, keepdims=True)
    spread = jnp.mean(centre * centre, axis=-1, keepdims=True)
    scale = lax.rsqrt(spread + 1e-05)
    return (centre * scale, scale)


def norm_input_back(grads, normed, scale, gain, mod_scale):
    inner = grads * (1.0 + mod_scale) * gain
    return scale * (
        inner
        - jnp.mean(inner, axis=-1, keepdims=True)
        - normed * jnp.mean(inner * normed, axis=-1, keepdims=True)
    )


def rotary_tables(places, lanes):
    half_size = HEAD // 2
    lane = jnp.arange(lanes)
    frequency = jnp.exp((lane % half_size).astype(F32) * (-math.log(10000.0) / half_size))
    angles = places.astype(F32)[:, None] * frequency[None, :]
    sign = jnp.where(lane % HEAD < half_size, -1.0, 1.0)
    return (jnp.cos(angles), jnp.sin(angles) * sign[None, :])


def kept_out(*arrays):
    return tuple(pltpu.with_memory_space_constraint(each, pltpu.HBM) for each in arrays)


def block_of(shape, *place):
    return pl.BlockSpec(shape, lambda *_: place)


def whole(*shape):
    return pl.BlockSpec(shape, lambda *_: (0,) * len(shape))


def limits(megabytes):
    return pltpu.CompilerParams(vmem_limit_bytes=megabytes << 20)


def partner(values):
    lanes = values.shape[1]
    lane = lax.broadcasted_iota(jnp.int32, values.shape, 1)
    above = pltpu.roll(values, lanes - HEAD // 2, 1)
    below = pltpu.roll(values, HEAD // 2, 1)
    return jnp.where(lane % HEAD < HEAD // 2, above, below)


def widened(table, lanes):
    return jnp.concatenate([table] * (lanes // table.shape[1]), axis=1)


def turned(values, cosine, sine):
    return values * widened(cosine, values.shape[1]) + partner(values) * widened(sine, values.shape[1])


def entry_kernel(
    *refs, count
):
    halves, refs = refs[: 2 * count], refs[2 * count :]
    cosine_ref, sine_ref, time_ref, bias_ref, gain_ref, shift_ref, weight_ref = refs[:7]
    tokens_ref, first_ref, query_ref, key_ref, value_ref = refs[-5:]
    rows = jnp.concatenate([halves[0][...], halves[1][...]], axis=0)
    for at in range(1, count):
        other = jnp.concatenate([halves[2 * at][...], halves[2 * at + 1][...]], axis=0)
        rows = jnp.where(pl.program_id(0) == at, other, rows)
    tokens_ref[...] = rows
    width = gain_ref.shape[1]
    mod = product(rows[:, width:], time_ref[...]) + bias_ref[...]
    normed, _ = norm_parts(rows[:, :width].astype(F32))
    base = normed * gain_ref[...] + shift_ref[...]
    first = (base * (1.0 + mod[:, :width]) + mod[:, width:]).astype(BF16)
    first_ref[...] = first
    cosine, sine = cosine_ref[...], sine_ref[...]
    query_ref[...] = turned(product(first, weight_ref[0]), cosine, sine).astype(BF16)
    key_ref[...] = turned(product(first, weight_ref[1]), cosine, sine).astype(BF16)
    value_ref[...] = product(first, weight_ref[2]).astype(BF16)


def entry(halves, tables, time_flat, bias, gain, shift, weight, places, groups, before):
    half, both = halves[0].shape
    count = len(places)
    apart = places[-1] - places[0]
    rows = 2 * half
    width = gain.shape[1]
    part = weight.shape[2]
    lanes = tables[0].shape[1]
    widths = (both, width, part, part, part)
    table = pl.BlockSpec((rows, lanes), lambda i: (places[0] + i * apart, 0))
    inputs = (*halves, *kept_out(*tables, time_flat, bias, gain, shift, weight))
    return pl.pallas_call(
        functools.partial(entry_kernel, count=count),
        grid=(count,),
        in_specs=[whole(half, both)] * (2 * count)
        + [table, table]
        + [block_of((both - width, 2 * width), 0, 0), block_of((1, 2 * width), 0, 0)]
        + [whole(*each.shape) for each in (gain, shift, weight)]
        + [pl.BlockSpec(memory_space=pl.ANY)] * len(before),
        out_specs=[pl.BlockSpec((rows, each), lambda i: (places[0] + i * apart, 0)) for each in widths],
        out_shape=[pltpu.HBM((rows * groups, each), BF16) for each in widths],
        input_output_aliases={len(inputs) + at: at for at in range(len(before))},
        compiler_params=limits(16),
        cost_estimate=pl.CostEstimate(
            flops=2 * rows * width * 4 * part + 4 * rows * width * (both - width),
            bytes_accessed=8 * rows * width + 6 * width * part,
            transcendentals=rows,
        ),
    )(*inputs, *kept_out(*before))


def head_lanes(values, head):
    pair = values[:, head // 2 * 2 * HEAD : (head // 2 + 1) * 2 * HEAD]
    lane = lax.broadcasted_iota(jnp.int32, pair.shape, 1)
    return jnp.where(lane // HEAD == head % 2, pair, jnp.zeros_like(pair))


def pair_lanes(values, head):
    return values[:, head // 2 * 2 * HEAD : (head // 2 + 1) * 2 * HEAD]


def attend_kernel(query_ref, key_ref, value_ref, own_ref, all_ref, out_ref, mixed_ref, logsum_ref, part_ref):
    queries, keys, values = query_ref[...], key_ref[...], value_ref[...]
    allowed = all_ref[...] == own_ref[...]
    scale = 1.0 / math.sqrt(HEAD)
    pairs = []
    for head in range(queries.shape[1] // HEAD):
        scores = product(pair_lanes(keys, head), head_lanes(queries, head), TRAIL) * scale
        scores = jnp.where(allowed, scores, -1e30)
        peak = jnp.max(scores, axis=0, keepdims=True)
        raised = jnp.exp(scores - peak)
        total = jnp.sum(raised, axis=0, keepdims=True)
        attention = (raised / total).astype(BF16)
        logsum_ref[head : head + 1, :] = peak + jnp.log(total)
        mixed = product(attention, pair_lanes(values, head), LEAD)
        if head % 2 == 0:
            pairs.append(mixed)
        else:
            lane = lax.broadcasted_iota(jnp.int32, mixed.shape, 1)
            pairs[-1] = jnp.where(lane < HEAD, pairs[-1], mixed)
    mixed = jnp.concatenate(pairs, axis=1).astype(BF16)
    mixed_ref[...] = mixed
    part_ref[...] = product(mixed, out_ref[...]).astype(BF16)


def attend(queries, keys, values, own_segments, all_segments, out_weight, place, rows):
    seq, part = keys.shape
    width = out_weight.shape[1]
    heads = part // HEAD
    return pl.pallas_call(
        attend_kernel,
        grid=(1,),
        in_specs=[
            pl.BlockSpec((rows, part), lambda i: (place, 0)),
            whole(seq, part),
            whole(seq, part),
            pl.BlockSpec((1, rows), lambda i: (0, place)),
            whole(seq, 1),
            whole(part, width),
        ],
        out_specs=[whole(rows, part), whole(heads, rows), whole(rows, width)],
        out_shape=[
            pltpu.HBM((rows, part), BF16),
            pltpu.HBM((heads, rows), F32),
            jax.ShapeDtypeStruct((rows, width), BF16),
        ],
        compiler_params=limits(16),
        cost_estimate=pl.CostEstimate(
            flops=4 * rows * seq * part + 2 * rows * part * width,
            bytes_accessed=4 * seq * part + 4 * rows * width,
            transcendentals=rows * seq * heads,
        ),
    )(queries, keys, values, own_segments, all_segments, out_weight)


def attend_back_kernel(
    query_ref, key_ref, value_ref, own_ref, all_ref, out_ref, cosine_ref, sine_ref, *refs, count
):
    halves, logsum_refs, (grad_ref, key_grad_ref, value_grad_ref) = (
        refs[: 2 * count],
        refs[2 * count : 3 * count],
        refs[3 * count :],
    )
    step = pl.program_id(0)
    queries, keys, values = query_ref[...], key_ref[...], value_ref[...]
    incoming = jnp.concatenate([halves[0][...], halves[1][...]], axis=0)
    logsums = logsum_refs[0][...]
    for at in range(1, count):
        other = jnp.concatenate([halves[2 * at][...], halves[2 * at + 1][...]], axis=0)
        incoming = jnp.where(step == at, other, incoming)
        logsums = jnp.where(step == at, logsum_refs[at][...], logsums)
    mixed_grad = product(incoming, out_ref[...], TRAIL).astype(BF16)
    allowed = all_ref[...] == own_ref[...]
    scale = 1.0 / math.sqrt(HEAD)
    query_pairs, key_pairs, value_pairs = [], [], []
    for head in range(queries.shape[1] // HEAD):
        query, grad = head_lanes(queries, head), head_lanes(mixed_grad, head)
        scores = product(pair_lanes(keys, head), query, TRAIL) * scale
        scores = jnp.where(allowed, scores, -1e30)
        probability = jnp.exp(scores - logsums[head : head + 1, :])
        prob_grad = product(pair_lanes(values, head), grad, TRAIL)
        row_dot = jnp.sum(probability * prob_grad, axis=0, keepdims=True)
        score_grad = (probability * (prob_grad - row_dot)).astype(BF16)
        value_part = product(probability.astype(BF16), grad)
        key_part = product(score_grad, query)
        query_part = product(score_grad, head_lanes(keys, head), LEAD)
        if head % 2 == 0:
            query_pairs.append(query_part)
            key_pairs.append(key_part)
            value_pairs.append(value_part)
        else:
            query_pairs[-1] += query_part
            key_pairs[-1] += key_part
            value_pairs[-1] += value_part
    query_grad = jnp.concatenate(query_pairs, axis=1) * scale
    key_grad = jnp.concatenate(key_pairs, axis=1) * scale
    value_grad = jnp.concatenate(value_pairs, axis=1)
    grad_ref[...] = turned(query_grad, cosine_ref[...], -sine_ref[...]).astype(BF16)

    @pl.when(step == 0)
    def _():
        key_grad_ref[...] = key_grad
        value_grad_ref[...] = value_grad

    @pl.when(step > 0)
    def _():
        key_grad_ref[...] += key_grad
        value_grad_ref[...] += value_grad


def attend_back(halves, queries, keys, values, logsums, own_segments, all_segments, out_weight, tables, places):
    seq, part = keys.shape
    heads, rows = logsums[0].shape
    width = out_weight.shape[1]
    count = len(places)
    apart = places[-1] - places[0]
    shard = pl.BlockSpec((rows, part), lambda i: (places[0] + i * apart, 0))
    table = pl.BlockSpec((rows, tables[0].shape[1]), lambda i: (places[0] + i * apart, 0))
    constants = (own_segments, all_segments, out_weight, *tables)
    return pl.pallas_call(
        functools.partial(attend_back_kernel, count=count),
        grid=(count,),
        in_specs=[
            shard,
            whole(seq, part),
            whole(seq, part),
            pl.BlockSpec((1, rows), lambda i: (0, places[0] + i * apart)),
            whole(seq, 1),
            whole(part, width),
            table,
            table,
        ]
        + [whole(rows // 2, width)] * (2 * count)
        + [whole(heads, rows)] * count,
        out_specs=[
            pl.BlockSpec((rows, part), lambda i: (i, 0)),
            whole(seq, part),
            whole(seq, part),
        ],
        out_shape=[
            pltpu.HBM((count * rows, part), BF16),
            pltpu.HBM((seq, part), F32),
            pltpu.HBM((seq, part), F32),
        ],
        compiler_params=limits(32),
        cost_estimate=pl.CostEstimate(
            flops=10 * count * rows * seq * part + 2 * count * rows * part * width,
            bytes_accessed=16 * seq * part,
            transcendentals=count * rows * seq * heads,
        ),
    )(queries, keys, values, *kept_out(*constants), *halves, *kept_out(*logsums))


def exit_kernel(
    place_ref, cosine_ref, sine_ref, tokens_ref, first_ref, *refs, groups, calls
):
    shards = list(refs[:-18])
    lengths = (groups, calls, calls, groups, groups, groups)
    query_refs, key_refs, value_refs, mixed_refs, top_refs, bottom_refs = (
        [shards.pop(0) for _ in range(length)] for length in lengths
    )
    (
        scale_two_ref, shift_two_ref, small_two_ref, own_embed_ref, time_ref, bias_ref, gain_ref, shift_ref, weight_ref,
        first_grad_ref, time_kept_ref, time_sent_ref, weight_kept_ref, weight_sent_ref,
        weight_sum, time_sum, small_sum, out_sum,
    ) = refs[-18:]
    step = pl.program_id(0)
    width = gain_ref.shape[1]
    key_grad = sum(ref[...] for ref in key_refs)
    key_grad = turned(key_grad, cosine_ref[...], -sine_ref[...]).astype(BF16)

    def this(refs):
        values = refs[0][...]
        for at in range(1, len(refs)):
            values = jnp.where(step == at, refs[at][...], values)
        return values

    incoming = jnp.concatenate([this(top_refs), this(bottom_refs)], axis=0)
    out_part = product(this(mixed_refs), incoming, LEAD)
    grads = (this(query_refs), key_grad, sum(ref[...] for ref in value_refs).astype(BF16))
    first_grad = sum(product(grad, weight_ref[at], TRAIL) for at, grad in enumerate(grads))
    first_half = first_grad.astype(BF16)
    first_grad_ref[...] = first_half
    first = first_ref[...]
    weight_parts = [product(first, grad, LEAD) for grad in grads]
    rows = tokens_ref[...]
    embed = rows[:, width:]
    factor = 1.0 + product(embed, time_ref[...]) + bias_ref[...]
    normed, _ = norm_parts(rows[:, :width].astype(F32))
    base = normed * gain_ref[...] + shift_ref[...]
    scale_grad = first_grad * base
    weighted = first_grad * factor
    both = jnp.concatenate([scale_grad.astype(BF16), first_half], axis=1)
    time_part = product(embed, both, LEAD)
    small = jnp.concatenate(
        [
            jnp.sum(each, axis=0, keepdims=True)
            for each in (weighted * normed, weighted, scale_grad, first_grad)
        ],
        axis=0,
    )

    @pl.when(step == 0)
    def _():
        for at, part in enumerate(weight_parts):
            weight_sum[at] = part
        time_sum[...] = time_part
        out_sum[...] = out_part
        small_sum[:4] = small
        small_sum[4:] = small_two_ref[...]

    @pl.when(step > 0)
    def _():
        for at, part in enumerate(weight_parts):
            weight_sum[at] += part
        time_sum[...] += time_part
        out_sum[...] += out_part
        small_sum[:4] += small

    @pl.when(step == pl.num_programs(0) - 1)
    def _():
        one = place_ref[0] == 1
        half = time_kept_ref.shape[0]

        def put(kept_ref, sent_ref, at, values):
            values = values.astype(BF16)
            columns = slice(at, at + values.shape[1])
            kept_ref[:, columns] = jnp.where(one, values[half:], values[:half])
            sent_ref[:, columns] = jnp.where(one, values[:half], values[half:])

        put(time_kept_ref, time_sent_ref, 0, time_sum[...])
        own_embed = own_embed_ref[...]
        put(time_kept_ref, time_sent_ref, 2 * width, product(own_embed, scale_two_ref[...], LEAD))
        put(time_kept_ref, time_sent_ref, 3 * width, product(own_embed, shift_two_ref[...], LEAD))
        smalls = small_sum[...]
        smalls = jnp.concatenate(
            [smalls[:, at : at + 128] for at in range(0, width, 128)]
            + [jnp.zeros((2 * half - width // 16, 128), F32)],
            axis=0,
        )
        put(time_kept_ref, time_sent_ref, 4 * width, smalls)
        part = weight_sum.shape[2]
        for at in range(3):
            for row in range(0, width, 2 * half):
                column = (at * width + row) // (2 * half) * part
                put(weight_kept_ref, weight_sent_ref, column, weight_sum[at, row : row + 2 * half])
        put(weight_kept_ref, weight_sent_ref, 3 * part * width // (2 * half), out_sum[...])


def leave(
    core, queries, keys, values, mixed, halves, tables, tokens_all, first_all, second_grads, own_embed, time_flat, bias, gain, shift, weight, rows
):
    seq, both = tokens_all.shape
    part = weight.shape[2]
    width = gain.shape[1]
    embed = both - width
    half = embed // 2
    time_lanes = 4 * width + 128
    weight_lanes = 3 * part * width // embed + width

    def shard(lanes):
        return pl.BlockSpec((rows, lanes), lambda i, _: (i, 0))

    inputs = (*tables, tokens_all, first_all)
    extras = (*second_grads, own_embed)
    constants = (time_flat, bias, gain, shift, weight)
    groups = seq // rows
    picked = [pl.BlockSpec((rows, part), lambda i, _, at=at: (at, 0)) for _, at in queries]
    shards = [each for each, _ in queries] + [*keys, *values, *mixed]
    shards += [pair[0] for pair in halves] + [pair[1] for pair in halves]
    shard_specs = picked + [shard(part)] * (len(keys) + len(values)) + [whole(rows, part)] * groups
    shard_specs += [whole(rows // 2, width)] * (2 * groups)
    return pl.pallas_call(
        functools.partial(exit_kernel, groups=groups, calls=len(keys)),
        grid_spec=pltpu.PrefetchScalarGridSpec(
            num_scalar_prefetch=1,
            grid=(seq // rows,),
            in_specs=[shard(each.shape[1]) for each in inputs]
            + shard_specs
            + [whole(*each.shape) for each in extras]
            + [block_of((embed, width), 0, 0), block_of((1, width), 0, 0)]
            + [whole(*each.shape) for each in (gain, shift, weight)],
            out_specs=[shard(width)]
            + [whole(half, time_lanes)] * 2
            + [whole(half, weight_lanes)] * 2,
            scratch_shapes=[
                pltpu.VMEM((3, width, part), F32),
                pltpu.VMEM((embed, 2 * width), F32),
                pltpu.VMEM((8, width), F32),
                pltpu.VMEM((part, width), F32),
            ],
        ),
        out_shape=[jax.ShapeDtypeStruct((seq, width), BF16)]
        + [jax.ShapeDtypeStruct((half, time_lanes), BF16)] * 2
        + [jax.ShapeDtypeStruct((half, weight_lanes), BF16)] * 2,
        compiler_params=limits(48),
        cost_estimate=pl.CostEstimate(
            flops=seq * width,
            bytes_accessed=seq * width,
            transcendentals=seq,
        ),
    )(core, *kept_out(*inputs, *shards, *extras, *constants))


def middle_kernel(
    tokens_ref, top_ref, bottom_ref, embed_ref, time_ref, bias_ref, gain_ref, shift_ref, residual_ref, second_ref
):
    width = gain_ref.shape[1]
    attended = jnp.concatenate([top_ref[...], bottom_ref[...]], axis=0)
    residual = tokens_ref[...].astype(F32) + attended
    residual_ref[...] = residual
    mod = product(embed_ref[...], time_ref[...]) + bias_ref[...]
    normed, _ = norm_parts(residual)
    base = normed * gain_ref[...] + shift_ref[...]
    second_ref[...] = (base * (1.0 + mod[:, :width]) + mod[:, width:]).astype(BF16)


def middle(tokens, top, bottom, embed, time_flat, bias, gain, shift):
    rows, width = tokens.shape
    inputs = (tokens, top, bottom, embed, time_flat, bias, gain, shift)
    shard = whole(rows, width)
    return pl.pallas_call(
        middle_kernel,
        grid=(1,),
        in_specs=[whole(*each.shape) for each in inputs[:4]]
        + [block_of((embed.shape[1], 2 * width), 0, 1), block_of((1, 2 * width), 0, 1)]
        + [whole(*each.shape) for each in inputs[6:]],
        out_specs=[shard, shard],
        out_shape=[pltpu.HBM((rows, width), F32), pltpu.HBM((rows, width), BF16)],
        compiler_params=limits(16),
    )(*kept_out(tokens), top, bottom, *kept_out(*inputs[3:]))


def middle_back_kernel(
    part_ref, other_ref, cotangent_ref, residual_ref, embed_ref, time_ref, bias_ref, gain_ref, shift_ref,
    residual_grad_ref, half_ref, scale_grad_ref, shift_grad_ref, small_ref,
):
    grads = part_ref[...] + other_ref[...]
    factor = 1.0 + product(embed_ref[...], time_ref[...]) + bias_ref[...]
    normed, scale = norm_parts(residual_ref[...])
    gain = gain_ref[...]
    base = normed * gain + shift_ref[...]
    weighted = grads * factor
    inner = weighted * gain
    back = scale * (
        inner
        - jnp.mean(inner, axis=-1, keepdims=True)
        - normed * jnp.mean(inner * normed, axis=-1, keepdims=True)
    )
    residual_grad = cotangent_ref[...].astype(F32) + back
    residual_grad_ref[...] = residual_grad
    half_ref[...] = residual_grad.astype(BF16)
    scale_grad = grads * base
    scale_grad_ref[...] = scale_grad.astype(BF16)
    shift_grad_ref[...] = grads.astype(BF16)
    small_ref[...] = jnp.concatenate(
        [
            jnp.sum(each, axis=0, keepdims=True)
            for each in (weighted * normed, weighted, scale_grad, grads)
        ],
        axis=0,
    )


def middle_back(part, other, cotangent, residual, embed, time_flat, bias, gain, shift):
    rows, width = cotangent.shape
    shard = whole(rows, width)
    inputs = (part, other, cotangent, residual, embed, time_flat, bias, gain, shift)
    return pl.pallas_call(
        middle_back_kernel,
        grid=(1,),
        in_specs=[whole(*each.shape) for each in inputs[:5]]
        + [block_of((embed.shape[1], width), 0, 2), block_of((1, width), 0, 2)]
        + [whole(*each.shape) for each in inputs[7:]],
        out_specs=[shard] * 4 + [whole(4, width)],
        out_shape=[
            pltpu.HBM((rows, width), F32),
            jax.ShapeDtypeStruct((rows, width), BF16),
            pltpu.HBM((rows, width), BF16),
            pltpu.HBM((rows, width), BF16),
            pltpu.HBM((4, width), F32),
        ],
        compiler_params=limits(20),
    )(part, other, *kept_out(*inputs[2:]))


def forward_kernel(
    place_ref, rows_ref, rows_other_ref, grads_ref, grads_other_ref, up_own_ref, down_own_ref, up_ref, down_ref,
    branch_ref, branch_other_ref, second_ref, second_other_ref, *grad_refs, planes,
):
    step = pl.program_id(0)
    mine = step == 0
    rows = jnp.concatenate([rows_ref[...], rows_other_ref[...]], axis=0)
    grads = jnp.concatenate([grads_ref[...], grads_other_ref[...]], axis=0)
    count = branch_ref.shape[0]
    up = jnp.where(mine, up_own_ref[...], up_ref[...]).reshape(rows.shape[1], up_ref.shape[2])
    packed = jnp.where(mine, down_own_ref[...], down_ref[...])
    half = packed.shape[1] // 2
    down = jnp.concatenate(
        [packed[:, :half].reshape(-1, packed.shape[2]), packed[:, half:].reshape(-1, packed.shape[2])],
        axis=1,
    )
    hidden = product(rows, up)
    active_grad = product(grads, down, TRAIL)
    tail = 0.5 * (1.0 + lax.erf(hidden * math.sqrt(0.5)))
    slope = tail + hidden * jnp.exp(hidden * hidden * -0.5) * (1.0 / math.sqrt(2.0 * math.pi))
    active = (hidden * tail).astype(BF16)
    hidden_grad = (active_grad * slope).astype(BF16)
    branch = product(active, down)
    second = product(hidden_grad, up, TRAIL)

    @pl.when(mine)
    def _():
        branch_ref[...] = branch[:count]
        branch_other_ref[...] = branch[count:]
        second_ref[...] = second[:count]
        second_other_ref[...] = second[count:]

    @pl.when(step > 0)
    def _():
        branch_ref[...] += branch[:count]
        branch_other_ref[...] += branch[count:]
        second_ref[...] += second[:count]
        second_other_ref[...] += second[count:]

    bits = planes.bit_length() - 1
    down_grad = product(active, grads, LEAD)
    up_grad = product(rows, hidden_grad, LEAD)
    for bit, at, kept_ref, sent_ref in ((0, 0, *grad_refs[:2]), (bits - 1, 1, *grad_refs[2:])):
        one = (place_ref[0] >> bit) & 1 == 1
        for part, grad in enumerate((down_grad, up_grad)):
            middle = grad.shape[1] // 2
            columns = grad[:, at * middle : (at + 1) * middle].astype(BF16)
            low = columns.shape[0] // planes << bit
            split = columns.reshape(-1, 2, low, middle)
            each = columns.shape[0] // planes
            down_rows = kept_ref.shape[2] // 2
            for ref, chosen in (
                (kept_ref, jnp.where(one, split[:, 1], split[:, 0])),
                (sent_ref, jnp.where(one, split[:, 0], split[:, 1])),
            ):
                chosen = chosen.reshape(planes // 2, each, middle)
                if part == 0:
                    ref[:, 0, :down_rows] = chosen
                else:
                    ref[:, 0, down_rows:, :middle] = chosen[:, :down_rows]
                    ref[:, 0, down_rows:, middle:] = chosen[:, down_rows:]


def feed_forward(place, rows, rows_other, grads, grads_other, own_weights, weights, groups):
    tokens, width = rows.shape
    planes, piece_rows, hidden = own_weights.shape
    half = whole(tokens, width)
    block = (planes, piece_rows // 2, hidden)

    def other(i):
        return jnp.maximum(i - 1, 0)

    piece = (planes // 2, 1, 2 * hidden // planes, width // 2)
    grad_spec = pl.BlockSpec(piece, lambda i, at: (0, i, 0, 0))
    grad_shape = pltpu.HBM((piece[0], groups, *piece[2:]), BF16)
    return pl.pallas_call(
        functools.partial(forward_kernel, planes=planes),
        grid_spec=pltpu.PrefetchScalarGridSpec(
            num_scalar_prefetch=1,
            grid=(groups,),
            in_specs=[
                half,
                half,
                half,
                half,
                pl.BlockSpec(block, lambda i, _: (0, 0, 0)),
                pl.BlockSpec(block, lambda i, _: (0, 1, 0)),
                pl.BlockSpec(block, lambda i, _: (other(i), 0, 0)),
                pl.BlockSpec(block, lambda i, _: (other(i), 1, 0)),
            ],
            out_specs=[half] * 4 + [grad_spec] * 4,
        ),
        out_shape=[jax.ShapeDtypeStruct((tokens, width), F32)] * 4 + [grad_shape] * 4,
        compiler_params=limits(48),
        cost_estimate=pl.CostEstimate(
            flops=24 * tokens * width * groups * hidden,
            bytes_accessed=8 * width * groups * hidden,
            transcendentals=4 * tokens * groups * hidden,
        ),
    )(place, *kept_out(rows), rows_other, *kept_out(grads, grads_other, own_weights, own_weights, weights, weights))


def spread_kernel(packed_ref, spread_ref):
    width = spread_ref.shape[2]
    for at in range(spread_ref.shape[1]):
        spread_ref[:, at, :] = packed_ref[:, at * width : (at + 1) * width].astype(F32)


def spread(packed, shape, rows):
    blocks = packed.shape[0] // rows
    columns = shape[1] * shape[2]
    return pl.pallas_call(
        spread_kernel,
        grid=(shape[0] // rows,),
        in_specs=[pl.BlockSpec((rows, columns), lambda i: (i % blocks, i // blocks))],
        out_specs=pl.BlockSpec((rows, shape[1], shape[2]), lambda i: (i, 0, 0)),
        out_shape=jax.ShapeDtypeStruct(shape, F32),
        compiler_params=limits(16),
    )(packed)


def unfold_kernel(packed_ref, out_ref):
    rows, width = packed_ref.shape[0], out_ref.shape[2]
    for at in range(packed_ref.shape[1] // width):
        out_ref[0, at * rows : (at + 1) * rows] = packed_ref[:, at * width : (at + 1) * width].astype(F32)


def unfold(packed, shape):
    rows = packed.shape[0]
    blocks = shape[1] // rows
    return pl.pallas_call(
        unfold_kernel,
        grid=(shape[0],),
        in_specs=[pl.BlockSpec((rows, blocks * shape[2]), lambda i: (0, i))],
        out_specs=pl.BlockSpec((1, *shape[1:]), lambda i: (i, 0, 0)),
        out_shape=jax.ShapeDtypeStruct(shape, F32),
        compiler_params=limits(16),
    )(packed)


def unpack_kernel(sums_ref, down_ref, up_ref):
    rows = sums_ref.shape[1] // 2
    half = up_ref.shape[1]
    quarter = half // 2
    for which in range(sums_ref.shape[0]):
        down_ref[which * rows : (which + 1) * rows] = sums_ref[which, :rows].astype(F32)
        upper = 2 * which * rows
        for at in range(2):
            columns = slice(at * quarter, (at + 1) * quarter)
            folded = sums_ref[which, rows:, at * half : (at + 1) * half].astype(F32)
            up_ref[upper : upper + rows, columns] = folded[:, :quarter]
            up_ref[upper + rows : upper + 2 * rows, columns] = folded[:, quarter:]


def unpack(sums, planes):
    pieces, both, width = sums.shape
    rows = both // 2
    half = width // 2
    return pl.pallas_call(
        unpack_kernel,
        grid=(pieces // 2,),
        in_specs=[pl.BlockSpec((2, both, width), lambda i: (i, 0, 0))],
        out_specs=[
            pl.BlockSpec((2 * rows, width), lambda i: (i, 0)),
            pl.BlockSpec((4 * rows, half), lambda i: (i % (planes // 2), i // (planes // 2))),
        ],
        out_shape=[
            jax.ShapeDtypeStruct((pieces * rows, width), F32),
            jax.ShapeDtypeStruct((planes * 2 * rows, half * pieces // planes), F32),
        ],
        compiler_params=limits(16),
    )(sums)


def swap(values, axis_name, bit):
    size = lax.axis_size(axis_name)
    return lax.ppermute(values, axis_name, [(at, at ^ (1 << bit)) for at in range(size)])


def bit_of(axis_name, bit):
    return (lax.axis_index(axis_name) >> bit) & 1


def after(values, *others):
    return lax.optimization_barrier((values, others))[0]


def exchange(values, axis_name, bit, dim):
    own = bit_of(axis_name, bit)
    kept = lax.dynamic_index_in_dim(values, own, dim, keepdims=False)
    sent = lax.dynamic_index_in_dim(values, 1 - own, dim, keepdims=False)
    return (kept, swap(sent, axis_name, bit))


def total(kept, got):
    return (kept.astype(F32) + got.astype(F32)).astype(BF16)


def double(values, axis_name, bit, dim):
    own = bit_of(axis_name, bit) == 0
    got = swap(values, axis_name, bit)
    return jnp.stack([jnp.where(own, values, got), jnp.where(own, got, values)], axis=dim)


class PlaneScatter:
    def __init__(self, arrays, orders, dim):
        bits = len(orders[0])
        self.dim = dim
        self.arrays = [
            each.reshape(each.shape[:dim] + (2,) * bits + each.shape[dim + 1 :]) for each in arrays
        ]
        self.orders = [list(order) for order in orders]
        self.left = [list(range(bits - 1, -1, -1)) for _ in orders]

    @classmethod
    def started(cls, kept, sent, orders, dim):
        self = cls.__new__(cls)
        bits = len(orders[0])
        self.dim = dim
        self.orders = [list(order[1:]) for order in orders]
        self.left = [[bit for bit in range(bits - 1, -1, -1) if bit != order[0]] for order in orders]
        self.kept = [
            each.reshape(each.shape[:dim] + (2,) * (bits - 1) + each.shape[dim + 1 :]) for each in kept
        ]
        self.got = [
            swap(each, "plane", order[0]).reshape(like.shape)
            for each, like, order in zip(sent, self.kept, orders)
        ]
        return self

    def send(self):
        self.kept, self.got = [], []
        for values, order, left in zip(self.arrays, self.orders, self.left):
            bit = order.pop(0)
            kept, got = exchange(values, "plane", bit, self.dim + left.index(bit))
            left.remove(bit)
            self.kept.append(kept)
            self.got.append(got)

    def meet(self, *others):
        self.got, others = lax.optimization_barrier((self.got, others))
        return others

    def add(self):
        self.arrays = [total(kept, got) for kept, got in zip(self.kept, self.got)]

    def finish(self):
        while self.orders[0]:
            self.send()
            self.add()
        return self.arrays


def plane_gather(values, order, dim):
    bits = len(order)
    left = []
    for bit in reversed(order):
        left = sorted(left + [bit], reverse=True)
        values = double(values, "plane", bit, dim + left.index(bit))
    shape = values.shape
    return values.reshape(shape[:dim] + (1 << bits,) + shape[dim + bits :])


def ring_gather(shard, meanwhile=None):
    size = lax.axis_size("tensor")
    half = shard.shape[0] // 2
    right, left = [shard[:half]], [shard[half:]]
    for step in range(1, size):
        others = () if meanwhile is None else meanwhile(step, right, left)
        right.append(lax.ppermute(right[-1], "tensor", [(at, (at + 1) % size) for at in range(size)]))
        left.append(lax.ppermute(left[-1], "tensor", [(at, (at - 1) % size) for at in range(size)]))
        right[-1], left[-1], others = lax.optimization_barrier((right[-1], left[-1], others))
        if meanwhile is not None:
            meanwhile(-step, others, None)
    return [(right[(size - at) % size], left[at]) for at in range(size)]


def ring_scatter(chunks, *gates):
    size = len(chunks)
    half = chunks[0].shape[0] // 2
    right = chunks[size - 1][:half]
    left = chunks[1 % size][half:]
    for step in range(1, size):
        right = lax.ppermute(right, "tensor", [(at, (at + 1) % size) for at in range(size)])
        left = lax.ppermute(left, "tensor", [(at, (at - 1) % size) for at in range(size)])
        right, left = after((right, left), *(gates[step - 1] if step <= len(gates) else ()))
        right = right.astype(F32) + chunks[size - 1 - step][:half].astype(F32)
        left = left.astype(F32) + chunks[(step + 1) % size][half:].astype(F32)
        if step < size - 1:
            right, left = right.astype(BF16), left.astype(BF16)
    return (right, left)


def own_first(values, dim):
    size = lax.axis_size("tensor")
    stretch = values.shape[dim] // size
    doubled = jnp.concatenate([values, values], axis=dim)
    return lax.dynamic_slice_in_dim(
        doubled, lax.axis_index("tensor") * stretch, values.shape[dim], dim
    )


def tensor_sum(values):
    size = lax.axis_size("tensor")
    for bit in range(size.bit_length() - 1):
        values = (values.astype(F32) + swap(values, "tensor", bit).astype(F32)).astype(BF16)
    return values


def local(
    tokens,
    time_embed,
    segment_ids,
    positions,
    first_gain,
    first_bias,
    second_gain,
    second_bias,
    time_weight,
    time_bias,
    qkv_weight,
    out_weight,
    up_weight,
    down_weight,
    cotangent,
):
    local_rows, width = tokens.shape
    embed_width = time_embed.shape[1]
    local_width = qkv_weight.shape[2]
    hidden_local = up_weight.shape[1]
    half_hidden = hidden_local // 2
    planes = lax.axis_size("plane")
    groups = lax.axis_size("tensor")
    plane_at = lax.axis_index("plane")
    core_at = lax.axis_index("core")
    place = plane_at.astype(jnp.int32).reshape(1)
    arrival = sorted(range(groups), key=lambda at: max(at, groups - at) if at else 0)
    rising = list(range(planes.bit_length() - 1))
    falling = rising[::-1]

    up_rows = width // planes
    up_piece = lax.dynamic_slice(
        up_weight, (plane_at * up_rows, core_at * half_hidden), (up_rows, half_hidden)
    )
    down_rows = half_hidden // planes
    down_piece = lax.dynamic_slice(
        down_weight, (core_at * half_hidden + plane_at * down_rows, 0), (down_rows, width)
    )
    piece = jnp.concatenate([up_piece, down_piece[:, :half_hidden], down_piece[:, half_hidden:]], axis=0)
    chosen = lax.all_gather(piece, "tensor", axis=0)
    up_half = lax.dynamic_slice_in_dim(up_weight, core_at * half_hidden, half_hidden, 1)
    down_half = lax.dynamic_slice_in_dim(down_weight, core_at * half_hidden, half_hidden, 0)
    down_half = down_half.reshape(planes, down_rows, width)
    own_pieces = jnp.concatenate(
        [
            up_half.reshape(planes, up_rows, half_hidden),
            down_half[..., :half_hidden],
            down_half[..., half_hidden:],
        ],
        axis=1,
    )

    held = {
        "time": time_weight.reshape(embed_width, 4 * width),
        "tables": rotary_tables(own_first(positions, 1).reshape(-1), 2 * HEAD),
        "pieces": own_pieces,
        "cotangent": swap(cotangent, "core", 0),
    }
    bias_flat = time_bias.reshape(1, 4 * width)
    first_gain, first_bias = first_gain.reshape(1, width), first_bias.reshape(1, width)
    second_gain, second_bias = second_gain.reshape(1, width), second_bias.reshape(1, width)
    qkv_planes = jnp.transpose(qkv_weight, (1, 0, 2))
    segments = own_first(segment_ids, 1)
    columns = segments.reshape(-1, 1)

    def enter(places, halves, row):
        return entry(
            halves, held["tables"], held["time"], bias_flat, first_gain, first_bias, qkv_planes, places, groups, row
        )

    def meanwhile(step, right, left):
        if step == 1:
            return held
        if step == -1:
            held.update(right)
        elif step == 2:
            return enter([0], (right[0], left[0]), ())
        elif step > 2 and 2 * (step - 1) == groups:
            return enter([step - 1], (right[step - 1], left[step - 1]), held["row"])
        elif step > 0:
            return held["row"]
        else:
            held["row"] = right
        return None

    gathered = ring_gather(jnp.concatenate([tokens, time_embed], axis=1), meanwhile)
    chosen = after(chosen, gathered[arrival[-1]])
    tensor_at = lax.axis_index("tensor")
    chosen = jnp.stack(
        [
            lax.dynamic_index_in_dim(chosen, (tensor_at + at) % groups, 0, keepdims=False)
            for at in range(1, groups)
        ]
    )
    pieces = lax.all_gather(chosen, "plane", axis=1)
    pieces = pieces.reshape((groups - 1) * planes, up_rows * 2, half_hidden)
    row = held["row"]
    for first in range(2, len(arrival), 2):
        places = arrival[first : first + 2]
        row = enter(places, [half for at in places for half in gathered[at]], row)
    tables, time_flat = held["tables"], held["time"]
    tokens_all, first_all, queries, keys, values = row
    keys, chosen = lax.optimization_barrier((keys, chosen))
    mixed, logsums, parts = {}, {}, {}
    for at in list(range(groups - 1, -1, -1)):
        mixed[at], logsums[at], parts[at] = attend(
            queries, keys, values, segments, columns, out_weight, at, local_rows
        )
    attended = ring_scatter([parts[at] for at in range(groups)])

    residual, second_normed = middle(
        tokens, *attended, time_embed, time_flat, bias_flat, second_gain, second_bias
    )
    branch_own, branch_other, second_own, second_other, *grad_parts = feed_forward(
        place,
        second_normed,
        swap(second_normed, "core", 0),
        cotangent,
        held["cotangent"],
        held["pieces"],
        pieces,
        groups,
    )
    second_other = swap(second_other, "core", 0)

    weight_sums = PlaneScatter.started(
        grad_parts[::2], grad_parts[1::2], [rising, falling], 0
    )
    branch = branch_own + swap(branch_other, "core", 0)
    result = (residual + branch).astype(BF16)

    residual_grad, attended_own, scale_two_grad, shift_two_grad, small_two = middle_back(
        second_own,
        second_other,
        cotangent,
        residual,
        time_embed,
        time_flat,
        bias_flat,
        second_gain,
        second_bias,
    )
    def turn(places, halves):
        return attend_back(
            halves,
            queries,
            keys,
            values,
            [logsums[at] for at in places],
            segments,
            columns,
            out_weight,
            tables,
            places,
        )

    back = {}

    def meanwhile_back(step, right, left):
        if step == 2:
            return turn([0], (right[0], left[0]))
        if step == -2:
            back[(0,)] = right
        elif step == groups - 1:
            done = ()
            if 2 * (step - 1) == groups:
                done = turn([step - 1], (right[step - 1], left[step - 1]))
            return (done, weight_sums.got)
        elif step == 1 - groups:
            done, weight_sums.got = right
            if done:
                back[(groups // 2,)] = done
        return ()

    attended_halves = ring_gather(attended_own, meanwhile_back)
    weight_sums.add()
    attended_halves[arrival[2]], weight_sums.arrays = lax.optimization_barrier(
        (attended_halves[arrival[2]], weight_sums.arrays)
    )
    if weight_sums.orders[0]:
        weight_sums.send()
    rest = [at for at in arrival if (at,) not in back]
    for first in range(0, len(rest), 2):
        places = tuple(rest[first : first + 2])
        back[places] = turn(places, [half for at in places for half in attended_halves[at]])
    query_shards = {at: (parts[0], which) for places, parts in back.items() for which, at in enumerate(places)}
    received = [
        lax.ppermute(parts[hop], "tensor", [(at, (at + hop) % groups) for at in range(groups)])
        for hop in range(1, groups)
    ]
    left = leave(
        core_at.astype(jnp.int32).reshape(1),
        [query_shards[at] for at in range(groups)],
        [parts[1] for parts in back.values()],
        [parts[2] for parts in back.values()],
        [mixed[at] for at in range(groups)],
        attended_halves,
        tables,
        tokens_all,
        first_all,
        (scale_two_grad, shift_two_grad, small_two),
        time_embed,
        time_flat,
        bias_flat,
        first_gain,
        first_bias,
        qkv_planes,
        local_rows,
    )
    (left,) = weight_sums.meet(left)
    weight_sums.add()
    by_link = weight_sums.finish()
    parts = [jnp.concatenate([each[at] for each in by_link], axis=-1) for at in range(groups)]
    received = [
        lax.ppermute(parts[hop], "tensor", [(at, (at + hop) % groups) for at in range(groups)])
        for hop in range(1, groups)
    ]
    first_half, time_kept, time_sent, weight_kept, weight_sent = left

    time_got, weight_got = swap(time_sent, "core", 0), swap(weight_sent, "core", 0)

    def by_plane(pack):
        return pack.reshape(planes, embed_width // (2 * planes), -1)

    pack_sums = PlaneScatter(
        [by_plane(total(time_kept, time_got)), by_plane(total(weight_kept, weight_got))], [rising, falling], 0
    )
    for _ in rising:
        pack_sums.send()
        if len(pack_sums.orders[0]) == 0:
            (received,) = pack_sums.meet(received)
        pack_sums.add()
    time_own, weight_own = pack_sums.arrays
    sums = sum(each.astype(F32) for each in [parts[0], *received]).astype(BF16)
    sums = lax.all_gather(sums, ("core", "plane"), axis=0)
    first_half, time_own = lax.optimization_barrier((first_half, time_own))
    time_sum = tensor_sum(time_own)
    time_halves = plane_gather(time_sum, rising, 0)
    weight_halves = plane_gather(weight_own, falling, 0)
    time_pack = double(time_halves.reshape(embed_width // 2, -1), "core", 0, 0)
    weight_pack = double(weight_halves.reshape(embed_width // 2, -1), "core", 0, 0)
    time_pack = time_pack.reshape(embed_width, -1)
    weight_pack = weight_pack.reshape(embed_width, -1)
    (sums,) = kept_out(sums)
    down_summed, up_summed = unpack(sums, planes)
    first_grad = ring_scatter(
        [first_half[at * local_rows : (at + 1) * local_rows] for at in range(groups)],
        (time_sum,),
        (time_halves, weight_halves),
        (time_pack, weight_pack, down_summed),
    )
    time_weight_grad = spread(time_pack, (embed_width, 4, width), min(64, embed_width))
    small = time_pack[: width // 16, 4 * width :].astype(F32)
    small = jnp.transpose(small.reshape(width // 128, 8, 128), (1, 0, 2)).reshape(8, width)
    qkv_lanes = 3 * local_width * width // embed_width
    qkv_summed = jnp.transpose(
        unfold(weight_pack, (3, width, local_width)), (1, 0, 2)
    )
    out_summed = weight_pack[:, qkv_lanes:].astype(F32)

    own_normed, own_scale = norm_parts(tokens.astype(F32))
    mod_own = product(time_embed, time_flat[:, :width]) + bias_flat[:, :width]
    first_grad = jnp.concatenate(first_grad, axis=0)
    input_grad = residual_grad + norm_input_back(first_grad, own_normed, own_scale, first_gain, mod_own)
    return (
        result,
        input_grad,
        small[0],
        small[1],
        small[4],
        small[5],
        time_weight_grad,
        jnp.concatenate([small[2:4], small[6:]], axis=0),
        qkv_summed,
        out_summed,
        up_summed,
        down_summed,
    )


def solution(mesh):
    whole, tensor = mesh.devices.shape
    finer = Mesh(mesh.devices.reshape(whole // 2, 2, tensor), ("plane", "core", "tensor"))
    rows = P(("plane", "core", "tensor"), None)
    group = P(("plane", "core"), None)
    return jax.shard_map(
        local,
        mesh=finer,
        in_specs=(
            rows,
            rows,
            group,
            group,
            P(),
            P(),
            P(),
            P(),
            P(),
            P(),
            P(None, None, "tensor"),
            P("tensor", None),
            P(None, "tensor"),
            P("tensor", None),
            rows,
        ),
        out_specs=(
            rows,
            rows,
            P(),
            P(),
            P(),
            P(),
            P(),
            P(),
            P(None, None, "tensor"),
            P("tensor", None),
            P(None, "tensor"),
            P("tensor", None),
        ),
        check_vma=False,
    )
```

```python
import functools
import math

import jax
import jax.numpy as jnp
from jax import lax
from jax.experimental import pallas as pl
from jax.experimental.pallas import tpu as pltpu
from jax.sharding import Mesh
from jax.sharding import PartitionSpec as P

HEAD = 64
F32 = jnp.float32
BF16 = jnp.bfloat16
LEAD = (((0,), (0,)), ((), ()))
TRAIL = (((1,), (1,)), ((), ()))


def product(left, right, dims=(((1,), (0,)), ((), ()))):
    return lax.dot_general(left, right, dims, preferred_element_type=F32)


def norm_parts(values):
    centre = values - jnp.mean(values, axis=-1, keepdims=True)
    spread = jnp.mean(centre * centre, axis=-1, keepdims=True)
    scale = lax.rsqrt(spread + 1e-05)
    return (centre * scale, scale)


def norm_input_back(grads, normed, scale, gain, mod_scale):
    inner = grads * (1.0 + mod_scale) * gain
    return scale * (
        inner
        - jnp.mean(inner, axis=-1, keepdims=True)
        - normed * jnp.mean(inner * normed, axis=-1, keepdims=True)
    )


def rotary_tables(places, lanes):
    half_size = HEAD // 2
    lane = jnp.arange(lanes)
    frequency = jnp.exp((lane % half_size).astype(F32) * (-math.log(10000.0) / half_size))
    angles = places.astype(F32)[:, None] * frequency[None, :]
    sign = jnp.where(lane % HEAD < half_size, -1.0, 1.0)
    return (jnp.cos(angles), jnp.sin(angles) * sign[None, :])


def kept_out(*arrays):
    return tuple(pltpu.with_memory_space_constraint(each, pltpu.HBM) for each in arrays)


def block_of(shape, *place):
    return pl.BlockSpec(shape, lambda *_: place)


def whole(*shape):
    return pl.BlockSpec(shape, lambda *_: (0,) * len(shape))


def limits(megabytes):
    return pltpu.CompilerParams(vmem_limit_bytes=megabytes << 20)


def partner(values):
    lanes = values.shape[1]
    lane = lax.broadcasted_iota(jnp.int32, values.shape, 1)
    above = pltpu.roll(values, lanes - HEAD // 2, 1)
    below = pltpu.roll(values, HEAD // 2, 1)
    return jnp.where(lane % HEAD < HEAD // 2, above, below)


def widened(table, lanes):
    return jnp.concatenate([table] * (lanes // table.shape[1]), axis=1)


def turned(values, cosine, sine):
    return values * widened(cosine, values.shape[1]) + partner(values) * widened(sine, values.shape[1])


def entry_kernel(
    *refs, count
):
    halves, refs = refs[: 2 * count], refs[2 * count :]
    cosine_ref, sine_ref, time_ref, bias_ref, gain_ref, shift_ref, weight_ref = refs[:7]
    tokens_ref, first_ref, query_ref, key_ref, value_ref = refs[-5:]
    rows = jnp.concatenate([halves[0][...], halves[1][...]], axis=0)
    for at in range(1, count):
        other = jnp.concatenate([halves[2 * at][...], halves[2 * at + 1][...]], axis=0)
        rows = jnp.where(pl.program_id(0) == at, other, rows)
    tokens_ref[...] = rows
    width = gain_ref.shape[1]
    mod = product(rows[:, width:], time_ref[...]) + bias_ref[...]
    normed, _ = norm_parts(rows[:, :width].astype(F32))
    base = normed * gain_ref[...] + shift_ref[...]
    first = (base * (1.0 + mod[:, :width]) + mod[:, width:]).astype(BF16)
    first_ref[...] = first
    cosine, sine = cosine_ref[...], sine_ref[...]
    query_ref[...] = turned(product(first, weight_ref[0]), cosine, sine).astype(BF16)
    key_ref[...] = turned(product(first, weight_ref[1]), cosine, sine).astype(BF16)
    value_ref[...] = product(first, weight_ref[2]).astype(BF16)


def entry(halves, tables, time_flat, bias, gain, shift, weight, places, groups, before):
    half, both = halves[0].shape
    count = len(places)
    apart = places[-1] - places[0]
    rows = 2 * half
    width = gain.shape[1]
    part = weight.shape[2]
    lanes = tables[0].shape[1]
    widths = (both, width, part, part, part)
    table = pl.BlockSpec((rows, lanes), lambda i: (places[0] + i * apart, 0))
    inputs = (*halves, *kept_out(*tables, time_flat, bias, gain, shift, weight))
    return pl.pallas_call(
        functools.partial(entry_kernel, count=count),
        grid=(count,),
        in_specs=[whole(half, both)] * (2 * count)
        + [table, table]
        + [block_of((both - width, 2 * width), 0, 0), block_of((1, 2 * width), 0, 0)]
        + [whole(*each.shape) for each in (gain, shift, weight)]
        + [pl.BlockSpec(memory_space=pl.ANY)] * len(before),
        out_specs=[pl.BlockSpec((rows, each), lambda i: (places[0] + i * apart, 0)) for each in widths],
        out_shape=[pltpu.HBM((rows * groups, each), BF16) for each in widths],
        input_output_aliases={len(inputs) + at: at for at in range(len(before))},
        compiler_params=limits(16),
        cost_estimate=pl.CostEstimate(
            flops=2 * rows * width * 4 * part + 4 * rows * width * (both - width),
            bytes_accessed=8 * rows * width + 6 * width * part,
            transcendentals=rows,
        ),
    )(*inputs, *kept_out(*before))


def head_lanes(values, head):
    pair = values[:, head // 2 * 2 * HEAD : (head // 2 + 1) * 2 * HEAD]
    lane = lax.broadcasted_iota(jnp.int32, pair.shape, 1)
    return jnp.where(lane // HEAD == head % 2, pair, jnp.zeros_like(pair))


def pair_lanes(values, head):
    return values[:, head // 2 * 2 * HEAD : (head // 2 + 1) * 2 * HEAD]


def attend_kernel(query_ref, key_ref, value_ref, own_ref, all_ref, out_ref, mixed_ref, logsum_ref, part_ref):
    queries, keys, values = query_ref[...], key_ref[...], value_ref[...]
    allowed = all_ref[...] == own_ref[...]
    scale = 1.0 / math.sqrt(HEAD)
    pairs = []
    for head in range(queries.shape[1] // HEAD):
        scores = product(pair_lanes(keys, head), head_lanes(queries, head), TRAIL) * scale
        scores = jnp.where(allowed, scores, -1e30)
        peak = jnp.max(scores, axis=0, keepdims=True)
        raised = jnp.exp(scores - peak)
        total = jnp.sum(raised, axis=0, keepdims=True)
        attention = (raised / total).astype(BF16)
        logsum_ref[head : head + 1, :] = peak + jnp.log(total)
        mixed = product(attention, pair_lanes(values, head), LEAD)
        if head % 2 == 0:
            pairs.append(mixed)
        else:
            lane = lax.broadcasted_iota(jnp.int32, mixed.shape, 1)
            pairs[-1] = jnp.where(lane < HEAD, pairs[-1], mixed)
    mixed = jnp.concatenate(pairs, axis=1).astype(BF16)
    mixed_ref[...] = mixed
    part_ref[...] = product(mixed, out_ref[...]).astype(BF16)


def attend(queries, keys, values, own_segments, all_segments, out_weight, place, rows):
    seq, part = keys.shape
    width = out_weight.shape[1]
    heads = part // HEAD
    return pl.pallas_call(
        attend_kernel,
        grid=(1,),
        in_specs=[
            pl.BlockSpec((rows, part), lambda i: (place, 0)),
            whole(seq, part),
            whole(seq, part),
            pl.BlockSpec((1, rows), lambda i: (0, place)),
            whole(seq, 1),
            whole(part, width),
        ],
        out_specs=[whole(rows, part), whole(heads, rows), whole(rows, width)],
        out_shape=[
            pltpu.HBM((rows, part), BF16),
            pltpu.HBM((heads, rows), F32),
            jax.ShapeDtypeStruct((rows, width), BF16),
        ],
        compiler_params=limits(16),
        cost_estimate=pl.CostEstimate(
            flops=4 * rows * seq * part + 2 * rows * part * width,
            bytes_accessed=4 * seq * part + 4 * rows * width,
            transcendentals=rows * seq * heads,
        ),
    )(queries, keys, values, own_segments, all_segments, out_weight)


def attend_back_kernel(
    query_ref, key_ref, value_ref, own_ref, all_ref, out_ref, cosine_ref, sine_ref, *refs, count
):
    halves, logsum_refs, (grad_ref, key_grad_ref, value_grad_ref) = (
        refs[: 2 * count],
        refs[2 * count : 3 * count],
        refs[3 * count :],
    )
    step = pl.program_id(0)
    queries, keys, values = query_ref[...], key_ref[...], value_ref[...]
    incoming = jnp.concatenate([halves[0][...], halves[1][...]], axis=0)
    logsums = logsum_refs[0][...]
    for at in range(1, count):
        other = jnp.concatenate([halves[2 * at][...], halves[2 * at + 1][...]], axis=0)
        incoming = jnp.where(step == at, other, incoming)
        logsums = jnp.where(step == at, logsum_refs[at][...], logsums)
    mixed_grad = product(incoming, out_ref[...], TRAIL).astype(BF16)
    allowed = all_ref[...] == own_ref[...]
    scale = 1.0 / math.sqrt(HEAD)
    query_pairs, key_pairs, value_pairs = [], [], []
    for head in range(queries.shape[1] // HEAD):
        query, grad = head_lanes(queries, head), head_lanes(mixed_grad, head)
        scores = product(pair_lanes(keys, head), query, TRAIL) * scale
        scores = jnp.where(allowed, scores, -1e30)
        probability = jnp.exp(scores - logsums[head : head + 1, :])
        prob_grad = product(pair_lanes(values, head), grad, TRAIL)
        row_dot = jnp.sum(probability * prob_grad, axis=0, keepdims=True)
        score_grad = (probability * (prob_grad - row_dot)).astype(BF16)
        value_part = product(probability.astype(BF16), grad)
        key_part = product(score_grad, query)
        query_part = product(score_grad, head_lanes(keys, head), LEAD)
        if head % 2 == 0:
            query_pairs.append(query_part)
            key_pairs.append(key_part)
            value_pairs.append(value_part)
        else:
            query_pairs[-1] += query_part
            key_pairs[-1] += key_part
            value_pairs[-1] += value_part
    query_grad = jnp.concatenate(query_pairs, axis=1) * scale
    key_grad = jnp.concatenate(key_pairs, axis=1) * scale
    value_grad = jnp.concatenate(value_pairs, axis=1)
    grad_ref[...] = turned(query_grad, cosine_ref[...], -sine_ref[...]).astype(BF16)

    @pl.when(step == 0)
    def _():
        key_grad_ref[...] = key_grad
        value_grad_ref[...] = value_grad

    @pl.when(step > 0)
    def _():
        key_grad_ref[...] += key_grad
        value_grad_ref[...] += value_grad


def attend_back(halves, queries, keys, values, logsums, own_segments, all_segments, out_weight, tables, places):
    seq, part = keys.shape
    heads, rows = logsums[0].shape
    width = out_weight.shape[1]
    count = len(places)
    apart = places[-1] - places[0]
    shard = pl.BlockSpec((rows, part), lambda i: (places[0] + i * apart, 0))
    table = pl.BlockSpec((rows, tables[0].shape[1]), lambda i: (places[0] + i * apart, 0))
    constants = (own_segments, all_segments, out_weight, *tables)
    return pl.pallas_call(
        functools.partial(attend_back_kernel, count=count),
        grid=(count,),
        in_specs=[
            shard,
            whole(seq, part),
            whole(seq, part),
            pl.BlockSpec((1, rows), lambda i: (0, places[0] + i * apart)),
            whole(seq, 1),
            whole(part, width),
            table,
            table,
        ]
        + [whole(rows // 2, width)] * (2 * count)
        + [whole(heads, rows)] * count,
        out_specs=[
            pl.BlockSpec((rows, part), lambda i: (i, 0)),
            whole(seq, part),
            whole(seq, part),
        ],
        out_shape=[
            pltpu.HBM((count * rows, part), BF16),
            pltpu.HBM((seq, part), F32),
            pltpu.HBM((seq, part), F32),
        ],
        compiler_params=limits(32),
        cost_estimate=pl.CostEstimate(
            flops=10 * count * rows * seq * part + 2 * count * rows * part * width,
            bytes_accessed=16 * seq * part,
            transcendentals=count * rows * seq * heads,
        ),
    )(queries, keys, values, *kept_out(*constants), *halves, *kept_out(*logsums))


def exit_kernel(
    place_ref, cosine_ref, sine_ref, tokens_ref, first_ref, *refs, groups, calls
):
    shards = list(refs[:-18])
    lengths = (groups, calls, calls, groups, groups, groups)
    query_refs, key_refs, value_refs, mixed_refs, top_refs, bottom_refs = (
        [shards.pop(0) for _ in range(length)] for length in lengths
    )
    (
        scale_two_ref, shift_two_ref, small_two_ref, own_embed_ref, time_ref, bias_ref, gain_ref, shift_ref, weight_ref,
        first_grad_ref, time_kept_ref, time_sent_ref, weight_kept_ref, weight_sent_ref,
        weight_sum, time_sum, small_sum, out_sum,
    ) = refs[-18:]
    step = pl.program_id(0)
    width = gain_ref.shape[1]
    key_grad = sum(ref[...] for ref in key_refs)
    key_grad = turned(key_grad, cosine_ref[...], -sine_ref[...]).astype(BF16)

    def this(refs):
        values = refs[0][...]
        for at in range(1, len(refs)):
            values = jnp.where(step == at, refs[at][...], values)
        return values

    incoming = jnp.concatenate([this(top_refs), this(bottom_refs)], axis=0)
    out_part = product(this(mixed_refs), incoming, LEAD)
    grads = (this(query_refs), key_grad, sum(ref[...] for ref in value_refs).astype(BF16))
    first_grad = sum(product(grad, weight_ref[at], TRAIL) for at, grad in enumerate(grads))
    first_half = first_grad.astype(BF16)
    first_grad_ref[...] = first_half
    first = first_ref[...]
    weight_parts = [product(first, grad, LEAD) for grad in grads]
    rows = tokens_ref[...]
    embed = rows[:, width:]
    factor = 1.0 + product(embed, time_ref[...]) + bias_ref[...]
    normed, _ = norm_parts(rows[:, :width].astype(F32))
    base = normed * gain_ref[...] + shift_ref[...]
    scale_grad = first_grad * base
    weighted = first_grad * factor
    both = jnp.concatenate([scale_grad.astype(BF16), first_half], axis=1)
    time_part = product(embed, both, LEAD)
    small = jnp.concatenate(
        [
            jnp.sum(each, axis=0, keepdims=True)
            for each in (weighted * normed, weighted, scale_grad, first_grad)
        ],
        axis=0,
    )

    @pl.when(step == 0)
    def _():
        for at, part in enumerate(weight_parts):
            weight_sum[at] = part
        time_sum[...] = time_part
        out_sum[...] = out_part
        small_sum[:4] = small
        small_sum[4:] = small_two_ref[...]

    @pl.when(step > 0)
    def _():
        for at, part in enumerate(weight_parts):
            weight_sum[at] += part
        time_sum[...] += time_part
        out_sum[...] += out_part
        small_sum[:4] += small

    @pl.when(step == pl.num_programs(0) - 1)
    def _():
        one = place_ref[0] == 1
        half = time_kept_ref.shape[0]

        def put(kept_ref, sent_ref, at, values):
            values = values.astype(BF16)
            columns = slice(at, at + values.shape[1])
            kept_ref[:, columns] = jnp.where(one, values[half:], values[:half])
            sent_ref[:, columns] = jnp.where(one, values[:half], values[half:])

        put(time_kept_ref, time_sent_ref, 0, time_sum[...])
        own_embed = own_embed_ref[...]
        put(time_kept_ref, time_sent_ref, 2 * width, product(own_embed, scale_two_ref[...], LEAD))
        put(time_kept_ref, time_sent_ref, 3 * width, product(own_embed, shift_two_ref[...], LEAD))
        smalls = small_sum[...]
        smalls = jnp.concatenate(
            [smalls[:, at : at + 128] for at in range(0, width, 128)]
            + [jnp.zeros((2 * half - width // 16, 128), F32)],
            axis=0,
        )
        put(time_kept_ref, time_sent_ref, 4 * width, smalls)
        part = weight_sum.shape[2]
        for at in range(3):
            for row in range(0, width, 2 * half):
                column = (at * width + row) // (2 * half) * part
                put(weight_kept_ref, weight_sent_ref, column, weight_sum[at, row : row + 2 * half])
        put(weight_kept_ref, weight_sent_ref, 3 * part * width // (2 * half), out_sum[...])


def leave(
    core, queries, keys, values, mixed, halves, tables, tokens_all, first_all, second_grads, own_embed, time_flat, bias, gain, shift, weight, rows
):
    seq, both = tokens_all.shape
    part = weight.shape[2]
    width = gain.shape[1]
    embed = both - width
    half = embed // 2
    time_lanes = 4 * width + 128
    weight_lanes = 3 * part * width // embed + width

    def shard(lanes):
        return pl.BlockSpec((rows, lanes), lambda i, _: (i, 0))

    inputs = (*tables, tokens_all, first_all)
    extras = (*second_grads, own_embed)
    constants = (time_flat, bias, gain, shift, weight)
    groups = seq // rows
    picked = [pl.BlockSpec((rows, part), lambda i, _, at=at: (at, 0)) for _, at in queries]
    shards = [each for each, _ in queries] + [*keys, *values, *mixed]
    shards += [pair[0] for pair in halves] + [pair[1] for pair in halves]
    shard_specs = picked + [shard(part)] * (len(keys) + len(values)) + [whole(rows, part)] * groups
    shard_specs += [whole(rows // 2, width)] * (2 * groups)
    return pl.pallas_call(
        functools.partial(exit_kernel, groups=groups, calls=len(keys)),
        grid_spec=pltpu.PrefetchScalarGridSpec(
            num_scalar_prefetch=1,
            grid=(seq // rows,),
            in_specs=[shard(each.shape[1]) for each in inputs]
            + shard_specs
            + [whole(*each.shape) for each in extras]
            + [block_of((embed, width), 0, 0), block_of((1, width), 0, 0)]
            + [whole(*each.shape) for each in (gain, shift, weight)],
            out_specs=[shard(width)]
            + [whole(half, time_lanes)] * 2
            + [whole(half, weight_lanes)] * 2,
            scratch_shapes=[
                pltpu.VMEM((3, width, part), F32),
                pltpu.VMEM((embed, 2 * width), F32),
                pltpu.VMEM((8, width), F32),
                pltpu.VMEM((part, width), F32),
            ],
        ),
        out_shape=[jax.ShapeDtypeStruct((seq, width), BF16)]
        + [jax.ShapeDtypeStruct((half, time_lanes), BF16)] * 2
        + [jax.ShapeDtypeStruct((half, weight_lanes), BF16)] * 2,
        compiler_params=limits(48),
        cost_estimate=pl.CostEstimate(
            flops=seq * width,
            bytes_accessed=seq * width,
            transcendentals=seq,
        ),
    )(core, *kept_out(*inputs, *shards, *extras, *constants))


def middle_kernel(
    tokens_ref, top_ref, bottom_ref, embed_ref, time_ref, bias_ref, gain_ref, shift_ref, residual_ref, second_ref
):
    width = gain_ref.shape[1]
    attended = jnp.concatenate([top_ref[...], bottom_ref[...]], axis=0)
    residual = tokens_ref[...].astype(F32) + attended
    residual_ref[...] = residual
    mod = product(embed_ref[...], time_ref[...]) + bias_ref[...]
    normed, _ = norm_parts(residual)
    base = normed * gain_ref[...] + shift_ref[...]
    second_ref[...] = (base * (1.0 + mod[:, :width]) + mod[:, width:]).astype(BF16)


def middle(tokens, top, bottom, embed, time_flat, bias, gain, shift):
    rows, width = tokens.shape
    inputs = (tokens, top, bottom, embed, time_flat, bias, gain, shift)
    shard = whole(rows, width)
    return pl.pallas_call(
        middle_kernel,
        grid=(1,),
        in_specs=[whole(*each.shape) for each in inputs[:4]]
        + [block_of((embed.shape[1], 2 * width), 0, 1), block_of((1, 2 * width), 0, 1)]
        + [whole(*each.shape) for each in inputs[6:]],
        out_specs=[shard, shard],
        out_shape=[pltpu.HBM((rows, width), F32), pltpu.HBM((rows, width), BF16)],
        compiler_params=limits(16),
    )(*kept_out(tokens), top, bottom, *kept_out(*inputs[3:]))


def middle_back_kernel(
    part_ref, other_ref, cotangent_ref, residual_ref, embed_ref, time_ref, bias_ref, gain_ref, shift_ref,
    residual_grad_ref, half_ref, scale_grad_ref, shift_grad_ref, small_ref,
):
    grads = part_ref[...] + other_ref[...]
    factor = 1.0 + product(embed_ref[...], time_ref[...]) + bias_ref[...]
    normed, scale = norm_parts(residual_ref[...])
    gain = gain_ref[...]
    base = normed * gain + shift_ref[...]
    weighted = grads * factor
    inner = weighted * gain
    back = scale * (
        inner
        - jnp.mean(inner, axis=-1, keepdims=True)
        - normed * jnp.mean(inner * normed, axis=-1, keepdims=True)
    )
    residual_grad = cotangent_ref[...].astype(F32) + back
    residual_grad_ref[...] = residual_grad
    half_ref[...] = residual_grad.astype(BF16)
    scale_grad = grads * base
    scale_grad_ref[...] = scale_grad.astype(BF16)
    shift_grad_ref[...] = grads.astype(BF16)
    small_ref[...] = jnp.concatenate(
        [
            jnp.sum(each, axis=0, keepdims=True)
            for each in (weighted * normed, weighted, scale_grad, grads)
        ],
        axis=0,
    )


def middle_back(part, other, cotangent, residual, embed, time_flat, bias, gain, shift):
    rows, width = cotangent.shape
    shard = whole(rows, width)
    inputs = (part, other, cotangent, residual, embed, time_flat, bias, gain, shift)
    return pl.pallas_call(
        middle_back_kernel,
        grid=(1,),
        in_specs=[whole(*each.shape) for each in inputs[:5]]
        + [block_of((embed.shape[1], width), 0, 2), block_of((1, width), 0, 2)]
        + [whole(*each.shape) for each in inputs[7:]],
        out_specs=[shard] * 4 + [whole(4, width)],
        out_shape=[
            pltpu.HBM((rows, width), F32),
            jax.ShapeDtypeStruct((rows, width), BF16),
            pltpu.HBM((rows, width), BF16),
            pltpu.HBM((rows, width), BF16),
            pltpu.HBM((4, width), F32),
        ],
        compiler_params=limits(20),
    )(part, other, *kept_out(*inputs[2:]))


def forward_kernel(
    place_ref, rows_ref, rows_other_ref, grads_ref, grads_other_ref, up_own_ref, down_own_ref, up_near_ref, down_near_ref,
    up_far_ref, down_far_ref,
    branch_ref, branch_other_ref, second_ref, second_other_ref, *grad_refs, planes,
):
    step = pl.program_id(0)
    mine = step == 0
    rows = jnp.concatenate([rows_ref[...], rows_other_ref[...]], axis=0)
    grads = jnp.concatenate([grads_ref[...], grads_other_ref[...]], axis=0)
    count = branch_ref.shape[0]
    far = step < 3
    up = jnp.where(mine, up_own_ref[...], jnp.where(far, up_far_ref[0], up_near_ref[...]))
    up = up.reshape(rows.shape[1], up.shape[2])
    packed = jnp.where(mine, down_own_ref[...], jnp.where(far, down_far_ref[0], down_near_ref[...]))
    half = packed.shape[1] // 2
    down = jnp.concatenate(
        [packed[:, :half].reshape(-1, packed.shape[2]), packed[:, half:].reshape(-1, packed.shape[2])],
        axis=1,
    )
    hidden = product(rows, up)
    active_grad = product(grads, down, TRAIL)
    tail = 0.5 * (1.0 + lax.erf(hidden * math.sqrt(0.5)))
    slope = tail + hidden * jnp.exp(hidden * hidden * -0.5) * (1.0 / math.sqrt(2.0 * math.pi))
    active = (hidden * tail).astype(BF16)
    hidden_grad = (active_grad * slope).astype(BF16)
    branch = product(active, down)
    second = product(hidden_grad, up, TRAIL)

    @pl.when(mine)
    def _():
        branch_ref[...] = branch[:count]
        branch_other_ref[...] = branch[count:]
        second_ref[...] = second[:count]
        second_other_ref[...] = second[count:]

    @pl.when(step > 0)
    def _():
        branch_ref[...] += branch[:count]
        branch_other_ref[...] += branch[count:]
        second_ref[...] += second[:count]
        second_other_ref[...] += second[count:]

    bits = planes.bit_length() - 1
    down_grad = product(active, grads, LEAD)
    up_grad = product(rows, hidden_grad, LEAD)
    grad_refs = list(grad_refs)
    for grad in (down_grad, up_grad):
        middle = grad.shape[1] // 2
        for bit, columns in ((0, grad[:, :middle]), (bits - 1, grad[:, middle:])):
            one = (place_ref[0] >> bit) & 1 == 1
            low = columns.shape[0] // planes << bit
            split = columns.astype(BF16).reshape(-1, 2, low, middle)
            kept_ref, sent_ref = grad_refs.pop(0), grad_refs.pop(0)
            kept_ref[...] = jnp.where(one, split[:, 1], split[:, 0]).reshape(kept_ref.shape)
            sent_ref[...] = jnp.where(one, split[:, 0], split[:, 1]).reshape(sent_ref.shape)


def feed_forward(place, rows, rows_other, grads, grads_other, own_weights, near, far, groups):
    tokens, width = rows.shape
    planes, piece_rows, hidden = own_weights.shape
    half = whole(tokens, width)
    block = (planes, piece_rows // 2, hidden)

    def side(i):
        return jnp.where(i > 1, 1, 0)

    grad_specs, grad_shapes = [], []
    for each_rows, columns in ((hidden // planes, width // 2), (width // planes, hidden // 2)):
        for _ in range(4):
            grad_specs.append(
                pl.BlockSpec((planes // 2, 1, each_rows, columns), lambda i, at: (0, i, 0, 0))
            )
            grad_shapes.append(pltpu.HBM((planes // 2, groups, each_rows, columns), BF16))
    return pl.pallas_call(
        functools.partial(forward_kernel, planes=planes),
        grid_spec=pltpu.PrefetchScalarGridSpec(
            num_scalar_prefetch=1,
            grid=(groups,),
            in_specs=[
                half,
                half,
                half,
                half,
                pl.BlockSpec(block, lambda i, _: (0, 0, 0)),
                pl.BlockSpec(block, lambda i, _: (0, 1, 0)),
                pl.BlockSpec(block, lambda i, _: (0, 0, 0)),
                pl.BlockSpec(block, lambda i, _: (0, 1, 0)),
                pl.BlockSpec((1, *block), lambda i, _: (side(i), 0, 0, 0)),
                pl.BlockSpec((1, *block), lambda i, _: (side(i), 0, 1, 0)),
            ],
            out_specs=[half] * 4 + grad_specs,
        ),
        out_shape=[jax.ShapeDtypeStruct((tokens, width), F32)] * 4 + grad_shapes,
        compiler_params=limits(48),
        cost_estimate=pl.CostEstimate(
            flops=24 * tokens * width * groups * hidden,
            bytes_accessed=8 * width * groups * hidden,
            transcendentals=4 * tokens * groups * hidden,
        ),
    )(place, *kept_out(rows), rows_other, *kept_out(grads, grads_other, own_weights, own_weights, near, near, far, far))


def spread_kernel(core_ref, own_ref, other_ref, out_ref, *, blocks):
    mine = pl.program_id(0) // blocks == core_ref[0]
    width = out_ref.shape[2]
    for at in range(out_ref.shape[1]):
        columns = slice(at * width, (at + 1) * width)
        out_ref[:, at, :] = jnp.where(mine, own_ref[:, columns], other_ref[:, columns]).astype(F32)


def spread(core, own, other, shape, rows):
    blocks = own.shape[0] // rows
    half = pl.BlockSpec((rows, shape[1] * shape[2]), lambda i, _: (i % blocks, 0))
    return pl.pallas_call(
        functools.partial(spread_kernel, blocks=blocks),
        grid_spec=pltpu.PrefetchScalarGridSpec(
            num_scalar_prefetch=1,
            grid=(2 * blocks,),
            in_specs=[half, half],
            out_specs=pl.BlockSpec((rows, shape[1], shape[2]), lambda i, _: (i, 0, 0)),
        ),
        out_shape=jax.ShapeDtypeStruct(shape, F32),
        compiler_params=limits(16),
    )(core, own, other)


def unfold_kernel(core_ref, own_ref, other_ref, out_ref):
    mine = core_ref[0] == 0
    rows, width = own_ref.shape[0], out_ref.shape[2]
    for at in range(own_ref.shape[1] // width):
        columns = slice(at * width, (at + 1) * width)
        own, other = own_ref[:, columns], other_ref[:, columns]
        first = 2 * at * rows
        out_ref[0, first : first + rows] = jnp.where(mine, own, other).astype(F32)
        out_ref[0, first + rows : first + 2 * rows] = jnp.where(mine, other, own).astype(F32)


def unfold(core, own, other, shape):
    rows = own.shape[0]
    blocks = shape[1] // (2 * rows)
    half = pl.BlockSpec((rows, blocks * shape[2]), lambda i, _: (0, i))
    return pl.pallas_call(
        unfold_kernel,
        grid_spec=pltpu.PrefetchScalarGridSpec(
            num_scalar_prefetch=1,
            grid=(shape[0],),
            in_specs=[half, half],
            out_specs=pl.BlockSpec((1, *shape[1:]), lambda i, _: (i, 0, 0)),
        ),
        out_shape=jax.ShapeDtypeStruct(shape, F32),
        compiler_params=limits(16),
    )(core, own, other)


def unpack_kernel(pieces_ref, out_ref):
    out_ref[...] = pieces_ref[...].reshape(out_ref.shape).astype(F32)


def unpack(pieces, planes):
    count, rows, width = pieces.shape
    step = min(planes, 2)
    return pl.pallas_call(
        unpack_kernel,
        grid=(count // step,),
        in_specs=[pl.BlockSpec((step, rows, width), lambda i: (i, 0, 0))],
        out_specs=pl.BlockSpec(
            (step * rows, width), lambda i: (i % (planes // step), i // (planes // step))
        ),
        out_shape=jax.ShapeDtypeStruct((planes * rows, width * count // planes), F32),
        compiler_params=limits(16),
    )(pieces)


def swap(values, axis_name, bit):
    size = lax.axis_size(axis_name)
    return lax.ppermute(values, axis_name, [(at, at ^ (1 << bit)) for at in range(size)])


def bit_of(axis_name, bit):
    return (lax.axis_index(axis_name) >> bit) & 1


def after(values, *others):
    return lax.optimization_barrier((values, others))[0]


def exchange(values, axis_name, bit, dim):
    own = bit_of(axis_name, bit)
    kept = lax.dynamic_index_in_dim(values, own, dim, keepdims=False)
    sent = lax.dynamic_index_in_dim(values, 1 - own, dim, keepdims=False)
    return (kept, swap(sent, axis_name, bit))


def total(kept, got):
    return (kept.astype(F32) + got.astype(F32)).astype(BF16)


def double(values, axis_name, bit, dim):
    own = bit_of(axis_name, bit) == 0
    got = swap(values, axis_name, bit)
    return jnp.stack([jnp.where(own, values, got), jnp.where(own, got, values)], axis=dim)


class PlaneScatter:
    def __init__(self, arrays, orders, dim):
        bits = len(orders[0])
        self.dim = dim
        self.arrays = [
            each.reshape(each.shape[:dim] + (2,) * bits + each.shape[dim + 1 :]) for each in arrays
        ]
        self.orders = [list(order) for order in orders]
        self.left = [list(range(bits - 1, -1, -1)) for _ in orders]

    @classmethod
    def started(cls, kept, sent, orders, dim):
        self = cls.__new__(cls)
        bits = len(orders[0])
        self.dim = dim
        self.orders = [list(order[1:]) for order in orders]
        self.left = [[bit for bit in range(bits - 1, -1, -1) if bit != order[0]] for order in orders]
        self.kept = [
            each.reshape(each.shape[:dim] + (2,) * (bits - 1) + each.shape[dim + 1 :]) for each in kept
        ]
        self.got = [
            swap(each, "plane", order[0]).reshape(like.shape)
            for each, like, order in zip(sent, self.kept, orders)
        ]
        return self

    def send(self):
        self.kept, self.got = [], []
        for values, order, left in zip(self.arrays, self.orders, self.left):
            bit = order.pop(0)
            kept, got = exchange(values, "plane", bit, self.dim + left.index(bit))
            left.remove(bit)
            self.kept.append(kept)
            self.got.append(got)
        self.meet()

    def meet(self, *others):
        self.got, others = lax.optimization_barrier((self.got, others))
        return others

    def add(self):
        self.arrays = [total(kept, got) for kept, got in zip(self.kept, self.got)]

    def finish(self):
        while self.orders[0]:
            self.send()
            self.add()
        return self.arrays


class PlaneGather:
    def __init__(self, arrays, orders):
        self.arrays = list(arrays)
        self.orders = [list(order) for order in orders]
        self.left = [[] for _ in orders]

    def send(self):
        self.bits = [order.pop() for order in self.orders]
        self.got = [swap(values, "plane", bit) for values, bit in zip(self.arrays, self.bits)]

    def join(self):
        for at, bit in enumerate(self.bits):
            self.left[at] = sorted(self.left[at] + [bit], reverse=True)
            own = bit_of("plane", bit) == 0
            values, got = self.arrays[at], self.got[at]
            pair = (jnp.where(own, values, got), jnp.where(own, got, values))
            self.arrays[at] = jnp.stack(pair, axis=self.left[at].index(bit))

    def finish(self):
        while self.orders[0]:
            self.send()
            self.arrays, self.got = lax.optimization_barrier((self.arrays, self.got))
            self.join()
        return self.arrays


def ring_gather(shard, meanwhile=None):
    size = lax.axis_size("tensor")
    half = shard.shape[0] // 2
    right, left = [shard[:half]], [shard[half:]]
    for step in range(1, size):
        others = () if meanwhile is None else meanwhile(step, right, left)
        right.append(lax.ppermute(right[-1], "tensor", [(at, (at + 1) % size) for at in range(size)]))
        left.append(lax.ppermute(left[-1], "tensor", [(at, (at - 1) % size) for at in range(size)]))
        right[-1], left[-1], others = lax.optimization_barrier((right[-1], left[-1], others))
        if meanwhile is not None:
            meanwhile(-step, others, None)
    return [(right[(size - at) % size], left[at]) for at in range(size)]


class RingScatter:
    def __init__(self, chunks):
        self.chunks = chunks
        self.size = len(chunks)
        self.half = chunks[0].shape[0] // 2
        self.step = 0
        self.right = chunks[-1][: self.half]
        self.left = chunks[1][self.half :]

    def send(self):
        size = self.size
        right = lax.ppermute(self.right, "tensor", [(at, (at + 1) % size) for at in range(size)])
        left = lax.ppermute(self.left, "tensor", [(at, (at - 1) % size) for at in range(size)])
        self.got = lax.optimization_barrier((right, left))

    def add(self):
        self.step += 1
        right, left = self.got
        self.right = right.astype(F32) + self.chunks[self.size - 1 - self.step][: self.half].astype(F32)
        self.left = left.astype(F32) + self.chunks[(self.step + 1) % self.size][self.half :].astype(F32)
        if self.step < self.size - 1:
            self.right, self.left = self.right.astype(BF16), self.left.astype(BF16)

    def finish(self):
        while self.step < self.size - 1:
            self.send()
            self.add()
        return (self.right, self.left)


def own_first(values, dim):
    size = lax.axis_size("tensor")
    stretch = values.shape[dim] // size
    doubled = jnp.concatenate([values, values], axis=dim)
    return lax.dynamic_slice_in_dim(
        doubled, lax.axis_index("tensor") * stretch, values.shape[dim], dim
    )


def local(
    tokens,
    time_embed,
    segment_ids,
    positions,
    first_gain,
    first_bias,
    second_gain,
    second_bias,
    time_weight,
    time_bias,
    qkv_weight,
    out_weight,
    up_weight,
    down_weight,
    cotangent,
):
    local_rows, width = tokens.shape
    embed_width = time_embed.shape[1]
    local_width = qkv_weight.shape[2]
    hidden_local = up_weight.shape[1]
    half_hidden = hidden_local // 2
    planes = lax.axis_size("plane")
    groups = lax.axis_size("tensor")
    plane_at = lax.axis_index("plane")
    core_at = lax.axis_index("core")
    place = plane_at.astype(jnp.int32).reshape(1)
    arrival = sorted(range(groups), key=lambda at: max(at, groups - at) if at else 0)
    rising = list(range(planes.bit_length() - 1))
    falling = rising[::-1]

    up_rows = width // planes
    up_piece = lax.dynamic_slice(
        up_weight, (plane_at * up_rows, core_at * half_hidden), (up_rows, half_hidden)
    )
    down_rows = half_hidden // planes
    down_piece = lax.dynamic_slice(
        down_weight, (core_at * half_hidden + plane_at * down_rows, 0), (down_rows, width)
    )
    piece = jnp.concatenate([up_piece, down_piece[:, :half_hidden], down_piece[:, half_hidden:]], axis=0)
    ahead = [(at, (at + 1) % groups) for at in range(groups)]
    behind = [(at, (at - 1) % groups) for at in range(groups)]
    up_half = lax.dynamic_slice_in_dim(up_weight, core_at * half_hidden, half_hidden, 1)
    down_half = lax.dynamic_slice_in_dim(down_weight, core_at * half_hidden, half_hidden, 0)
    down_half = down_half.reshape(planes, down_rows, width)
    own_pieces = jnp.concatenate(
        [
            up_half.reshape(planes, up_rows, half_hidden),
            down_half[..., :half_hidden],
            down_half[..., half_hidden:],
        ],
        axis=1,
    )

    held = {
        "time": time_weight.reshape(embed_width, 4 * width),
        "tables": rotary_tables(own_first(positions, 1).reshape(-1), 2 * HEAD),
        "pieces": own_pieces,
        "cotangent": swap(cotangent, "core", 0),
        "near": lax.ppermute(piece, "tensor", ahead),
    }
    bias_flat = time_bias.reshape(1, 4 * width)
    first_gain, first_bias = first_gain.reshape(1, width), first_bias.reshape(1, width)
    second_gain, second_bias = second_gain.reshape(1, width), second_bias.reshape(1, width)
    qkv_planes = jnp.transpose(qkv_weight, (1, 0, 2))
    segments = own_first(segment_ids, 1)
    columns = segments.reshape(-1, 1)

    def enter(places, halves, row):
        return entry(
            halves, held["tables"], held["time"], bias_flat, first_gain, first_bias, qkv_planes, places, groups, row
        )

    def meanwhile(step, right, left):
        if step == 1:
            return held
        if step == -1:
            held.update(right)
        elif step == 2:
            return enter([0], (right[0], left[0]), ())
        elif step > 2 and 2 * (step - 1) == groups:
            return enter([step - 1], (right[step - 1], left[step - 1]), held["row"])
        elif step > 0:
            return held["row"]
        else:
            held["row"] = right
        return None

    gathered = ring_gather(jnp.concatenate([tokens, time_embed], axis=1), meanwhile)
    near = lax.all_gather(held["near"], "plane", axis=0)
    piece, passed = after((piece, held["near"]), gathered[arrival[-1]])
    far = [lax.ppermute(piece, "tensor", behind), lax.ppermute(passed, "tensor", ahead)]
    row = held["row"]
    for first in range(2, len(arrival), 2):
        places = arrival[first : first + 2]
        row = enter(places, [half for at in places for half in gathered[at]], row)
    tables, time_flat = held["tables"], held["time"]
    tokens_all, first_all, queries, keys, values = row
    keys, far, near = lax.optimization_barrier((keys, far, near))
    far = lax.all_gather(jnp.stack(far), "plane", axis=1)
    mixed, logsums, parts = {}, {}, {}
    for at in list(range(groups - 1, -1, -1)):
        mixed[at], logsums[at], parts[at] = attend(
            queries, keys, values, segments, columns, out_weight, at, local_rows
        )
    attended = RingScatter([parts[at] for at in range(groups)]).finish()

    residual, second_normed = middle(
        tokens, *attended, time_embed, time_flat, bias_flat, second_gain, second_bias
    )
    branch_own, branch_other, second_own, second_other, *grad_parts = feed_forward(
        place,
        second_normed,
        swap(second_normed, "core", 0),
        cotangent,
        held["cotangent"],
        held["pieces"],
        near.reshape(planes, 2 * up_rows, half_hidden),
        far,
        groups,
    )
    second_other = swap(second_other, "core", 0)

    sums = {"down": PlaneScatter.started(grad_parts[:4:2], grad_parts[1:4:2], [rising, falling], 0)}
    branch = branch_own + swap(branch_other, "core", 0)
    result = (residual + branch).astype(BF16)

    residual_grad, attended_own, scale_two_grad, shift_two_grad, small_two = middle_back(
        second_own,
        second_other,
        cotangent,
        residual,
        time_embed,
        time_flat,
        bias_flat,
        second_gain,
        second_bias,
    )
    def turn(places, halves):
        return attend_back(
            halves,
            queries,
            keys,
            values,
            [logsums[at] for at in places],
            segments,
            columns,
            out_weight,
            tables,
            places,
        )

    back = {}

    def meanwhile_back(step, right, left):
        if step == 2:
            return (turn([0], (right[0], left[0])), sums["down"].got)
        elif step == -2:
            back[(0,)], sums["down"].got = right
            sums["down"].add()
            if sums["down"].orders[0]:
                sums["down"].send()
        elif step == 3:
            return (turn([2], (right[2], left[2])), sums["down"].got)
        elif step == -3:
            back[(2,)], sums["down"].got = right
            up_parts = after(grad_parts[4:], sums["down"].got)
            sums["up"] = PlaneScatter.started(up_parts[::2], up_parts[1::2], [rising, falling], 0)
        return ()

    def to_tensor(arrays):
        parts = [jnp.concatenate([each[at] for each in arrays], axis=-1) for at in range(groups)]
        received = [
            lax.ppermute(parts[hop], "tensor", [(at, (at + hop) % groups) for at in range(groups)])
            for hop in range(1, groups)
        ]
        return (parts[0], received)

    def joined(own_part, received):
        return sum(each.astype(F32) for each in [own_part, *received]).astype(BF16)

    attended_halves = ring_gather(attended_own, meanwhile_back)
    sums["down"].add()
    down_own, down_received = to_tensor(sums["down"].finish())
    places = (1, 3)
    back[places] = turn(places, [half for at in places for half in attended_halves[at]])
    (back[places],) = sums["up"].meet(back[places])
    sums["up"].add()
    if sums["up"].orders[0]:
        sums["up"].send()
    query_shards = {at: (parts[0], which) for places, parts in back.items() for which, at in enumerate(places)}
    received = [
        lax.ppermute(parts[hop], "tensor", [(at, (at + hop) % groups) for at in range(groups)])
        for hop in range(1, groups)
    ]
    core_own = core_at.astype(jnp.int32).reshape(1)
    left = leave(
        core_own,
        [query_shards[at] for at in range(groups)],
        [parts[1] for parts in back.values()],
        [parts[2] for parts in back.values()],
        [mixed[at] for at in range(groups)],
        attended_halves,
        tables,
        tokens_all,
        first_all,
        (scale_two_grad, shift_two_grad, small_two),
        time_embed,
        time_flat,
        bias_flat,
        first_gain,
        first_bias,
        qkv_planes,
        local_rows,
    )
    left, down_received = sums["up"].meet(left, down_received)
    sums["up"].add()
    up_own, up_received = to_tensor(sums["up"].finish())
    down_all = lax.all_gather(joined(down_own, down_received), ("core", "plane"), axis=0, tiled=True)
    first_half, time_kept, time_sent, weight_kept, weight_sent = left

    time_got, weight_got = swap(time_sent, "core", 0), swap(weight_sent, "core", 0)

    def by_plane(pack):
        return pack.reshape(planes, embed_width // (2 * planes), -1)

    pack_sums = PlaneScatter(
        [by_plane(total(time_kept, time_got)), by_plane(total(weight_kept, weight_got))], [rising, falling], 0
    )
    ring = RingScatter([first_half[at * local_rows : (at + 1) * local_rows] for at in range(groups)])
    pack_sums.send()
    pack_sums.add()
    ring.send()
    second = bool(pack_sums.orders[0])
    if second:
        pack_sums.send()
    (ring.got, up_received) = pack_sums.meet(ring.got, up_received)
    if second:
        pack_sums.add()
    time_own, weight_own = pack_sums.finish()
    ring.add()
    up_all = lax.all_gather(joined(up_own, up_received), ("core", "plane"), axis=0)
    time_got = swap(time_own, "tensor", 0)
    time_got, down_all = lax.optimization_barrier((time_got, down_all))
    down_summed = down_all.astype(F32)
    time_own = total(time_own, time_got)
    time_got = swap(time_own, "tensor", 1)
    time_got, down_summed = lax.optimization_barrier((time_got, down_summed))
    time_sum = total(time_own, time_got)
    (ring.right, ring.left), time_sum = lax.optimization_barrier(((ring.right, ring.left), time_sum))
    gather = PlaneGather([time_sum, weight_own], [rising, falling])
    ring.send()
    gather.send()
    ring.got, gather.got, up_all = lax.optimization_barrier((ring.got, gather.got, up_all))
    gather.join()
    ring.add()
    ring.send()
    (up_all,) = kept_out(up_all)
    up_summed = unpack(up_all, planes)
    if gather.orders[0]:
        gather.send()
        ring.got, gather.got, up_summed = lax.optimization_barrier((ring.got, gather.got, up_summed))
        gather.join()
    ring.add()
    time_half, weight_half = gather.finish()
    packs = [time_half.reshape(embed_width // 2, -1), weight_half.reshape(embed_width // 2, -1)]
    (time_half, time_other), (weight_half, weight_other) = ((pack, swap(pack, "core", 0)) for pack in packs)
    first_grad = ring.finish()
    time_weight_grad = spread(
        core_own, time_half, time_other, (embed_width, 4, width), min(64, embed_width // 2)
    )
    qkv_lanes = 3 * local_width * width // embed_width
    qkv_summed = jnp.transpose(
        unfold(core_own, weight_half, weight_other, (3, width, local_width)), (1, 0, 2)
    )

    def both_cores(own_half, other_half):
        mine = core_at == 0
        halves = [jnp.where(mine, own_half, other_half), jnp.where(mine, other_half, own_half)]
        return jnp.concatenate(halves, axis=0).astype(F32)

    out_summed = both_cores(weight_half[:, qkv_lanes:], weight_other[:, qkv_lanes:])
    small = both_cores(time_half[:, 4 * width :], time_other[:, 4 * width :])[: width // 16]
    small = jnp.transpose(small.reshape(width // 128, 8, 128), (1, 0, 2)).reshape(8, width)

    own_normed, own_scale = norm_parts(tokens.astype(F32))
    mod_own = product(time_embed, time_flat[:, :width]) + bias_flat[:, :width]
    first_grad = jnp.concatenate(first_grad, axis=0)
    input_grad = residual_grad + norm_input_back(first_grad, own_normed, own_scale, first_gain, mod_own)
    return (
        result,
        input_grad,
        small[0],
        small[1],
        small[4],
        small[5],
        time_weight_grad,
        jnp.concatenate([small[2:4], small[6:]], axis=0),
        qkv_summed,
        out_summed,
        up_summed,
        down_summed,
    )


def solution(mesh):
    whole, tensor = mesh.devices.shape
    finer = Mesh(mesh.devices.reshape(whole // 2, 2, tensor), ("plane", "core", "tensor"))
    rows = P(("plane", "core", "tensor"), None)
    group = P(("plane", "core"), None)
    return jax.shard_map(
        local,
        mesh=finer,
        in_specs=(
            rows,
            rows,
            group,
            group,
            P(),
            P(),
            P(),
            P(),
            P(),
            P(),
            P(None, None, "tensor"),
            P("tensor", None),
            P(None, "tensor"),
            P("tensor", None),
            rows,
        ),
        out_specs=(
            rows,
            rows,
            P(),
            P(),
            P(),
            P(),
            P(),
            P(),
            P(None, None, "tensor"),
            P("tensor", None),
            P(None, "tensor"),
            P("tensor", None),
        ),
        check_vma=False,
    )
```

```python
import functools
import math

import jax
import jax.numpy as jnp
from jax import lax
from jax.experimental import pallas as pl
from jax.experimental.pallas import tpu as pltpu
from jax.sharding import Mesh
from jax.sharding import PartitionSpec as P

HEAD = 64
F32 = jnp.float32
BF16 = jnp.bfloat16
LEAD = (((0,), (0,)), ((), ()))
TRAIL = (((1,), (1,)), ((), ()))


def product(left, right, dims=(((1,), (0,)), ((), ()))):
    return lax.dot_general(left, right, dims, preferred_element_type=F32)


def norm_parts(values):
    centre = values - jnp.mean(values, axis=-1, keepdims=True)
    spread = jnp.mean(centre * centre, axis=-1, keepdims=True)
    scale = lax.rsqrt(spread + 1e-05)
    return (centre * scale, scale)


def norm_input_back(grads, normed, scale, gain, mod_scale):
    inner = grads * (1.0 + mod_scale) * gain
    return scale * (
        inner
        - jnp.mean(inner, axis=-1, keepdims=True)
        - normed * jnp.mean(inner * normed, axis=-1, keepdims=True)
    )


def rotary_tables(places, lanes):
    half_size = HEAD // 2
    lane = jnp.arange(lanes)
    frequency = jnp.exp((lane % half_size).astype(F32) * (-math.log(10000.0) / half_size))
    angles = places.astype(F32)[:, None] * frequency[None, :]
    sign = jnp.where(lane % HEAD < half_size, -1.0, 1.0)
    return (jnp.cos(angles), jnp.sin(angles) * sign[None, :])


def kept_out(*arrays):
    return tuple(pltpu.with_memory_space_constraint(each, pltpu.HBM) for each in arrays)


def block_of(shape, *place):
    return pl.BlockSpec(shape, lambda *_: place)


def whole(*shape):
    return pl.BlockSpec(shape, lambda *_: (0,) * len(shape))


def limits(megabytes):
    return pltpu.CompilerParams(vmem_limit_bytes=megabytes << 20)


def partner(values):
    lanes = values.shape[1]
    lane = lax.broadcasted_iota(jnp.int32, values.shape, 1)
    above = pltpu.roll(values, lanes - HEAD // 2, 1)
    below = pltpu.roll(values, HEAD // 2, 1)
    return jnp.where(lane % HEAD < HEAD // 2, above, below)


def widened(table, lanes):
    return jnp.concatenate([table] * (lanes // table.shape[1]), axis=1)


def turned(values, cosine, sine):
    return values * widened(cosine, values.shape[1]) + partner(values) * widened(sine, values.shape[1])


def entry_kernel(
    *refs, count
):
    halves, refs = refs[: 2 * count], refs[2 * count :]
    cosine_ref, sine_ref, time_ref, bias_ref, gain_ref, shift_ref, weight_ref = refs[:7]
    tokens_ref, first_ref, query_ref, key_ref, value_ref = refs[-5:]
    rows = jnp.concatenate([halves[0][...], halves[1][...]], axis=0)
    for at in range(1, count):
        other = jnp.concatenate([halves[2 * at][...], halves[2 * at + 1][...]], axis=0)
        rows = jnp.where(pl.program_id(0) == at, other, rows)
    tokens_ref[...] = rows
    width = gain_ref.shape[1]
    mod = product(rows[:, width:], time_ref[...]) + bias_ref[...]
    normed, _ = norm_parts(rows[:, :width].astype(F32))
    base = normed * gain_ref[...] + shift_ref[...]
    first = (base * (1.0 + mod[:, :width]) + mod[:, width:]).astype(BF16)
    first_ref[...] = first
    cosine, sine = cosine_ref[...], sine_ref[...]
    query_ref[...] = turned(product(first, weight_ref[0]), cosine, sine).astype(BF16)
    key_ref[...] = turned(product(first, weight_ref[1]), cosine, sine).astype(BF16)
    value_ref[...] = product(first, weight_ref[2]).astype(BF16)


def entry(halves, tables, time_flat, bias, gain, shift, weight, places, groups, before):
    half, both = halves[0].shape
    count = len(places)
    apart = places[-1] - places[0]
    rows = 2 * half
    width = gain.shape[1]
    part = weight.shape[2]
    lanes = tables[0].shape[1]
    widths = (both, width, part, part, part)
    table = pl.BlockSpec((rows, lanes), lambda i: (places[0] + i * apart, 0))
    inputs = (*halves, *kept_out(*tables, time_flat, bias, gain, shift, weight))
    return pl.pallas_call(
        functools.partial(entry_kernel, count=count),
        grid=(count,),
        in_specs=[whole(half, both)] * (2 * count)
        + [table, table]
        + [block_of((both - width, 2 * width), 0, 0), block_of((1, 2 * width), 0, 0)]
        + [whole(*each.shape) for each in (gain, shift, weight)]
        + [pl.BlockSpec(memory_space=pl.ANY)] * len(before),
        out_specs=[pl.BlockSpec((rows, each), lambda i: (places[0] + i * apart, 0)) for each in widths],
        out_shape=[pltpu.HBM((rows * groups, each), BF16) for each in widths],
        input_output_aliases={len(inputs) + at: at for at in range(len(before))},
        compiler_params=limits(16),
        cost_estimate=pl.CostEstimate(
            flops=2 * rows * width * 4 * part + 4 * rows * width * (both - width),
            bytes_accessed=8 * rows * width + 6 * width * part,
            transcendentals=rows,
        ),
    )(*inputs, *kept_out(*before))


def pair_lanes(values, pair):
    return values[:, pair * 2 * HEAD : (pair + 1) * 2 * HEAD]


def apart(values, pair):
    values = pair_lanes(values, pair)
    lane = lax.broadcasted_iota(jnp.int32, values.shape, 1)
    zeros = jnp.zeros_like(values)
    return jnp.concatenate(
        [jnp.where(lane < HEAD, values, zeros), jnp.where(lane < HEAD, zeros, values)], axis=0
    )


def together(values):
    rows = values.shape[0] // 2
    lane = lax.broadcasted_iota(jnp.int32, (rows, values.shape[1]), 1)
    return jnp.where(lane < HEAD, values[:rows], values[rows:])


def attend_kernel(query_ref, key_ref, value_ref, own_ref, all_ref, out_ref, mixed_ref, logsum_ref, part_ref):
    queries, keys, values = query_ref[...], key_ref[...], value_ref[...]
    own = own_ref[...]
    allowed = all_ref[...] == jnp.concatenate([own, own], axis=1)
    scale = 1.0 / math.sqrt(HEAD)
    rows = queries.shape[0]
    pairs = []
    for pair in range(queries.shape[1] // (2 * HEAD)):
        scores = product(pair_lanes(keys, pair), apart(queries, pair), TRAIL) * scale
        scores = jnp.where(allowed, scores, -1e30)
        peak = jnp.max(scores, axis=0, keepdims=True)
        raised = jnp.exp(scores - peak)
        total_raised = jnp.sum(raised, axis=0, keepdims=True)
        attention = (raised / total_raised).astype(BF16)
        logsum = peak + jnp.log(total_raised)
        logsum_ref[2 * pair : 2 * pair + 1, :] = logsum[:, :rows]
        logsum_ref[2 * pair + 1 : 2 * pair + 2, :] = logsum[:, rows:]
        pairs.append(together(product(attention, pair_lanes(values, pair), LEAD)))
    mixed = jnp.concatenate(pairs, axis=1).astype(BF16)
    mixed_ref[...] = mixed
    part_ref[...] = product(mixed, out_ref[...]).astype(BF16)


def attend(queries, keys, values, own_segments, all_segments, out_weight, place, rows):
    seq, part = keys.shape
    width = out_weight.shape[1]
    heads = part // HEAD
    return pl.pallas_call(
        attend_kernel,
        grid=(1,),
        in_specs=[
            pl.BlockSpec((rows, part), lambda i: (place, 0)),
            whole(seq, part),
            whole(seq, part),
            pl.BlockSpec((1, rows), lambda i: (0, place)),
            whole(seq, 1),
            whole(part, width),
        ],
        out_specs=[whole(rows, part), whole(heads, rows), whole(rows, width)],
        out_shape=[
            pltpu.HBM((rows, part), BF16),
            pltpu.HBM((heads, rows), F32),
            jax.ShapeDtypeStruct((rows, width), BF16),
        ],
        compiler_params=limits(28),
        cost_estimate=pl.CostEstimate(
            flops=4 * rows * seq * part + 2 * rows * part * width,
            bytes_accessed=4 * seq * part + 4 * rows * width,
            transcendentals=rows * seq * heads,
        ),
    )(queries, keys, values, own_segments, all_segments, out_weight)


def attend_back_kernel(
    query_ref, key_ref, value_ref, own_ref, all_ref, out_ref, cosine_ref, sine_ref, *refs, count
):
    halves, logsum_refs, (grad_ref, key_grad_ref, value_grad_ref) = (
        refs[: 2 * count],
        refs[2 * count : 3 * count],
        refs[3 * count :],
    )
    step = pl.program_id(0)
    queries, keys, values = query_ref[...], key_ref[...], value_ref[...]
    incoming = jnp.concatenate([halves[0][...], halves[1][...]], axis=0)
    logsums = logsum_refs[0][...]
    for at in range(1, count):
        other = jnp.concatenate([halves[2 * at][...], halves[2 * at + 1][...]], axis=0)
        incoming = jnp.where(step == at, other, incoming)
        logsums = jnp.where(step == at, logsum_refs[at][...], logsums)
    mixed_grad = product(incoming, out_ref[...], TRAIL).astype(BF16)
    own = own_ref[...]
    allowed = all_ref[...] == jnp.concatenate([own, own], axis=1)
    scale = 1.0 / math.sqrt(HEAD)
    query_pairs, key_pairs, value_pairs = [], [], []
    for pair in range(queries.shape[1] // (2 * HEAD)):
        query, grad = apart(queries, pair), apart(mixed_grad, pair)
        scores = product(pair_lanes(keys, pair), query, TRAIL) * scale
        scores = jnp.where(allowed, scores, -1e30)
        logsum = jnp.concatenate(
            [logsums[2 * pair : 2 * pair + 1], logsums[2 * pair + 1 : 2 * pair + 2]], axis=1
        )
        probability = jnp.exp(scores - logsum)
        prob_grad = product(pair_lanes(values, pair), grad, TRAIL)
        row_dot = jnp.sum(probability * prob_grad, axis=0, keepdims=True)
        score_grad = (probability * (prob_grad - row_dot)).astype(BF16)
        value_pairs.append(product(probability.astype(BF16), grad))
        key_pairs.append(product(score_grad, query))
        query_pairs.append(together(product(score_grad, pair_lanes(keys, pair), LEAD)))
    query_grad = jnp.concatenate(query_pairs, axis=1) * scale
    key_grad = jnp.concatenate(key_pairs, axis=1) * scale
    value_grad = jnp.concatenate(value_pairs, axis=1)
    grad_ref[...] = turned(query_grad, cosine_ref[...], -sine_ref[...]).astype(BF16)

    @pl.when(step == 0)
    def _():
        key_grad_ref[...] = key_grad
        value_grad_ref[...] = value_grad

    @pl.when(step > 0)
    def _():
        key_grad_ref[...] += key_grad
        value_grad_ref[...] += value_grad


def attend_back(halves, queries, keys, values, logsums, own_segments, all_segments, out_weight, tables, places):
    seq, part = keys.shape
    heads, rows = logsums[0].shape
    width = out_weight.shape[1]
    count = len(places)
    apart = places[-1] - places[0]
    shard = pl.BlockSpec((rows, part), lambda i: (places[0] + i * apart, 0))
    table = pl.BlockSpec((rows, tables[0].shape[1]), lambda i: (places[0] + i * apart, 0))
    constants = (own_segments, all_segments, out_weight, *tables)
    return pl.pallas_call(
        functools.partial(attend_back_kernel, count=count),
        grid=(count,),
        in_specs=[
            shard,
            whole(seq, part),
            whole(seq, part),
            pl.BlockSpec((1, rows), lambda i: (0, places[0] + i * apart)),
            whole(seq, 1),
            whole(part, width),
            table,
            table,
        ]
        + [whole(rows // 2, width)] * (2 * count)
        + [whole(heads, rows)] * count,
        out_specs=[
            pl.BlockSpec((rows, part), lambda i: (i, 0)),
            whole(seq, part),
            whole(seq, part),
        ],
        out_shape=[
            pltpu.HBM((count * rows, part), BF16),
            pltpu.HBM((seq, part), F32),
            pltpu.HBM((seq, part), F32),
        ],
        compiler_params=limits(44),
        cost_estimate=pl.CostEstimate(
            flops=10 * count * rows * seq * part + 2 * count * rows * part * width,
            bytes_accessed=16 * seq * part,
            transcendentals=count * rows * seq * heads,
        ),
    )(queries, keys, values, *kept_out(*constants), *halves, *kept_out(*logsums))


def exit_kernel(
    place_ref, cosine_ref, sine_ref, tokens_ref, first_ref, *refs, groups, calls
):
    shards = list(refs[:-18])
    lengths = (groups, calls, calls, groups, groups, groups)
    query_refs, key_refs, value_refs, mixed_refs, top_refs, bottom_refs = (
        [shards.pop(0) for _ in range(length)] for length in lengths
    )
    (
        scale_two_ref, shift_two_ref, small_two_ref, own_embed_ref, time_ref, bias_ref, gain_ref, shift_ref, weight_ref,
        first_grad_ref, time_kept_ref, time_sent_ref, weight_kept_ref, weight_sent_ref,
        weight_sum, time_sum, small_sum, out_sum,
    ) = refs[-18:]
    step = pl.program_id(0)
    width = gain_ref.shape[1]
    key_grad = sum(ref[...] for ref in key_refs)
    key_grad = turned(key_grad, cosine_ref[...], -sine_ref[...]).astype(BF16)

    def this(refs):
        values = refs[0][...]
        for at in range(1, len(refs)):
            values = jnp.where(step == at, refs[at][...], values)
        return values

    incoming = jnp.concatenate([this(top_refs), this(bottom_refs)], axis=0)
    out_part = product(this(mixed_refs), incoming, LEAD)
    grads = (this(query_refs), key_grad, sum(ref[...] for ref in value_refs).astype(BF16))
    first_grad = sum(product(grad, weight_ref[at], TRAIL) for at, grad in enumerate(grads))
    first_half = first_grad.astype(BF16)
    first_grad_ref[...] = first_half
    first = first_ref[...]
    weight_parts = [product(first, grad, LEAD) for grad in grads]
    rows = tokens_ref[...]
    embed = rows[:, width:]
    factor = 1.0 + product(embed, time_ref[...]) + bias_ref[...]
    normed, _ = norm_parts(rows[:, :width].astype(F32))
    base = normed * gain_ref[...] + shift_ref[...]
    scale_grad = first_grad * base
    weighted = first_grad * factor
    both = jnp.concatenate([scale_grad.astype(BF16), first_half], axis=1)
    time_part = product(embed, both, LEAD)
    small = jnp.concatenate(
        [
            jnp.sum(each, axis=0, keepdims=True)
            for each in (weighted * normed, weighted, scale_grad, first_grad)
        ],
        axis=0,
    )

    @pl.when(step == 0)
    def _():
        for at, part in enumerate(weight_parts):
            weight_sum[at] = part
        time_sum[...] = time_part
        out_sum[...] = out_part
        small_sum[:4] = small
        small_sum[4:] = small_two_ref[...]

    @pl.when(step > 0)
    def _():
        for at, part in enumerate(weight_parts):
            weight_sum[at] += part
        time_sum[...] += time_part
        out_sum[...] += out_part
        small_sum[:4] += small

    @pl.when(step == pl.num_programs(0) - 1)
    def _():
        one = place_ref[0] == 1
        half = time_kept_ref.shape[0]

        def put(kept_ref, sent_ref, at, values):
            values = values.astype(BF16)
            columns = slice(at, at + values.shape[1])
            kept_ref[:, columns] = jnp.where(one, values[half:], values[:half])
            sent_ref[:, columns] = jnp.where(one, values[:half], values[half:])

        put(time_kept_ref, time_sent_ref, 0, time_sum[...])
        own_embed = own_embed_ref[...]
        put(time_kept_ref, time_sent_ref, 2 * width, product(own_embed, scale_two_ref[...], LEAD))
        put(time_kept_ref, time_sent_ref, 3 * width, product(own_embed, shift_two_ref[...], LEAD))
        smalls = small_sum[...]
        smalls = jnp.concatenate(
            [smalls[:, at : at + 128] for at in range(0, width, 128)]
            + [jnp.zeros((2 * half - width // 16, 128), F32)],
            axis=0,
        )
        put(time_kept_ref, time_sent_ref, 4 * width, smalls)
        part = weight_sum.shape[2]
        for at in range(3):
            for row in range(0, width, 2 * half):
                column = (at * width + row) // (2 * half) * part
                put(weight_kept_ref, weight_sent_ref, column, weight_sum[at, row : row + 2 * half])
        put(weight_kept_ref, weight_sent_ref, 3 * part * width // (2 * half), out_sum[...])


def leave(
    core, queries, keys, values, mixed, halves, tables, tokens_all, first_all, second_grads, own_embed, time_flat, bias, gain, shift, weight, rows
):
    seq, both = tokens_all.shape
    part = weight.shape[2]
    width = gain.shape[1]
    embed = both - width
    half = embed // 2
    time_lanes = 4 * width + 128
    weight_lanes = 3 * part * width // embed + width

    def shard(lanes):
        return pl.BlockSpec((rows, lanes), lambda i, _: (i, 0))

    inputs = (*tables, tokens_all, first_all)
    extras = (*second_grads, own_embed)
    constants = (time_flat, bias, gain, shift, weight)
    groups = seq // rows
    picked = [pl.BlockSpec((rows, part), lambda i, _, at=at: (at, 0)) for _, at in queries]
    shards = [each for each, _ in queries] + [*keys, *values, *mixed]
    shards += [pair[0] for pair in halves] + [pair[1] for pair in halves]
    shard_specs = picked + [shard(part)] * (len(keys) + len(values)) + [whole(rows, part)] * groups
    shard_specs += [whole(rows // 2, width)] * (2 * groups)
    return pl.pallas_call(
        functools.partial(exit_kernel, groups=groups, calls=len(keys)),
        grid_spec=pltpu.PrefetchScalarGridSpec(
            num_scalar_prefetch=1,
            grid=(seq // rows,),
            in_specs=[shard(each.shape[1]) for each in inputs]
            + shard_specs
            + [whole(*each.shape) for each in extras]
            + [block_of((embed, width), 0, 0), block_of((1, width), 0, 0)]
            + [whole(*each.shape) for each in (gain, shift, weight)],
            out_specs=[shard(width)]
            + [whole(half, time_lanes)] * 2
            + [whole(half, weight_lanes)] * 2,
            scratch_shapes=[
                pltpu.VMEM((3, width, part), F32),
                pltpu.VMEM((embed, 2 * width), F32),
                pltpu.VMEM((8, width), F32),
                pltpu.VMEM((part, width), F32),
            ],
        ),
        out_shape=[jax.ShapeDtypeStruct((seq, width), BF16)]
        + [jax.ShapeDtypeStruct((half, time_lanes), BF16)] * 2
        + [jax.ShapeDtypeStruct((half, weight_lanes), BF16)] * 2,
        compiler_params=limits(48),
        cost_estimate=pl.CostEstimate(
            flops=seq * width,
            bytes_accessed=seq * width,
            transcendentals=seq,
        ),
    )(core, *kept_out(*inputs, *shards, *extras, *constants))


def middle_kernel(
    tokens_ref, top_ref, bottom_ref, embed_ref, time_ref, bias_ref, gain_ref, shift_ref, residual_ref, second_ref
):
    width = gain_ref.shape[1]
    attended = jnp.concatenate([top_ref[...], bottom_ref[...]], axis=0)
    residual = tokens_ref[...].astype(F32) + attended
    residual_ref[...] = residual
    mod = product(embed_ref[...], time_ref[...]) + bias_ref[...]
    normed, _ = norm_parts(residual)
    base = normed * gain_ref[...] + shift_ref[...]
    second_ref[...] = (base * (1.0 + mod[:, :width]) + mod[:, width:]).astype(BF16)


def middle(tokens, top, bottom, embed, time_flat, bias, gain, shift):
    rows, width = tokens.shape
    inputs = (tokens, top, bottom, embed, time_flat, bias, gain, shift)
    shard = whole(rows, width)
    return pl.pallas_call(
        middle_kernel,
        grid=(1,),
        in_specs=[whole(*each.shape) for each in inputs[:4]]
        + [block_of((embed.shape[1], 2 * width), 0, 1), block_of((1, 2 * width), 0, 1)]
        + [whole(*each.shape) for each in inputs[6:]],
        out_specs=[shard, shard],
        out_shape=[pltpu.HBM((rows, width), F32), pltpu.HBM((rows, width), BF16)],
        compiler_params=limits(16),
    )(*kept_out(tokens), top, bottom, *kept_out(*inputs[3:]))


def middle_back_kernel(
    part_ref, other_ref, cotangent_ref, residual_ref, embed_ref, time_ref, bias_ref, gain_ref, shift_ref,
    residual_grad_ref, half_ref, scale_grad_ref, shift_grad_ref, small_ref,
):
    grads = part_ref[...] + other_ref[...]
    factor = 1.0 + product(embed_ref[...], time_ref[...]) + bias_ref[...]
    normed, scale = norm_parts(residual_ref[...])
    gain = gain_ref[...]
    base = normed * gain + shift_ref[...]
    weighted = grads * factor
    inner = weighted * gain
    back = scale * (
        inner
        - jnp.mean(inner, axis=-1, keepdims=True)
        - normed * jnp.mean(inner * normed, axis=-1, keepdims=True)
    )
    residual_grad = cotangent_ref[...].astype(F32) + back
    residual_grad_ref[...] = residual_grad
    half_ref[...] = residual_grad.astype(BF16)
    scale_grad = grads * base
    scale_grad_ref[...] = scale_grad.astype(BF16)
    shift_grad_ref[...] = grads.astype(BF16)
    small_ref[...] = jnp.concatenate(
        [
            jnp.sum(each, axis=0, keepdims=True)
            for each in (weighted * normed, weighted, scale_grad, grads)
        ],
        axis=0,
    )


def middle_back(part, other, cotangent, residual, embed, time_flat, bias, gain, shift):
    rows, width = cotangent.shape
    shard = whole(rows, width)
    inputs = (part, other, cotangent, residual, embed, time_flat, bias, gain, shift)
    return pl.pallas_call(
        middle_back_kernel,
        grid=(1,),
        in_specs=[whole(*each.shape) for each in inputs[:5]]
        + [block_of((embed.shape[1], width), 0, 2), block_of((1, width), 0, 2)]
        + [whole(*each.shape) for each in inputs[7:]],
        out_specs=[shard] * 4 + [whole(4, width)],
        out_shape=[
            pltpu.HBM((rows, width), F32),
            jax.ShapeDtypeStruct((rows, width), BF16),
            pltpu.HBM((rows, width), BF16),
            pltpu.HBM((rows, width), BF16),
            pltpu.HBM((4, width), F32),
        ],
        compiler_params=limits(20),
    )(part, other, *kept_out(*inputs[2:]))


def forward_kernel(
    place_ref, rows_ref, rows_other_ref, grads_ref, grads_other_ref, up_own_ref, down_own_ref, up_near_ref, down_near_ref,
    up_far_ref, down_far_ref,
    branch_ref, branch_other_ref, second_ref, second_other_ref, *grad_refs, planes,
):
    step = pl.program_id(0)
    mine = step == 0
    rows = jnp.concatenate([rows_ref[...], rows_other_ref[...]], axis=0)
    grads = jnp.concatenate([grads_ref[...], grads_other_ref[...]], axis=0)
    count = branch_ref.shape[0]
    far = step < 3
    up = jnp.where(mine, up_own_ref[...], jnp.where(far, up_far_ref[0], up_near_ref[...]))
    up = up.reshape(rows.shape[1], up.shape[2])
    packed = jnp.where(mine, down_own_ref[...], jnp.where(far, down_far_ref[0], down_near_ref[...]))
    half = packed.shape[1] // 2
    down = jnp.concatenate(
        [packed[:, :half].reshape(-1, packed.shape[2]), packed[:, half:].reshape(-1, packed.shape[2])],
        axis=1,
    )
    hidden = product(rows, up)
    active_grad = product(grads, down, TRAIL)
    tail = 0.5 * (1.0 + lax.erf(hidden * math.sqrt(0.5)))
    slope = tail + hidden * jnp.exp(hidden * hidden * -0.5) * (1.0 / math.sqrt(2.0 * math.pi))
    active = (hidden * tail).astype(BF16)
    hidden_grad = (active_grad * slope).astype(BF16)
    branch = product(active, down)
    second = product(hidden_grad, up, TRAIL)

    @pl.when(mine)
    def _():
        branch_ref[...] = branch[:count]
        branch_other_ref[...] = branch[count:]
        second_ref[...] = second[:count]
        second_other_ref[...] = second[count:]

    @pl.when(step > 0)
    def _():
        branch_ref[...] += branch[:count]
        branch_other_ref[...] += branch[count:]
        second_ref[...] += second[:count]
        second_other_ref[...] += second[count:]

    bits = planes.bit_length() - 1
    down_grad = product(active, grads, LEAD)
    up_grad = product(rows, hidden_grad, LEAD)
    grad_refs = list(grad_refs)
    for grad in (down_grad, up_grad):
        middle = grad.shape[1] // 2
        for bit, columns in ((0, grad[:, :middle]), (bits - 1, grad[:, middle:])):
            one = (place_ref[0] >> bit) & 1 == 1
            low = columns.shape[0] // planes << bit
            split = columns.astype(BF16).reshape(-1, 2, low, middle)
            kept_ref, sent_ref = grad_refs.pop(0), grad_refs.pop(0)
            kept_ref[...] = jnp.where(one, split[:, 1], split[:, 0]).reshape(kept_ref.shape)
            sent_ref[...] = jnp.where(one, split[:, 0], split[:, 1]).reshape(sent_ref.shape)


def feed_forward(place, rows, rows_other, grads, grads_other, own_weights, near, far, groups):
    tokens, width = rows.shape
    planes, piece_rows, hidden = own_weights.shape
    half = whole(tokens, width)
    block = (planes, piece_rows // 2, hidden)

    def side(i):
        return jnp.where(i > 1, 1, 0)

    grad_specs, grad_shapes = [], []
    for each_rows, columns in ((hidden // planes, width // 2), (width // planes, hidden // 2)):
        for _ in range(4):
            grad_specs.append(
                pl.BlockSpec((planes // 2, 1, each_rows, columns), lambda i, at: (0, i, 0, 0))
            )
            grad_shapes.append(pltpu.HBM((planes // 2, groups, each_rows, columns), BF16))
    return pl.pallas_call(
        functools.partial(forward_kernel, planes=planes),
        grid_spec=pltpu.PrefetchScalarGridSpec(
            num_scalar_prefetch=1,
            grid=(groups,),
            in_specs=[
                half,
                half,
                half,
                half,
                pl.BlockSpec(block, lambda i, _: (0, 0, 0)),
                pl.BlockSpec(block, lambda i, _: (0, 1, 0)),
                pl.BlockSpec(block, lambda i, _: (0, 0, 0)),
                pl.BlockSpec(block, lambda i, _: (0, 1, 0)),
                pl.BlockSpec((1, *block), lambda i, _: (side(i), 0, 0, 0)),
                pl.BlockSpec((1, *block), lambda i, _: (side(i), 0, 1, 0)),
            ],
            out_specs=[half] * 4 + grad_specs,
        ),
        out_shape=[pltpu.HBM((tokens, width), F32)] * 2
        + [jax.ShapeDtypeStruct((tokens, width), F32)] * 2
        + grad_shapes,
        compiler_params=limits(48),
        cost_estimate=pl.CostEstimate(
            flops=24 * tokens * width * groups * hidden,
            bytes_accessed=8 * width * groups * hidden,
            transcendentals=4 * tokens * groups * hidden,
        ),
    )(place, *kept_out(rows), rows_other, *kept_out(grads, grads_other, own_weights, own_weights, near, near, far, far))


def spread_kernel(core_ref, own_ref, other_ref, out_ref, *, blocks):
    mine = pl.program_id(0) // blocks == core_ref[0]
    width = out_ref.shape[2]
    for at in range(out_ref.shape[1]):
        columns = slice(at * width, (at + 1) * width)
        out_ref[:, at, :] = jnp.where(mine, own_ref[:, columns], other_ref[:, columns]).astype(F32)


def spread(core, own, other, shape, rows):
    blocks = own.shape[0] // rows
    half = pl.BlockSpec((rows, shape[1] * shape[2]), lambda i, _: (i % blocks, 0))
    return pl.pallas_call(
        functools.partial(spread_kernel, blocks=blocks),
        grid_spec=pltpu.PrefetchScalarGridSpec(
            num_scalar_prefetch=1,
            grid=(2 * blocks,),
            in_specs=[half, half],
            out_specs=pl.BlockSpec((rows, shape[1], shape[2]), lambda i, _: (i, 0, 0)),
        ),
        out_shape=jax.ShapeDtypeStruct(shape, F32),
        compiler_params=limits(16),
    )(core, own, other)


def unfold_kernel(core_ref, own_ref, other_ref, out_ref):
    mine = core_ref[0] == 0
    rows, width = own_ref.shape[0], out_ref.shape[2]
    for at in range(own_ref.shape[1] // width):
        columns = slice(at * width, (at + 1) * width)
        own, other = own_ref[:, columns], other_ref[:, columns]
        first = 2 * at * rows
        out_ref[0, first : first + rows] = jnp.where(mine, own, other).astype(F32)
        out_ref[0, first + rows : first + 2 * rows] = jnp.where(mine, other, own).astype(F32)


def unfold(core, own, other, shape):
    rows = own.shape[0]
    blocks = shape[1] // (2 * rows)
    half = pl.BlockSpec((rows, blocks * shape[2]), lambda i, _: (0, i))
    return pl.pallas_call(
        unfold_kernel,
        grid_spec=pltpu.PrefetchScalarGridSpec(
            num_scalar_prefetch=1,
            grid=(shape[0],),
            in_specs=[half, half],
            out_specs=pl.BlockSpec((1, *shape[1:]), lambda i, _: (i, 0, 0)),
        ),
        out_shape=jax.ShapeDtypeStruct(shape, F32),
        compiler_params=limits(16),
    )(core, own, other)


def unpack_kernel(pieces_ref, out_ref):
    out_ref[...] = pieces_ref[...].reshape(out_ref.shape).astype(F32)


def unpack(pieces, planes):
    count, rows, width = pieces.shape
    step = min(planes, 2)
    return pl.pallas_call(
        unpack_kernel,
        grid=(count // step,),
        in_specs=[pl.BlockSpec((step, rows, width), lambda i: (i, 0, 0))],
        out_specs=pl.BlockSpec(
            (step * rows, width), lambda i: (i % (planes // step), i // (planes // step))
        ),
        out_shape=jax.ShapeDtypeStruct((planes * rows, width * count // planes), F32),
        compiler_params=limits(16),
    )(pieces)


def swap(values, axis_name, bit):
    size = lax.axis_size(axis_name)
    return lax.ppermute(values, axis_name, [(at, at ^ (1 << bit)) for at in range(size)])


def bit_of(axis_name, bit):
    return (lax.axis_index(axis_name) >> bit) & 1


def after(values, *others):
    return lax.optimization_barrier((values, others))[0]


def exchange(values, axis_name, bit, dim):
    own = bit_of(axis_name, bit)
    kept = lax.dynamic_index_in_dim(values, own, dim, keepdims=False)
    sent = lax.dynamic_index_in_dim(values, 1 - own, dim, keepdims=False)
    return (kept, swap(sent, axis_name, bit))


def total(kept, got):
    return (kept.astype(F32) + got.astype(F32)).astype(BF16)


def double(values, axis_name, bit, dim):
    own = bit_of(axis_name, bit) == 0
    got = swap(values, axis_name, bit)
    return jnp.stack([jnp.where(own, values, got), jnp.where(own, got, values)], axis=dim)


class PlaneScatter:
    def __init__(self, arrays, orders, dim):
        bits = len(orders[0])
        self.dim = dim
        self.arrays = [
            each.reshape(each.shape[:dim] + (2,) * bits + each.shape[dim + 1 :]) for each in arrays
        ]
        self.orders = [list(order) for order in orders]
        self.left = [list(range(bits - 1, -1, -1)) for _ in orders]

    @classmethod
    def started(cls, kept, sent, orders, dim):
        self = cls.__new__(cls)
        bits = len(orders[0])
        self.dim = dim
        self.orders = [list(order[1:]) for order in orders]
        self.left = [[bit for bit in range(bits - 1, -1, -1) if bit != order[0]] for order in orders]
        self.kept = [
            each.reshape(each.shape[:dim] + (2,) * (bits - 1) + each.shape[dim + 1 :]) for each in kept
        ]
        self.got = [
            swap(each, "plane", order[0]).reshape(like.shape)
            for each, like, order in zip(sent, self.kept, orders)
        ]
        return self

    def send(self):
        self.kept, self.got = [], []
        for values, order, left in zip(self.arrays, self.orders, self.left):
            bit = order.pop(0)
            kept, got = exchange(values, "plane", bit, self.dim + left.index(bit))
            left.remove(bit)
            self.kept.append(kept)
            self.got.append(got)
        self.meet()

    def meet(self, *others):
        self.got, others = lax.optimization_barrier((self.got, others))
        return others

    def add(self):
        self.arrays = [total(kept, got) for kept, got in zip(self.kept, self.got)]

    def finish(self):
        while self.orders[0]:
            self.send()
            self.add()
        return self.arrays


class PlaneGather:
    def __init__(self, arrays, orders):
        self.arrays = list(arrays)
        self.orders = [list(order) for order in orders]
        self.left = [[] for _ in orders]

    def send(self):
        self.bits = [order.pop() for order in self.orders]
        self.got = [swap(values, "plane", bit) for values, bit in zip(self.arrays, self.bits)]

    def join(self):
        for at, bit in enumerate(self.bits):
            self.left[at] = sorted(self.left[at] + [bit], reverse=True)
            own = bit_of("plane", bit) == 0
            values, got = self.arrays[at], self.got[at]
            pair = (jnp.where(own, values, got), jnp.where(own, got, values))
            self.arrays[at] = jnp.stack(pair, axis=self.left[at].index(bit))

    def finish(self):
        while self.orders[0]:
            self.send()
            self.arrays, self.got = lax.optimization_barrier((self.arrays, self.got))
            self.join()
        return self.arrays


def ring_gather(shard, meanwhile=None):
    size = lax.axis_size("tensor")
    half = shard.shape[0] // 2
    right, left = [shard[:half]], [shard[half:]]
    for step in range(1, size):
        others = () if meanwhile is None else meanwhile(step, right, left)
        right.append(lax.ppermute(right[-1], "tensor", [(at, (at + 1) % size) for at in range(size)]))
        left.append(lax.ppermute(left[-1], "tensor", [(at, (at - 1) % size) for at in range(size)]))
        right[-1], left[-1], others = lax.optimization_barrier((right[-1], left[-1], others))
        if meanwhile is not None:
            meanwhile(-step, others, None)
    return [(right[(size - at) % size], left[at]) for at in range(size)]


class RingScatter:
    def __init__(self, chunks):
        self.chunks = chunks
        self.size = len(chunks)
        self.half = chunks[0].shape[0] // 2
        self.step = 0
        self.right = chunks[-1][: self.half]
        self.left = chunks[1][self.half :]

    def send(self):
        size = self.size
        right = lax.ppermute(self.right, "tensor", [(at, (at + 1) % size) for at in range(size)])
        left = lax.ppermute(self.left, "tensor", [(at, (at - 1) % size) for at in range(size)])
        self.got = lax.optimization_barrier((right, left))

    def add(self):
        self.step += 1
        right, left = self.got
        self.right = right.astype(F32) + self.chunks[self.size - 1 - self.step][: self.half].astype(F32)
        self.left = left.astype(F32) + self.chunks[(self.step + 1) % self.size][self.half :].astype(F32)
        if self.step < self.size - 1:
            self.right, self.left = self.right.astype(BF16), self.left.astype(BF16)

    def finish(self):
        while self.step < self.size - 1:
            self.send()
            self.add()
        return (self.right, self.left)


def own_first(values, dim):
    size = lax.axis_size("tensor")
    stretch = values.shape[dim] // size
    doubled = jnp.concatenate([values, values], axis=dim)
    return lax.dynamic_slice_in_dim(
        doubled, lax.axis_index("tensor") * stretch, values.shape[dim], dim
    )


def local(
    tokens,
    time_embed,
    segment_ids,
    positions,
    first_gain,
    first_bias,
    second_gain,
    second_bias,
    time_weight,
    time_bias,
    qkv_weight,
    out_weight,
    up_weight,
    down_weight,
    cotangent,
):
    local_rows, width = tokens.shape
    embed_width = time_embed.shape[1]
    local_width = qkv_weight.shape[2]
    hidden_local = up_weight.shape[1]
    half_hidden = hidden_local // 2
    planes = lax.axis_size("plane")
    groups = lax.axis_size("tensor")
    plane_at = lax.axis_index("plane")
    core_at = lax.axis_index("core")
    place = plane_at.astype(jnp.int32).reshape(1)
    arrival = sorted(range(groups), key=lambda at: max(at, groups - at) if at else 0)
    rising = list(range(planes.bit_length() - 1))
    falling = rising[::-1]

    up_rows = width // planes
    up_piece = lax.dynamic_slice(
        up_weight, (plane_at * up_rows, core_at * half_hidden), (up_rows, half_hidden)
    )
    down_rows = half_hidden // planes
    down_piece = lax.dynamic_slice(
        down_weight, (core_at * half_hidden + plane_at * down_rows, 0), (down_rows, width)
    )
    piece = jnp.concatenate([up_piece, down_piece[:, :half_hidden], down_piece[:, half_hidden:]], axis=0)
    ahead = [(at, (at + 1) % groups) for at in range(groups)]
    behind = [(at, (at - 1) % groups) for at in range(groups)]
    up_half = lax.dynamic_slice_in_dim(up_weight, core_at * half_hidden, half_hidden, 1)
    down_half = lax.dynamic_slice_in_dim(down_weight, core_at * half_hidden, half_hidden, 0)
    down_half = down_half.reshape(planes, down_rows, width)
    own_pieces = jnp.concatenate(
        [
            up_half.reshape(planes, up_rows, half_hidden),
            down_half[..., :half_hidden],
            down_half[..., half_hidden:],
        ],
        axis=1,
    )

    held = {
        "time": time_weight.reshape(embed_width, 4 * width),
        "tables": rotary_tables(own_first(positions, 1).reshape(-1), 2 * HEAD),
        "pieces": own_pieces,
        "cotangent": swap(cotangent, "core", 0),
        "near": lax.ppermute(piece, "tensor", ahead),
    }
    bias_flat = time_bias.reshape(1, 4 * width)
    first_gain, first_bias = first_gain.reshape(1, width), first_bias.reshape(1, width)
    second_gain, second_bias = second_gain.reshape(1, width), second_bias.reshape(1, width)
    qkv_planes = jnp.transpose(qkv_weight, (1, 0, 2))
    segments = own_first(segment_ids, 1)
    columns = segments.reshape(-1, 1)

    def enter(places, halves, row):
        return entry(
            halves, held["tables"], held["time"], bias_flat, first_gain, first_bias, qkv_planes, places, groups, row
        )

    def meanwhile(step, right, left):
        if step == 1:
            return held
        if step == -1:
            held.update(right)
        elif step == 2:
            return enter([0], (right[0], left[0]), ())
        elif step > 2 and 2 * (step - 1) == groups:
            return enter([step - 1], (right[step - 1], left[step - 1]), held["row"])
        elif step > 0:
            return held["row"]
        else:
            held["row"] = right
        return None

    gathered = ring_gather(jnp.concatenate([tokens, time_embed], axis=1), meanwhile)
    near = lax.all_gather(held["near"], "plane", axis=0)
    piece, passed = after((piece, held["near"]), gathered[arrival[-1]])
    far = [lax.ppermute(piece, "tensor", behind), lax.ppermute(passed, "tensor", ahead)]
    row = held["row"]
    for first in range(2, len(arrival), 2):
        places = arrival[first : first + 2]
        row = enter(places, [half for at in places for half in gathered[at]], row)
    tables, time_flat = held["tables"], held["time"]
    tokens_all, first_all, queries, keys, values = row
    keys, far, near = lax.optimization_barrier((keys, far, near))
    far = lax.all_gather(jnp.stack(far), "plane", axis=1)
    mixed, logsums, parts = {}, {}, {}
    for at in list(range(groups - 1, -1, -1)):
        mixed[at], logsums[at], parts[at] = attend(
            queries, keys, values, segments, columns, out_weight, at, local_rows
        )
    attended = RingScatter([parts[at] for at in range(groups)]).finish()

    residual, second_normed = middle(
        tokens, *attended, time_embed, time_flat, bias_flat, second_gain, second_bias
    )
    branch_own, branch_other, second_own, second_other, *grad_parts = feed_forward(
        place,
        second_normed,
        swap(second_normed, "core", 0),
        cotangent,
        held["cotangent"],
        held["pieces"],
        near.reshape(planes, 2 * up_rows, half_hidden),
        far,
        groups,
    )
    second_other = swap(second_other, "core", 0)

    sums = {"down": PlaneScatter.started(grad_parts[:4:2], grad_parts[1:4:2], [rising, falling], 0)}
    branch = branch_own + swap(branch_other, "core", 0)
    result = (residual + branch).astype(BF16)

    residual_grad, attended_own, scale_two_grad, shift_two_grad, small_two = middle_back(
        second_own,
        second_other,
        cotangent,
        residual,
        time_embed,
        time_flat,
        bias_flat,
        second_gain,
        second_bias,
    )
    def turn(places, halves):
        return attend_back(
            halves,
            queries,
            keys,
            values,
            [logsums[at] for at in places],
            segments,
            columns,
            out_weight,
            tables,
            places,
        )

    back = {}

    def meanwhile_back(step, right, left):
        if step == 2:
            return (turn([0], (right[0], left[0])), sums["down"].got)
        elif step == -2:
            back[(0,)], sums["down"].got = right
            sums["down"].add()
            if sums["down"].orders[0]:
                sums["down"].send()
            up_parts = after(grad_parts[4:], sums["down"].arrays)
            sums["up"] = PlaneScatter.started(up_parts[::2], up_parts[1::2], [rising, falling], 0)
        elif step == 3:
            return turn([2], (right[2], left[2]))
        elif step == -3:
            back[(2,)] = right
        return ()

    def to_tensor(arrays):
        parts = [jnp.concatenate([each[at] for each in arrays], axis=-1) for at in range(groups)]
        received = [
            lax.ppermute(parts[hop], "tensor", [(at, (at + hop) % groups) for at in range(groups)])
            for hop in range(1, groups)
        ]
        return (parts[0], received)

    def joined(own_part, received):
        return sum(each.astype(F32) for each in [own_part, *received]).astype(BF16)

    attended_halves = ring_gather(attended_own, meanwhile_back)
    places = (1, 3)
    back[places] = turn(places, [half for at in places for half in attended_halves[at]])
    back[places], sums["down"].got = sums["up"].meet(back[places], sums["down"].got)
    sums["down"].add()
    down_own, down_received = to_tensor(sums["down"].finish())
    sums["up"].add()
    if sums["up"].orders[0]:
        sums["up"].send()
    query_shards = {at: (parts[0], which) for places, parts in back.items() for which, at in enumerate(places)}
    received = [
        lax.ppermute(parts[hop], "tensor", [(at, (at + hop) % groups) for at in range(groups)])
        for hop in range(1, groups)
    ]
    core_own = core_at.astype(jnp.int32).reshape(1)
    left = leave(
        core_own,
        [query_shards[at] for at in range(groups)],
        [parts[1] for parts in back.values()],
        [parts[2] for parts in back.values()],
        [mixed[at] for at in range(groups)],
        attended_halves,
        tables,
        tokens_all,
        first_all,
        (scale_two_grad, shift_two_grad, small_two),
        time_embed,
        time_flat,
        bias_flat,
        first_gain,
        first_bias,
        qkv_planes,
        local_rows,
    )
    left, down_received = sums["up"].meet(left, down_received)
    sums["up"].add()
    up_own, up_received = to_tensor(sums["up"].finish())
    down_all = lax.all_gather(joined(down_own, down_received), ("core", "plane"), axis=0, tiled=True)
    first_half, time_kept, time_sent, weight_kept, weight_sent = left

    time_got, weight_got = swap(time_sent, "core", 0), swap(weight_sent, "core", 0)

    def by_plane(pack):
        return pack.reshape(planes, embed_width // (2 * planes), -1)

    pack_sums = PlaneScatter(
        [by_plane(total(time_kept, time_got)), by_plane(total(weight_kept, weight_got))], [rising, falling], 0
    )
    ring = RingScatter([first_half[at * local_rows : (at + 1) * local_rows] for at in range(groups)])
    pack_sums.send()
    pack_sums.add()
    ring.send()
    second = bool(pack_sums.orders[0])
    if second:
        pack_sums.send()
    (ring.got, up_received) = pack_sums.meet(ring.got, up_received)
    if second:
        pack_sums.add()
    time_own, weight_own = pack_sums.finish()
    ring.add()
    up_all = lax.all_gather(joined(up_own, up_received), ("core", "plane"), axis=0)
    time_got = swap(time_own, "tensor", 0)
    time_got, down_all = lax.optimization_barrier((time_got, down_all))
    down_summed = down_all.astype(F32)
    time_own = total(time_own, time_got)
    time_got = swap(time_own, "tensor", 1)
    time_got, down_summed = lax.optimization_barrier((time_got, down_summed))
    time_sum = total(time_own, time_got)
    (ring.right, ring.left), time_sum = lax.optimization_barrier(((ring.right, ring.left), time_sum))
    gather = PlaneGather([time_sum, weight_own], [rising, falling])
    ring.send()
    gather.send()
    ring.got, gather.got, up_all = lax.optimization_barrier((ring.got, gather.got, up_all))
    gather.join()
    ring.add()
    ring.send()
    (up_all,) = kept_out(up_all)
    up_summed = unpack(up_all, planes)
    if gather.orders[0]:
        gather.send()
        ring.got, gather.got, up_summed = lax.optimization_barrier((ring.got, gather.got, up_summed))
        gather.join()
    ring.add()
    time_half, weight_half = gather.finish()
    packs = [time_half.reshape(embed_width // 2, -1), weight_half.reshape(embed_width // 2, -1)]
    (time_half, time_other), (weight_half, weight_other) = ((pack, swap(pack, "core", 0)) for pack in packs)
    first_grad = ring.finish()
    time_weight_grad = spread(
        core_own, time_half, time_other, (embed_width, 4, width), min(64, embed_width // 2)
    )
    qkv_lanes = 3 * local_width * width // embed_width
    qkv_summed = jnp.transpose(
        unfold(core_own, weight_half, weight_other, (3, width, local_width)), (1, 0, 2)
    )

    def both_cores(own_half, other_half):
        mine = core_at == 0
        halves = [jnp.where(mine, own_half, other_half), jnp.where(mine, other_half, own_half)]
        return jnp.concatenate(halves, axis=0).astype(F32)

    out_summed = both_cores(weight_half[:, qkv_lanes:], weight_other[:, qkv_lanes:])
    small = both_cores(time_half[:, 4 * width :], time_other[:, 4 * width :])[: width // 16]
    small = jnp.transpose(small.reshape(width // 128, 8, 128), (1, 0, 2)).reshape(8, width)

    own_normed, own_scale = norm_parts(tokens.astype(F32))
    mod_own = product(time_embed, time_flat[:, :width]) + bias_flat[:, :width]
    first_grad = jnp.concatenate(first_grad, axis=0)
    input_grad = residual_grad + norm_input_back(first_grad, own_normed, own_scale, first_gain, mod_own)
    return (
        result,
        input_grad,
        small[0],
        small[1],
        small[4],
        small[5],
        time_weight_grad,
        jnp.concatenate([small[2:4], small[6:]], axis=0),
        qkv_summed,
        out_summed,
        up_summed,
        down_summed,
    )


def solution(mesh):
    whole, tensor = mesh.devices.shape
    finer = Mesh(mesh.devices.reshape(whole // 2, 2, tensor), ("plane", "core", "tensor"))
    rows = P(("plane", "core", "tensor"), None)
    group = P(("plane", "core"), None)
    return jax.shard_map(
        local,
        mesh=finer,
        in_specs=(
            rows,
            rows,
            group,
            group,
            P(),
            P(),
            P(),
            P(),
            P(),
            P(),
            P(None, None, "tensor"),
            P("tensor", None),
            P(None, "tensor"),
            P("tensor", None),
            rows,
        ),
        out_specs=(
            rows,
            rows,
            P(),
            P(),
            P(),
            P(),
            P(),
            P(),
            P(None, None, "tensor"),
            P("tensor", None),
            P(None, "tensor"),
            P("tensor", None),
        ),
        check_vma=False,
    )
```

```python
import functools
import math

import jax
import jax.numpy as jnp
from jax import lax
from jax.experimental import pallas as pl
from jax.experimental.pallas import tpu as pltpu
from jax.sharding import Mesh
from jax.sharding import PartitionSpec as P

HEAD = 64
F32 = jnp.float32
BF16 = jnp.bfloat16
LEAD = (((0,), (0,)), ((), ()))
TRAIL = (((1,), (1,)), ((), ()))


def product(left, right, dims=(((1,), (0,)), ((), ()))):
    return lax.dot_general(left, right, dims, preferred_element_type=F32)


def norm_parts(values):
    centre = values - jnp.mean(values, axis=-1, keepdims=True)
    spread = jnp.mean(centre * centre, axis=-1, keepdims=True)
    scale = lax.rsqrt(spread + 1e-05)
    return (centre * scale, scale)


def norm_input_back(grads, normed, scale, gain, mod_scale):
    inner = grads * (1.0 + mod_scale) * gain
    return scale * (
        inner
        - jnp.mean(inner, axis=-1, keepdims=True)
        - normed * jnp.mean(inner * normed, axis=-1, keepdims=True)
    )


def rotary_tables(places, lanes):
    half_size = HEAD // 2
    lane = jnp.arange(lanes)
    frequency = jnp.exp((lane % half_size).astype(F32) * (-math.log(10000.0) / half_size))
    angles = places.astype(F32)[:, None] * frequency[None, :]
    sign = jnp.where(lane % HEAD < half_size, -1.0, 1.0)
    return (jnp.cos(angles), jnp.sin(angles) * sign[None, :])


def kept_out(*arrays):
    return tuple(pltpu.with_memory_space_constraint(each, pltpu.HBM) for each in arrays)


def block_of(shape, *place):
    return pl.BlockSpec(shape, lambda *_: place)


def whole(*shape):
    return pl.BlockSpec(shape, lambda *_: (0,) * len(shape))


def limits(megabytes):
    return pltpu.CompilerParams(vmem_limit_bytes=megabytes << 20)


def partner(values):
    lanes = values.shape[1]
    lane = lax.broadcasted_iota(jnp.int32, values.shape, 1)
    above = pltpu.roll(values, lanes - HEAD // 2, 1)
    below = pltpu.roll(values, HEAD // 2, 1)
    return jnp.where(lane % HEAD < HEAD // 2, above, below)


def widened(table, lanes):
    return jnp.concatenate([table] * (lanes // table.shape[1]), axis=1)


def turned(values, cosine, sine):
    return values * widened(cosine, values.shape[1]) + partner(values) * widened(sine, values.shape[1])


def entry_kernel(
    *refs, count
):
    halves, refs = refs[: 2 * count], refs[2 * count :]
    cosine_ref, sine_ref, time_ref, bias_ref, gain_ref, shift_ref, weight_ref = refs[:7]
    tokens_ref, first_ref, query_ref, key_ref, value_ref = refs[-5:]
    rows = jnp.concatenate([halves[0][...], halves[1][...]], axis=0)
    for at in range(1, count):
        other = jnp.concatenate([halves[2 * at][...], halves[2 * at + 1][...]], axis=0)
        rows = jnp.where(pl.program_id(0) == at, other, rows)
    tokens_ref[...] = rows
    width = gain_ref.shape[1]
    mod = product(rows[:, width:], time_ref[...]) + bias_ref[...]
    normed, _ = norm_parts(rows[:, :width].astype(F32))
    base = normed * gain_ref[...] + shift_ref[...]
    first = (base * (1.0 + mod[:, :width]) + mod[:, width:]).astype(BF16)
    first_ref[...] = first
    cosine, sine = cosine_ref[...], sine_ref[...]
    query_ref[...] = turned(product(first, weight_ref[0]), cosine, sine).astype(BF16)
    key_ref[...] = turned(product(first, weight_ref[1]), cosine, sine).astype(BF16)
    value_ref[...] = product(first, weight_ref[2]).astype(BF16)


def entry(halves, tables, time_flat, bias, gain, shift, weight, places, groups, before):
    half, both = halves[0].shape
    count = len(places)
    apart = places[-1] - places[0]
    rows = 2 * half
    width = gain.shape[1]
    part = weight.shape[2]
    lanes = tables[0].shape[1]
    widths = (both, width, part, part, part)
    table = pl.BlockSpec((rows, lanes), lambda i: (places[0] + i * apart, 0))
    inputs = (*halves, *kept_out(*tables, time_flat, bias, gain, shift, weight))
    return pl.pallas_call(
        functools.partial(entry_kernel, count=count),
        grid=(count,),
        in_specs=[whole(half, both)] * (2 * count)
        + [table, table]
        + [block_of((both - width, 2 * width), 0, 0), block_of((1, 2 * width), 0, 0)]
        + [whole(*each.shape) for each in (gain, shift, weight)]
        + [pl.BlockSpec(memory_space=pl.ANY)] * len(before),
        out_specs=[pl.BlockSpec((rows, each), lambda i: (places[0] + i * apart, 0)) for each in widths],
        out_shape=[pltpu.HBM((rows * groups, each), BF16) for each in widths],
        input_output_aliases={len(inputs) + at: at for at in range(len(before))},
        compiler_params=limits(16),
        cost_estimate=pl.CostEstimate(
            flops=2 * rows * width * 4 * part + 4 * rows * width * (both - width),
            bytes_accessed=8 * rows * width + 6 * width * part,
            transcendentals=rows,
        ),
    )(*inputs, *kept_out(*before))


def pair_lanes(values, pair):
    return values[:, pair * 2 * HEAD : (pair + 1) * 2 * HEAD]


def apart(values, pair):
    values = pair_lanes(values, pair)
    lane = lax.broadcasted_iota(jnp.int32, values.shape, 1)
    zeros = jnp.zeros_like(values)
    return jnp.concatenate(
        [jnp.where(lane < HEAD, values, zeros), jnp.where(lane < HEAD, zeros, values)], axis=0
    )


def together(values):
    rows = values.shape[0] // 2
    lane = lax.broadcasted_iota(jnp.int32, (rows, values.shape[1]), 1)
    return jnp.where(lane < HEAD, values[:rows], values[rows:])


def attend_kernel(query_ref, key_ref, value_ref, own_ref, all_ref, out_ref, mixed_ref, logsum_ref, part_ref):
    queries, keys, values = query_ref[...], key_ref[...], value_ref[...]
    own = own_ref[...]
    allowed = all_ref[...] == jnp.concatenate([own, own], axis=1)
    scale = 1.0 / math.sqrt(HEAD)
    rows = queries.shape[0]
    pairs = []
    for pair in range(queries.shape[1] // (2 * HEAD)):
        scores = product(pair_lanes(keys, pair), apart(queries, pair), TRAIL) * scale
        scores = jnp.where(allowed, scores, -1e30)
        peak = jnp.max(scores, axis=0, keepdims=True)
        raised = jnp.exp(scores - peak)
        total_raised = jnp.sum(raised, axis=0, keepdims=True)
        attention = (raised / total_raised).astype(BF16)
        logsum = peak + jnp.log(total_raised)
        logsum_ref[2 * pair : 2 * pair + 1, :] = logsum[:, :rows]
        logsum_ref[2 * pair + 1 : 2 * pair + 2, :] = logsum[:, rows:]
        pairs.append(together(product(attention, pair_lanes(values, pair), LEAD)))
    mixed = jnp.concatenate(pairs, axis=1).astype(BF16)
    mixed_ref[...] = mixed
    part_ref[...] = product(mixed, out_ref[...]).astype(BF16)


def attend(queries, keys, values, own_segments, all_segments, out_weight, place, rows):
    seq, part = keys.shape
    width = out_weight.shape[1]
    heads = part // HEAD
    return pl.pallas_call(
        attend_kernel,
        grid=(1,),
        in_specs=[
            pl.BlockSpec((rows, part), lambda i: (place, 0)),
            whole(seq, part),
            whole(seq, part),
            pl.BlockSpec((1, rows), lambda i: (0, place)),
            whole(seq, 1),
            whole(part, width),
        ],
        out_specs=[whole(rows, part), whole(heads, rows), whole(rows, width)],
        out_shape=[
            pltpu.HBM((rows, part), BF16),
            pltpu.HBM((heads, rows), F32),
            jax.ShapeDtypeStruct((rows, width), BF16),
        ],
        compiler_params=limits(28),
        cost_estimate=pl.CostEstimate(
            flops=4 * rows * seq * part + 2 * rows * part * width,
            bytes_accessed=4 * seq * part + 4 * rows * width,
            transcendentals=rows * seq * heads,
        ),
    )(queries, keys, values, own_segments, all_segments, out_weight)


def attend_back_kernel(
    query_ref, key_ref, value_ref, own_ref, all_ref, out_ref, cosine_ref, sine_ref, *refs, count
):
    halves, logsum_refs, (grad_ref, key_grad_ref, value_grad_ref) = (
        refs[: 2 * count],
        refs[2 * count : 3 * count],
        refs[3 * count :],
    )
    step = pl.program_id(0)
    queries, keys, values = query_ref[...], key_ref[...], value_ref[...]
    incoming = jnp.concatenate([halves[0][...], halves[1][...]], axis=0)
    logsums = logsum_refs[0][...]
    for at in range(1, count):
        other = jnp.concatenate([halves[2 * at][...], halves[2 * at + 1][...]], axis=0)
        incoming = jnp.where(step == at, other, incoming)
        logsums = jnp.where(step == at, logsum_refs[at][...], logsums)
    mixed_grad = product(incoming, out_ref[...], TRAIL).astype(BF16)
    own = own_ref[...]
    allowed = all_ref[...] == jnp.concatenate([own, own], axis=1)
    scale = 1.0 / math.sqrt(HEAD)
    query_pairs, key_pairs, value_pairs = [], [], []
    for pair in range(queries.shape[1] // (2 * HEAD)):
        query, grad = apart(queries, pair), apart(mixed_grad, pair)
        scores = product(pair_lanes(keys, pair), query, TRAIL) * scale
        scores = jnp.where(allowed, scores, -1e30)
        logsum = jnp.concatenate(
            [logsums[2 * pair : 2 * pair + 1], logsums[2 * pair + 1 : 2 * pair + 2]], axis=1
        )
        probability = jnp.exp(scores - logsum)
        prob_grad = product(pair_lanes(values, pair), grad, TRAIL)
        row_dot = jnp.sum(probability * prob_grad, axis=0, keepdims=True)
        score_grad = (probability * (prob_grad - row_dot)).astype(BF16)
        value_pairs.append(product(probability.astype(BF16), grad))
        key_pairs.append(product(score_grad, query))
        query_pairs.append(together(product(score_grad, pair_lanes(keys, pair), LEAD)))
    query_grad = jnp.concatenate(query_pairs, axis=1) * scale
    key_grad = jnp.concatenate(key_pairs, axis=1) * scale
    value_grad = jnp.concatenate(value_pairs, axis=1)
    grad_ref[...] = turned(query_grad, cosine_ref[...], -sine_ref[...]).astype(BF16)

    @pl.when(step == 0)
    def _():
        key_grad_ref[...] = key_grad
        value_grad_ref[...] = value_grad

    @pl.when(step > 0)
    def _():
        key_grad_ref[...] += key_grad
        value_grad_ref[...] += value_grad


def attend_back(halves, queries, keys, values, logsums, own_segments, all_segments, out_weight, tables, places):
    seq, part = keys.shape
    heads, rows = logsums[0].shape
    width = out_weight.shape[1]
    count = len(places)
    apart = places[-1] - places[0]
    shard = pl.BlockSpec((rows, part), lambda i: (places[0] + i * apart, 0))
    table = pl.BlockSpec((rows, tables[0].shape[1]), lambda i: (places[0] + i * apart, 0))
    constants = (own_segments, all_segments, out_weight, *tables)
    return pl.pallas_call(
        functools.partial(attend_back_kernel, count=count),
        grid=(count,),
        in_specs=[
            shard,
            whole(seq, part),
            whole(seq, part),
            pl.BlockSpec((1, rows), lambda i: (0, places[0] + i * apart)),
            whole(seq, 1),
            whole(part, width),
            table,
            table,
        ]
        + [whole(rows // 2, width)] * (2 * count)
        + [whole(heads, rows)] * count,
        out_specs=[
            pl.BlockSpec((rows, part), lambda i: (i, 0)),
            whole(seq, part),
            whole(seq, part),
        ],
        out_shape=[
            pltpu.HBM((count * rows, part), BF16),
            pltpu.HBM((seq, part), F32),
            pltpu.HBM((seq, part), F32),
        ],
        compiler_params=limits(44),
        cost_estimate=pl.CostEstimate(
            flops=10 * count * rows * seq * part + 2 * count * rows * part * width,
            bytes_accessed=16 * seq * part,
            transcendentals=count * rows * seq * heads,
        ),
    )(queries, keys, values, *kept_out(*constants), *halves, *kept_out(*logsums))


def exit_kernel(
    place_ref, cosine_ref, sine_ref, tokens_ref, first_ref, *refs, groups, calls
):
    shards = list(refs[:-18])
    lengths = (groups, calls, calls, groups, groups, groups)
    query_refs, key_refs, value_refs, mixed_refs, top_refs, bottom_refs = (
        [shards.pop(0) for _ in range(length)] for length in lengths
    )
    (
        scale_two_ref, shift_two_ref, small_two_ref, own_embed_ref, time_ref, bias_ref, gain_ref, shift_ref, weight_ref,
        first_grad_ref, time_kept_ref, time_sent_ref, weight_kept_ref, weight_sent_ref,
        weight_sum, time_sum, small_sum, out_sum,
    ) = refs[-18:]
    step = pl.program_id(0)
    width = gain_ref.shape[1]
    key_grad = sum(ref[...] for ref in key_refs)
    key_grad = turned(key_grad, cosine_ref[...], -sine_ref[...]).astype(BF16)

    def this(refs):
        values = refs[0][...]
        for at in range(1, len(refs)):
            values = jnp.where(step == at, refs[at][...], values)
        return values

    incoming = jnp.concatenate([this(top_refs), this(bottom_refs)], axis=0)
    out_part = product(this(mixed_refs), incoming, LEAD)
    grads = (this(query_refs), key_grad, sum(ref[...] for ref in value_refs).astype(BF16))
    first_grad = sum(product(grad, weight_ref[at], TRAIL) for at, grad in enumerate(grads))
    first_half = first_grad.astype(BF16)
    first_grad_ref[...] = first_half
    first = first_ref[...]
    weight_parts = [product(first, grad, LEAD) for grad in grads]
    rows = tokens_ref[...]
    embed = rows[:, width:]
    factor = 1.0 + product(embed, time_ref[...]) + bias_ref[...]
    normed, _ = norm_parts(rows[:, :width].astype(F32))
    base = normed * gain_ref[...] + shift_ref[...]
    scale_grad = first_grad * base
    weighted = first_grad * factor
    both = jnp.concatenate([scale_grad.astype(BF16), first_half], axis=1)
    time_part = product(embed, both, LEAD)
    small = jnp.concatenate(
        [
            jnp.sum(each, axis=0, keepdims=True)
            for each in (weighted * normed, weighted, scale_grad, first_grad)
        ],
        axis=0,
    )

    @pl.when(step == 0)
    def _():
        for at, part in enumerate(weight_parts):
            weight_sum[at] = part
        time_sum[...] = time_part
        out_sum[...] = out_part
        small_sum[:4] = small
        small_sum[4:] = small_two_ref[...]

    @pl.when(step > 0)
    def _():
        for at, part in enumerate(weight_parts):
            weight_sum[at] += part
        time_sum[...] += time_part
        out_sum[...] += out_part
        small_sum[:4] += small

    @pl.when(step == pl.num_programs(0) - 1)
    def _():
        one = place_ref[0] == 1
        half = time_kept_ref.shape[0]

        def put(kept_ref, sent_ref, at, values):
            values = values.astype(BF16)
            columns = slice(at, at + values.shape[1])
            kept_ref[:, columns] = jnp.where(one, values[half:], values[:half])
            sent_ref[:, columns] = jnp.where(one, values[:half], values[half:])

        put(time_kept_ref, time_sent_ref, 0, time_sum[...])
        own_embed = own_embed_ref[...]
        put(time_kept_ref, time_sent_ref, 2 * width, product(own_embed, scale_two_ref[...], LEAD))
        put(time_kept_ref, time_sent_ref, 3 * width, product(own_embed, shift_two_ref[...], LEAD))
        smalls = small_sum[...]
        smalls = jnp.concatenate(
            [smalls[:, at : at + 128] for at in range(0, width, 128)]
            + [jnp.zeros((2 * half - width // 16, 128), F32)],
            axis=0,
        )
        put(time_kept_ref, time_sent_ref, 4 * width, smalls)
        part = weight_sum.shape[2]
        for at in range(3):
            for row in range(0, width, 2 * half):
                column = (at * width + row) // (2 * half) * part
                put(weight_kept_ref, weight_sent_ref, column, weight_sum[at, row : row + 2 * half])
        put(weight_kept_ref, weight_sent_ref, 3 * part * width // (2 * half), out_sum[...])


def leave(
    core, queries, keys, values, mixed, halves, tables, tokens_all, first_all, second_grads, own_embed, time_flat, bias, gain, shift, weight, rows
):
    seq, both = tokens_all.shape
    part = weight.shape[2]
    width = gain.shape[1]
    embed = both - width
    half = embed // 2
    time_lanes = 4 * width + 128
    weight_lanes = 3 * part * width // embed + width

    def shard(lanes):
        return pl.BlockSpec((rows, lanes), lambda i, _: (i, 0))

    inputs = (*tables, tokens_all, first_all)
    extras = (*second_grads, own_embed)
    constants = (time_flat, bias, gain, shift, weight)
    groups = seq // rows
    picked = [pl.BlockSpec((rows, part), lambda i, _, at=at: (at, 0)) for _, at in queries]
    shards = [each for each, _ in queries] + [*keys, *values, *mixed]
    shards += [pair[0] for pair in halves] + [pair[1] for pair in halves]
    shard_specs = picked + [shard(part)] * (len(keys) + len(values)) + [whole(rows, part)] * groups
    shard_specs += [whole(rows // 2, width)] * (2 * groups)
    return pl.pallas_call(
        functools.partial(exit_kernel, groups=groups, calls=len(keys)),
        grid_spec=pltpu.PrefetchScalarGridSpec(
            num_scalar_prefetch=1,
            grid=(seq // rows,),
            in_specs=[shard(each.shape[1]) for each in inputs]
            + shard_specs
            + [whole(*each.shape) for each in extras]
            + [block_of((embed, width), 0, 0), block_of((1, width), 0, 0)]
            + [whole(*each.shape) for each in (gain, shift, weight)],
            out_specs=[shard(width)]
            + [whole(half, time_lanes)] * 2
            + [whole(half, weight_lanes)] * 2,
            scratch_shapes=[
                pltpu.VMEM((3, width, part), F32),
                pltpu.VMEM((embed, 2 * width), F32),
                pltpu.VMEM((8, width), F32),
                pltpu.VMEM((part, width), F32),
            ],
        ),
        out_shape=[jax.ShapeDtypeStruct((seq, width), BF16)]
        + [jax.ShapeDtypeStruct((half, time_lanes), BF16)] * 2
        + [jax.ShapeDtypeStruct((half, weight_lanes), BF16)] * 2,
        compiler_params=limits(48),
        cost_estimate=pl.CostEstimate(
            flops=seq * width,
            bytes_accessed=seq * width,
            transcendentals=seq,
        ),
    )(core, *kept_out(*inputs, *shards, *extras, *constants))


def middle_kernel(
    tokens_ref, top_ref, bottom_ref, embed_ref, time_ref, bias_ref, gain_ref, shift_ref, residual_ref, second_ref
):
    width = gain_ref.shape[1]
    attended = jnp.concatenate([top_ref[...], bottom_ref[...]], axis=0)
    residual = tokens_ref[...].astype(F32) + attended
    residual_ref[...] = residual
    mod = product(embed_ref[...], time_ref[...]) + bias_ref[...]
    normed, _ = norm_parts(residual)
    base = normed * gain_ref[...] + shift_ref[...]
    second_ref[...] = (base * (1.0 + mod[:, :width]) + mod[:, width:]).astype(BF16)


def middle(tokens, top, bottom, embed, time_flat, bias, gain, shift):
    rows, width = tokens.shape
    inputs = (tokens, top, bottom, embed, time_flat, bias, gain, shift)
    shard = whole(rows, width)
    return pl.pallas_call(
        middle_kernel,
        grid=(1,),
        in_specs=[whole(*each.shape) for each in inputs[:4]]
        + [block_of((embed.shape[1], 2 * width), 0, 1), block_of((1, 2 * width), 0, 1)]
        + [whole(*each.shape) for each in inputs[6:]],
        out_specs=[shard, shard],
        out_shape=[pltpu.HBM((rows, width), F32), pltpu.HBM((rows, width), BF16)],
        compiler_params=limits(16),
    )(*kept_out(tokens), top, bottom, *kept_out(*inputs[3:]))


def middle_back_kernel(
    part_ref, other_ref, cotangent_ref, residual_ref, embed_ref, time_ref, bias_ref, gain_ref, shift_ref,
    residual_grad_ref, half_ref, scale_grad_ref, shift_grad_ref, small_ref,
):
    grads = part_ref[...] + other_ref[...]
    factor = 1.0 + product(embed_ref[...], time_ref[...]) + bias_ref[...]
    normed, scale = norm_parts(residual_ref[...])
    gain = gain_ref[...]
    base = normed * gain + shift_ref[...]
    weighted = grads * factor
    inner = weighted * gain
    back = scale * (
        inner
        - jnp.mean(inner, axis=-1, keepdims=True)
        - normed * jnp.mean(inner * normed, axis=-1, keepdims=True)
    )
    residual_grad = cotangent_ref[...].astype(F32) + back
    residual_grad_ref[...] = residual_grad
    half_ref[...] = residual_grad.astype(BF16)
    scale_grad = grads * base
    scale_grad_ref[...] = scale_grad.astype(BF16)
    shift_grad_ref[...] = grads.astype(BF16)
    small_ref[...] = jnp.concatenate(
        [
            jnp.sum(each, axis=0, keepdims=True)
            for each in (weighted * normed, weighted, scale_grad, grads)
        ],
        axis=0,
    )


def middle_back(part, other, cotangent, residual, embed, time_flat, bias, gain, shift):
    rows, width = cotangent.shape
    shard = whole(rows, width)
    inputs = (part, other, cotangent, residual, embed, time_flat, bias, gain, shift)
    return pl.pallas_call(
        middle_back_kernel,
        grid=(1,),
        in_specs=[whole(*each.shape) for each in inputs[:5]]
        + [block_of((embed.shape[1], width), 0, 2), block_of((1, width), 0, 2)]
        + [whole(*each.shape) for each in inputs[7:]],
        out_specs=[shard] * 4 + [whole(4, width)],
        out_shape=[
            pltpu.HBM((rows, width), F32),
            jax.ShapeDtypeStruct((rows, width), BF16),
            pltpu.HBM((rows, width), BF16),
            pltpu.HBM((rows, width), BF16),
            pltpu.HBM((4, width), F32),
        ],
        compiler_params=limits(20),
    )(part, other, *kept_out(*inputs[2:]))


def forward_kernel(
    place_ref, rows_ref, rows_other_ref, grads_ref, grads_other_ref, up_own_ref, down_own_ref, up_near_ref, down_near_ref,
    up_far_ref, down_far_ref,
    branch_ref, branch_other_ref, second_ref, second_other_ref, *grad_refs, planes,
):
    step = pl.program_id(0)
    mine = step == 0
    rows = jnp.concatenate([rows_ref[...], rows_other_ref[...]], axis=0)
    grads = jnp.concatenate([grads_ref[...], grads_other_ref[...]], axis=0)
    count = branch_ref.shape[0]
    far = step < 3
    up = jnp.where(mine, up_own_ref[...], jnp.where(far, up_far_ref[0], up_near_ref[...]))
    up = up.reshape(rows.shape[1], up.shape[2])
    packed = jnp.where(mine, down_own_ref[...], jnp.where(far, down_far_ref[0], down_near_ref[...]))
    half = packed.shape[1] // 2
    down = jnp.concatenate(
        [packed[:, :half].reshape(-1, packed.shape[2]), packed[:, half:].reshape(-1, packed.shape[2])],
        axis=1,
    )
    hidden = product(rows, up)
    active_grad = product(grads, down, TRAIL)
    tail = 0.5 * (1.0 + lax.erf(hidden * math.sqrt(0.5)))
    slope = tail + hidden * jnp.exp(hidden * hidden * -0.5) * (1.0 / math.sqrt(2.0 * math.pi))
    active = (hidden * tail).astype(BF16)
    hidden_grad = (active_grad * slope).astype(BF16)
    branch = product(active, down)
    second = product(hidden_grad, up, TRAIL)

    @pl.when(mine)
    def _():
        branch_ref[...] = branch[:count]
        branch_other_ref[...] = branch[count:]
        second_ref[...] = second[:count]
        second_other_ref[...] = second[count:]

    @pl.when(step > 0)
    def _():
        branch_ref[...] += branch[:count]
        branch_other_ref[...] += branch[count:]
        second_ref[...] += second[:count]
        second_other_ref[...] += second[count:]

    bits = planes.bit_length() - 1
    down_grad = product(active, grads, LEAD)
    up_grad = product(rows, hidden_grad, LEAD)
    grad_refs = list(grad_refs)
    for grad in (down_grad, up_grad):
        middle = grad.shape[1] // 2
        for bit, columns in ((0, grad[:, :middle]), (bits - 1, grad[:, middle:])):
            one = (place_ref[0] >> bit) & 1 == 1
            low = columns.shape[0] // planes << bit
            split = columns.astype(BF16).reshape(-1, 2, low, middle)
            kept_ref, sent_ref = grad_refs.pop(0), grad_refs.pop(0)
            kept_ref[...] = jnp.where(one, split[:, 1], split[:, 0]).reshape(kept_ref.shape)
            sent_ref[...] = jnp.where(one, split[:, 0], split[:, 1]).reshape(sent_ref.shape)


def feed_forward(place, rows, rows_other, grads, grads_other, own_weights, near, far, groups):
    tokens, width = rows.shape
    planes, piece_rows, hidden = own_weights.shape
    half = whole(tokens, width)
    block = (planes, piece_rows // 2, hidden)

    def side(i):
        return jnp.where(i > 1, 1, 0)

    grad_specs, grad_shapes = [], []
    for each_rows, columns in ((hidden // planes, width // 2), (width // planes, hidden // 2)):
        for _ in range(4):
            grad_specs.append(
                pl.BlockSpec((planes // 2, 1, each_rows, columns), lambda i, at: (0, i, 0, 0))
            )
            grad_shapes.append(pltpu.HBM((planes // 2, groups, each_rows, columns), BF16))
    return pl.pallas_call(
        functools.partial(forward_kernel, planes=planes),
        grid_spec=pltpu.PrefetchScalarGridSpec(
            num_scalar_prefetch=1,
            grid=(groups,),
            in_specs=[
                half,
                half,
                half,
                half,
                pl.BlockSpec(block, lambda i, _: (0, 0, 0)),
                pl.BlockSpec(block, lambda i, _: (0, 1, 0)),
                pl.BlockSpec(block, lambda i, _: (0, 0, 0)),
                pl.BlockSpec(block, lambda i, _: (0, 1, 0)),
                pl.BlockSpec((1, *block), lambda i, _: (side(i), 0, 0, 0)),
                pl.BlockSpec((1, *block), lambda i, _: (side(i), 0, 1, 0)),
            ],
            out_specs=[half] * 4 + grad_specs,
        ),
        out_shape=[pltpu.HBM((tokens, width), F32)] * 2
        + [jax.ShapeDtypeStruct((tokens, width), F32)] * 2
        + grad_shapes,
        compiler_params=limits(48),
        cost_estimate=pl.CostEstimate(
            flops=24 * tokens * width * groups * hidden,
            bytes_accessed=8 * width * groups * hidden,
            transcendentals=4 * tokens * groups * hidden,
        ),
    )(place, *kept_out(rows), rows_other, *kept_out(grads, grads_other, own_weights, own_weights, near, near, far, far))


def spread_kernel(core_ref, own_ref, other_ref, out_ref, *, blocks):
    mine = pl.program_id(0) // blocks == core_ref[0]
    width = out_ref.shape[2]
    for at in range(out_ref.shape[1]):
        columns = slice(at * width, (at + 1) * width)
        out_ref[:, at, :] = jnp.where(mine, own_ref[:, columns], other_ref[:, columns]).astype(F32)


def spread(core, own, other, shape, rows):
    blocks = own.shape[0] // rows
    half = pl.BlockSpec((rows, shape[1] * shape[2]), lambda i, _: (i % blocks, 0))
    return pl.pallas_call(
        functools.partial(spread_kernel, blocks=blocks),
        grid_spec=pltpu.PrefetchScalarGridSpec(
            num_scalar_prefetch=1,
            grid=(2 * blocks,),
            in_specs=[half, half],
            out_specs=pl.BlockSpec((rows, shape[1], shape[2]), lambda i, _: (i, 0, 0)),
        ),
        out_shape=jax.ShapeDtypeStruct(shape, F32),
        compiler_params=limits(16),
    )(core, own, other)


def unfold_kernel(core_ref, own_ref, other_ref, out_ref):
    mine = core_ref[0] == 0
    rows, width = own_ref.shape[0], out_ref.shape[2]
    for at in range(own_ref.shape[1] // width):
        columns = slice(at * width, (at + 1) * width)
        own, other = own_ref[:, columns], other_ref[:, columns]
        first = 2 * at * rows
        out_ref[0, first : first + rows] = jnp.where(mine, own, other).astype(F32)
        out_ref[0, first + rows : first + 2 * rows] = jnp.where(mine, other, own).astype(F32)


def unfold(core, own, other, shape):
    rows = own.shape[0]
    blocks = shape[1] // (2 * rows)
    half = pl.BlockSpec((rows, blocks * shape[2]), lambda i, _: (0, i))
    return pl.pallas_call(
        unfold_kernel,
        grid_spec=pltpu.PrefetchScalarGridSpec(
            num_scalar_prefetch=1,
            grid=(shape[0],),
            in_specs=[half, half],
            out_specs=pl.BlockSpec((1, *shape[1:]), lambda i, _: (i, 0, 0)),
        ),
        out_shape=jax.ShapeDtypeStruct(shape, F32),
        compiler_params=limits(16),
    )(core, own, other)


def unpack_kernel(pieces_ref, out_ref):
    out_ref[...] = pieces_ref[...].reshape(out_ref.shape).astype(F32)


def unpack(pieces, planes):
    count, rows, width = pieces.shape
    step = min(planes, 2)
    return pl.pallas_call(
        unpack_kernel,
        grid=(count // step,),
        in_specs=[pl.BlockSpec((step, rows, width), lambda i: (i, 0, 0))],
        out_specs=pl.BlockSpec(
            (step * rows, width), lambda i: (i % (planes // step), i // (planes // step))
        ),
        out_shape=jax.ShapeDtypeStruct((planes * rows, width * count // planes), F32),
        compiler_params=limits(16),
    )(pieces)


def swap(values, axis_name, bit):
    size = lax.axis_size(axis_name)
    return lax.ppermute(values, axis_name, [(at, at ^ (1 << bit)) for at in range(size)])


def bit_of(axis_name, bit):
    return (lax.axis_index(axis_name) >> bit) & 1


def after(values, *others):
    return lax.optimization_barrier((values, others))[0]


def exchange(values, axis_name, bit, dim):
    own = bit_of(axis_name, bit)
    kept = lax.dynamic_index_in_dim(values, own, dim, keepdims=False)
    sent = lax.dynamic_index_in_dim(values, 1 - own, dim, keepdims=False)
    return (kept, swap(sent, axis_name, bit))


def total(kept, got):
    return (kept.astype(F32) + got.astype(F32)).astype(BF16)


def double(values, axis_name, bit, dim):
    own = bit_of(axis_name, bit) == 0
    got = swap(values, axis_name, bit)
    return jnp.stack([jnp.where(own, values, got), jnp.where(own, got, values)], axis=dim)


class PlaneScatter:
    def __init__(self, arrays, orders, dim):
        bits = len(orders[0])
        self.dim = dim
        self.arrays = [
            each.reshape(each.shape[:dim] + (2,) * bits + each.shape[dim + 1 :]) for each in arrays
        ]
        self.orders = [list(order) for order in orders]
        self.left = [list(range(bits - 1, -1, -1)) for _ in orders]

    @classmethod
    def started(cls, kept, sent, orders, dim):
        self = cls.__new__(cls)
        bits = len(orders[0])
        self.dim = dim
        self.orders = [list(order[1:]) for order in orders]
        self.left = [[bit for bit in range(bits - 1, -1, -1) if bit != order[0]] for order in orders]
        self.kept = [
            each.reshape(each.shape[:dim] + (2,) * (bits - 1) + each.shape[dim + 1 :]) for each in kept
        ]
        self.got = [
            swap(each, "plane", order[0]).reshape(like.shape)
            for each, like, order in zip(sent, self.kept, orders)
        ]
        return self

    def send(self):
        self.kept, self.got = [], []
        for values, order, left in zip(self.arrays, self.orders, self.left):
            bit = order.pop(0)
            kept, got = exchange(values, "plane", bit, self.dim + left.index(bit))
            left.remove(bit)
            self.kept.append(kept)
            self.got.append(got)
        self.meet()

    def meet(self, *others):
        self.got, others = lax.optimization_barrier((self.got, others))
        return others

    def add(self):
        self.arrays = [total(kept, got) for kept, got in zip(self.kept, self.got)]

    def finish(self):
        while self.orders[0]:
            self.send()
            self.add()
        return self.arrays


class PlaneGather:
    def __init__(self, arrays, orders):
        self.arrays = list(arrays)
        self.orders = [list(order) for order in orders]
        self.left = [[] for _ in orders]

    def send(self):
        self.bits = [order.pop() for order in self.orders]
        self.got = [swap(values, "plane", bit) for values, bit in zip(self.arrays, self.bits)]

    def join(self):
        for at, bit in enumerate(self.bits):
            self.left[at] = sorted(self.left[at] + [bit], reverse=True)
            own = bit_of("plane", bit) == 0
            values, got = self.arrays[at], self.got[at]
            pair = (jnp.where(own, values, got), jnp.where(own, got, values))
            self.arrays[at] = jnp.stack(pair, axis=self.left[at].index(bit))

    def finish(self):
        while self.orders[0]:
            self.send()
            self.arrays, self.got = lax.optimization_barrier((self.arrays, self.got))
            self.join()
        return self.arrays


def ring_gather(shard, meanwhile=None):
    size = lax.axis_size("tensor")
    half = shard.shape[0] // 2
    right, left = [shard[:half]], [shard[half:]]
    for step in range(1, size):
        others = () if meanwhile is None else meanwhile(step, right, left)
        right.append(lax.ppermute(right[-1], "tensor", [(at, (at + 1) % size) for at in range(size)]))
        left.append(lax.ppermute(left[-1], "tensor", [(at, (at - 1) % size) for at in range(size)]))
        right[-1], left[-1], others = lax.optimization_barrier((right[-1], left[-1], others))
        if meanwhile is not None:
            meanwhile(-step, others, None)
    return [(right[(size - at) % size], left[at]) for at in range(size)]


class RingScatter:
    def __init__(self, chunks):
        self.chunks = chunks
        self.size = len(chunks)
        self.half = chunks[0].shape[0] // 2
        self.step = 0
        self.right = chunks[-1][: self.half]
        self.left = chunks[1][self.half :]

    def send(self):
        size = self.size
        right = lax.ppermute(self.right, "tensor", [(at, (at + 1) % size) for at in range(size)])
        left = lax.ppermute(self.left, "tensor", [(at, (at - 1) % size) for at in range(size)])
        self.got = lax.optimization_barrier((right, left))

    def add(self):
        self.step += 1
        right, left = self.got
        self.right = right.astype(F32) + self.chunks[self.size - 1 - self.step][: self.half].astype(F32)
        self.left = left.astype(F32) + self.chunks[(self.step + 1) % self.size][self.half :].astype(F32)
        if self.step < self.size - 1:
            self.right, self.left = self.right.astype(BF16), self.left.astype(BF16)

    def finish(self):
        while self.step < self.size - 1:
            self.send()
            self.add()
        return (self.right, self.left)


def own_first(values, dim):
    size = lax.axis_size("tensor")
    stretch = values.shape[dim] // size
    doubled = jnp.concatenate([values, values], axis=dim)
    return lax.dynamic_slice_in_dim(
        doubled, lax.axis_index("tensor") * stretch, values.shape[dim], dim
    )


def local(
    tokens,
    time_embed,
    segment_ids,
    positions,
    first_gain,
    first_bias,
    second_gain,
    second_bias,
    time_weight,
    time_bias,
    qkv_weight,
    out_weight,
    up_weight,
    down_weight,
    cotangent,
):
    local_rows, width = tokens.shape
    embed_width = time_embed.shape[1]
    local_width = qkv_weight.shape[2]
    hidden_local = up_weight.shape[1]
    half_hidden = hidden_local // 2
    planes = lax.axis_size("plane")
    groups = lax.axis_size("tensor")
    plane_at = lax.axis_index("plane")
    core_at = lax.axis_index("core")
    place = plane_at.astype(jnp.int32).reshape(1)
    arrival = sorted(range(groups), key=lambda at: max(at, groups - at) if at else 0)
    rising = list(range(planes.bit_length() - 1))
    falling = rising[::-1]

    up_rows = width // planes
    up_piece = lax.dynamic_slice(
        up_weight, (plane_at * up_rows, core_at * half_hidden), (up_rows, half_hidden)
    )
    down_rows = half_hidden // planes
    down_piece = lax.dynamic_slice(
        down_weight, (core_at * half_hidden + plane_at * down_rows, 0), (down_rows, width)
    )
    piece = jnp.concatenate([up_piece, down_piece[:, :half_hidden], down_piece[:, half_hidden:]], axis=0)
    ahead = [(at, (at + 1) % groups) for at in range(groups)]
    behind = [(at, (at - 1) % groups) for at in range(groups)]
    up_half = lax.dynamic_slice_in_dim(up_weight, core_at * half_hidden, half_hidden, 1)
    down_half = lax.dynamic_slice_in_dim(down_weight, core_at * half_hidden, half_hidden, 0)
    down_half = down_half.reshape(planes, down_rows, width)
    own_pieces = jnp.concatenate(
        [
            up_half.reshape(planes, up_rows, half_hidden),
            down_half[..., :half_hidden],
            down_half[..., half_hidden:],
        ],
        axis=1,
    )

    held = {
        "time": time_weight.reshape(embed_width, 4 * width),
        "tables": rotary_tables(own_first(positions, 1).reshape(-1), 2 * HEAD),
        "pieces": own_pieces,
        "cotangent": swap(cotangent, "core", 0),
        "near": lax.ppermute(piece, "tensor", ahead),
    }
    bias_flat = time_bias.reshape(1, 4 * width)
    first_gain, first_bias = first_gain.reshape(1, width), first_bias.reshape(1, width)
    second_gain, second_bias = second_gain.reshape(1, width), second_bias.reshape(1, width)
    qkv_planes = jnp.transpose(qkv_weight, (1, 0, 2))
    segments = own_first(segment_ids, 1)
    columns = segments.reshape(-1, 1)

    def enter(places, halves, row):
        return entry(
            halves, held["tables"], held["time"], bias_flat, first_gain, first_bias, qkv_planes, places, groups, row
        )

    def meanwhile(step, right, left):
        if step == 1:
            return held
        if step == -1:
            held.update(right)
        elif step == 2:
            return enter([0], (right[0], left[0]), ())
        elif step > 2 and 2 * (step - 1) == groups:
            return enter([step - 1], (right[step - 1], left[step - 1]), held["row"])
        elif step > 0:
            return held["row"]
        else:
            held["row"] = right
        return None

    gathered = ring_gather(jnp.concatenate([tokens, time_embed], axis=1), meanwhile)
    near = lax.all_gather(held["near"], "plane", axis=0)
    piece, passed = after((piece, held["near"]), gathered[arrival[-1]])
    far = [lax.ppermute(piece, "tensor", behind), lax.ppermute(passed, "tensor", ahead)]
    row = held["row"]
    for first in range(2, len(arrival), 2):
        places = arrival[first : first + 2]
        row = enter(places, [half for at in places for half in gathered[at]], row)
    tables, time_flat = held["tables"], held["time"]
    tokens_all, first_all, queries, keys, values = row
    keys, far, near = lax.optimization_barrier((keys, far, near))
    far = lax.all_gather(jnp.stack(far), "plane", axis=1)
    mixed, logsums, parts = {}, {}, {}
    for at in list(range(groups - 1, -1, -1)):
        mixed[at], logsums[at], parts[at] = attend(
            queries, keys, values, segments, columns, out_weight, at, local_rows
        )
    attended = RingScatter([parts[at] for at in range(groups)]).finish()

    residual, second_normed = middle(
        tokens, *attended, time_embed, time_flat, bias_flat, second_gain, second_bias
    )
    branch_own, branch_other, second_own, second_other, *grad_parts = feed_forward(
        place,
        second_normed,
        swap(second_normed, "core", 0),
        cotangent,
        held["cotangent"],
        held["pieces"],
        near.reshape(planes, 2 * up_rows, half_hidden),
        far,
        groups,
    )
    second_other = swap(second_other, "core", 0)

    sums = {"down": PlaneScatter.started(grad_parts[:4:2], grad_parts[1:4:2], [rising, falling], 0)}
    branch = branch_own + swap(branch_other, "core", 0)
    result = (residual + branch).astype(BF16)

    residual_grad, attended_own, scale_two_grad, shift_two_grad, small_two = middle_back(
        second_own,
        second_other,
        cotangent,
        residual,
        time_embed,
        time_flat,
        bias_flat,
        second_gain,
        second_bias,
    )
    def turn(places, halves):
        return attend_back(
            halves,
            queries,
            keys,
            values,
            [logsums[at] for at in places],
            segments,
            columns,
            out_weight,
            tables,
            places,
        )

    back = {}

    def meanwhile_back(step, right, left):
        if step == 2:
            return (turn([0], (right[0], left[0])), sums["down"].got)
        elif step == -2:
            back[(0,)], sums["down"].got = right
            sums["down"].add()
            if sums["down"].orders[0]:
                sums["down"].send()
            up_parts = after(grad_parts[4:], sums["down"].arrays)
            sums["up"] = PlaneScatter.started(up_parts[::2], up_parts[1::2], [rising, falling], 0)
        elif step == 3:
            return turn([2], (right[2], left[2]))
        elif step == -3:
            back[(2,)] = right
        return ()

    def to_tensor(arrays):
        parts = [jnp.concatenate([each[at] for each in arrays], axis=-1) for at in range(groups)]
        received = [
            lax.ppermute(parts[hop], "tensor", [(at, (at + hop) % groups) for at in range(groups)])
            for hop in range(1, groups)
        ]
        return (parts[0], received)

    def joined(own_part, received):
        return sum(each.astype(F32) for each in [own_part, *received]).astype(BF16)

    attended_halves = ring_gather(attended_own, meanwhile_back)
    places = (1, 3)
    back[places] = turn(places, [half for at in places for half in attended_halves[at]])
    back[places], sums["down"].got = sums["up"].meet(back[places], sums["down"].got)
    sums["down"].add()
    down_own, down_received = to_tensor(sums["down"].finish())
    sums["up"].add()
    if sums["up"].orders[0]:
        sums["up"].send()
    query_shards = {at: (parts[0], which) for places, parts in back.items() for which, at in enumerate(places)}
    received = [
        lax.ppermute(parts[hop], "tensor", [(at, (at + hop) % groups) for at in range(groups)])
        for hop in range(1, groups)
    ]
    core_own = core_at.astype(jnp.int32).reshape(1)
    left = leave(
        core_own,
        [query_shards[at] for at in range(groups)],
        [parts[1] for parts in back.values()],
        [parts[2] for parts in back.values()],
        [mixed[at] for at in range(groups)],
        attended_halves,
        tables,
        tokens_all,
        first_all,
        (scale_two_grad, shift_two_grad, small_two),
        time_embed,
        time_flat,
        bias_flat,
        first_gain,
        first_bias,
        qkv_planes,
        local_rows,
    )
    left, down_received = sums["up"].meet(left, down_received)
    sums["up"].add()
    up_own, up_received = to_tensor(sums["up"].finish())
    down_all = lax.all_gather(joined(down_own, down_received), ("core", "plane"), axis=0, tiled=True)
    first_half, time_kept, time_sent, weight_kept, weight_sent = left

    time_got, weight_got = swap(time_sent, "core", 0), swap(weight_sent, "core", 0)

    def by_plane(pack):
        return pack.reshape(planes, embed_width // (2 * planes), -1)

    pack_sums = PlaneScatter(
        [by_plane(total(time_kept, time_got)), by_plane(total(weight_kept, weight_got))], [rising, falling], 0
    )
    ring = RingScatter([first_half[at * local_rows : (at + 1) * local_rows] for at in range(groups)])
    pack_sums.send()
    pack_sums.add()
    ring.send()
    second = bool(pack_sums.orders[0])
    if second:
        pack_sums.send()
    (ring.got, up_received) = pack_sums.meet(ring.got, up_received)
    if second:
        pack_sums.add()
    time_own, weight_own = pack_sums.finish()
    ring.add()
    up_all = lax.all_gather(joined(up_own, up_received), ("core", "plane"), axis=0)
    time_got = swap(time_own, "tensor", 0)
    time_got, down_all = lax.optimization_barrier((time_got, down_all))
    down_summed = down_all.astype(F32)
    time_own = total(time_own, time_got)
    time_got = swap(time_own, "tensor", 1)
    time_got, down_summed = lax.optimization_barrier((time_got, down_summed))
    time_sum = total(time_own, time_got)
    (ring.right, ring.left), time_sum = lax.optimization_barrier(((ring.right, ring.left), time_sum))
    gather = PlaneGather([time_sum, weight_own], [rising, falling])
    ring.send()
    gather.send()
    ring.got, gather.got, up_all = lax.optimization_barrier((ring.got, gather.got, up_all))
    gather.join()
    ring.add()
    ring.send()
    (up_all,) = kept_out(up_all)
    up_summed = unpack(up_all, planes)
    if gather.orders[0]:
        gather.send()
        gather.got = lax.optimization_barrier(gather.got)
        gather.join()
    ring.add()
    time_half, weight_half = gather.finish()
    packs = [time_half.reshape(embed_width // 2, -1), weight_half.reshape(embed_width // 2, -1)]
    (time_half, time_other), (weight_half, weight_other) = ((pack, swap(pack, "core", 0)) for pack in packs)
    first_grad = ring.finish()
    time_weight_grad = spread(
        core_own, time_half, time_other, (embed_width, 4, width), min(64, embed_width // 2)
    )
    qkv_lanes = 3 * local_width * width // embed_width
    qkv_summed = jnp.transpose(
        unfold(core_own, weight_half, weight_other, (3, width, local_width)), (1, 0, 2)
    )

    def both_cores(own_half, other_half):
        mine = core_at == 0
        halves = [jnp.where(mine, own_half, other_half), jnp.where(mine, other_half, own_half)]
        return jnp.concatenate(halves, axis=0).astype(F32)

    out_summed = both_cores(weight_half[:, qkv_lanes:], weight_other[:, qkv_lanes:])
    small = both_cores(time_half[:, 4 * width :], time_other[:, 4 * width :])[: width // 16]
    small = jnp.transpose(small.reshape(width // 128, 8, 128), (1, 0, 2)).reshape(8, width)

    own_normed, own_scale = norm_parts(tokens.astype(F32))
    mod_own = product(time_embed, time_flat[:, :width]) + bias_flat[:, :width]
    first_grad = jnp.concatenate(first_grad, axis=0)
    input_grad = residual_grad + norm_input_back(first_grad, own_normed, own_scale, first_gain, mod_own)
    return (
        result,
        input_grad,
        small[0],
        small[1],
        small[4],
        small[5],
        time_weight_grad,
        jnp.concatenate([small[2:4], small[6:]], axis=0),
        qkv_summed,
        out_summed,
        up_summed,
        down_summed,
    )


def solution(mesh):
    whole, tensor = mesh.devices.shape
    finer = Mesh(mesh.devices.reshape(whole // 2, 2, tensor), ("plane", "core", "tensor"))
    rows = P(("plane", "core", "tensor"), None)
    group = P(("plane", "core"), None)
    return jax.shard_map(
        local,
        mesh=finer,
        in_specs=(
            rows,
            rows,
            group,
            group,
            P(),
            P(),
            P(),
            P(),
            P(),
            P(),
            P(None, None, "tensor"),
            P("tensor", None),
            P(None, "tensor"),
            P("tensor", None),
            rows,
        ),
        out_specs=(
            rows,
            rows,
            P(),
            P(),
            P(),
            P(),
            P(),
            P(),
            P(None, None, "tensor"),
            P("tensor", None),
            P(None, "tensor"),
            P("tensor", None),
        ),
        check_vma=False,
    )
```
